32 devices in a mesh: dp: 8 (over z, x), tensor: 4 (over y, core).
Axes of the slice: x: 2, y: 2, z: 4, core: 2. Of those that a mesh axis runs over, the one named last changes fastest.
Arguments:
- tokens: bfloat16 [16, 1024, 2048], P('dp', 'tensor'), may hold values from -6 to 6
- pre_gain: float32 [2048], replicated, may hold values from 0.1 to 1.9
- weight_gate: bfloat16 [2048, 4096], P(None, 'tensor'), may hold values from -0.125 to 0.125
- weight_inner: bfloat16 [2048, 4096], P(None, 'tensor'), may hold values from -0.125 to 0.125
- weight_step: bfloat16 [2048, 64], P(None, 'tensor'), may hold values from -0.0625 to 0.0625
- weight_shared: bfloat16 [2048, 256], replicated, may hold values from -0.125 to 0.125
- conv_kernel: float32 [4, 4096], P(None, 'tensor'), may hold values from -3 to 3
- conv_offset: float32 [4096], P('tensor'), may hold values from -1.8 to 1.8
- shared_kernel: float32 [4, 256], replicated, may hold values from -3 to 3
- shared_offset: float32 [256], replicated, may hold values from -1.8 to 1.8
- step_bias: float32 [64], P('tensor'), may hold values from -7 to -2.3
- log_rate: float32 [64], P('tensor'), may hold values from 0 to 2.77
- skip_gain: float32 [64], P('tensor'), may hold values from 0.5 to 2
- gate_gain: float32 [4096], P('tensor'), may hold values from 0.1 to 1.9
- weight_out: bfloat16 [4096, 2048], P('tensor'), may hold values from -0.09375 to 0.09375
- cotangent: bfloat16 [16, 1024, 2048], P('dp', 'tensor'), may hold values from -6 to 6
- segments: int32 [16, 1024], P('dp'), may hold values from 0 to 7, never falling along the last dimension, each value on 1 to 512 neighbouring positions
- image_span: int32 [16, 2], P('dp'), may hold values from 0 to 4, as said below
Outputs:
- block_out: bfloat16 [16, 1024, 2048], P('dp', 'tensor')
- tokens_grad: bfloat16 [16, 1024, 2048], P('dp', 'tensor')
- pre_gain_grad: float32 [2048], replicated
- weight_gate_grad: float32 [2048, 4096], P(None, 'tensor')
- weight_inner_grad: float32 [2048, 4096], P(None, 'tensor')
- weight_step_grad: float32 [2048, 64], P(None, 'tensor')
- weight_shared_grad: float32 [2048, 256], replicated
- conv_kernel_grad: float32 [4, 4096], P(None, 'tensor')
- conv_offset_grad: float32 [4096], P('tensor')
- shared_kernel_grad: float32 [4, 256], replicated
- shared_offset_grad: float32 [256], replicated
- step_bias_grad: float32 [64], P('tensor')
- log_rate_grad: float32 [64], P('tensor')
- skip_gain_grad: float32 [64], P('tensor')
- gate_gain_grad: float32 [4096], P('tensor')
- weight_out_grad: float32 [4096, 2048], P('tensor')
The draws below stay inside these ranges and needn't reach their ends.
Inputs may be any that keep to these rules, and one draw needn't show every extreme that they name: `segments`: along a sequence the document ids never fall; a document has 1 to 512 tokens. `image_span`: each row holds (first image piece, number of image pieces); first + number <= 4; a sequence may have no image piece.
All inputs are finite; a program needn't handle non-finite values.
Results may differ from the reference program's by a relative error of at most 0.0087.
Values may be sent and summed in bfloat16 or wider, within the bound.
No kernel may reach another device: no remote copies, remote signals or barrier semaphores. Data moves between devices by JAX's collectives and lax.ppermute only.
A program may use at most 320 MiB of HBM per device.

```python
import math
import jax
import jax.numpy as jnp
import numpy as np
from jax import lax

D = 2048
HEADS = 64
STATE = 128
CONV = 4
STRETCH = 256
SEQ_LEN = 1024
SEQS = 16
DI = 4096
NCHUNK = 4


def draw_image_span(key, part):
    key_length, key_start = jax.random.split(key)
    span_length = jax.random.randint(key_length, (SEQS,), 0, NCHUNK + 1)
    span_start = jax.random.randint(key_start, (SEQS,), 0, NCHUNK + 1 - span_length)
    return jnp.stack([span_start, span_length], axis=1).astype(jnp.int32)


def steps_of(own_key, shape, cuts, least, top_value):
    factor_of, own = 1.0, jax.random.fold_in(own_key, 6)
    for dim, parts in cuts:
        draws = jnp.exp(jax.random.uniform(jax.random.fold_in(own, dim), (parts,), jnp.float32, least / len(cuts), top_value / len(cuts)))
        factor_of = factor_of * jnp.repeat(draws, shape[dim] // parts).reshape([-1 if axis == dim else 1 for axis in range(len(shape))])
    return factor_of


def length_profile(amount, total, most, slope):
    portions = [(1 << 20) // math.isqrt(grade ** slope) + 1 for grade in range(2, amount + 1)]
    rest, given = total - most - (amount - 1), [1] * (amount - 1)
    while rest > 0:
        candidates = [i for i in range(amount - 1) if given[i] < most]
        whole, left = sum([portions[i] for i in candidates]), rest
        for i in candidates:
            addition = min(most - given[i], max(1, left * portions[i] // whole), rest)
            given[i] = given[i] + addition
            rest = rest - addition
    return np.array([most] + given)


def uneven(own_key, amount, total, most, lean):
    if amount == 2:
        one = jax.random.randint(own_key, (), max(1, total - most), min(most, total - 1) + 1)
        return jnp.stack([one, total - one])
    lengths = jnp.asarray(length_profile(amount, total, most, lean), jnp.int32)
    couples = (amount - 1) // 2
    giver, sink = lengths[1:1 + 2 * couples:2], lengths[2:2 + 2 * couples:2]
    margin = jnp.minimum(giver - 1, most - sink)
    moved = jax.random.randint(jax.random.fold_in(own_key, 1), (couples,), 0, 1 << 20) % (margin + 1)
    lengths = lengths.at[1:1 + 2 * couples:2].set(giver - moved).at[2:2 + 2 * couples:2].set(sink + moved)
    return lengths[jax.random.permutation(jax.random.fold_in(own_key, 2), amount)]


def gaussian(own_key, extent, scale, limit, cuts=(), held_as=jnp.bfloat16):
    array = scale * jax.random.normal(own_key, extent, jnp.float32)
    if cuts:
        array = array * steps_of(own_key, extent, cuts, -0.22, 0.18)
    return jnp.clip(array, -limit, limit).astype(held_as)


def setup_inputs(seed: int = 0) -> dict:
    splits = jax.random.split(jax.random.key(seed), 19)
    return {
        "tokens": gaussian(splits[0], (SEQS, SEQ_LEN, D), 1.0, 6.0, ((0, 8), (1, 4))),
        "pre_gain": jnp.clip(1.0 + 0.18 * jax.random.normal(splits[1], (D,), jnp.float32), 0.1, 1.9),
        "weight_gate": gaussian(splits[2], (D, DI), D ** -0.5, 0.125, ((1, 4),)),
        "weight_inner": gaussian(splits[3], (D, DI), D ** -0.5, 0.125, ((1, 4),)),
        "weight_step": gaussian(splits[4], (D, HEADS), (4 * D) ** -0.5, 0.0625, ((1, 4),)),
        "weight_shared": gaussian(splits[5], (D, 2 * STATE), D ** -0.5, 0.125),
        "conv_kernel": gaussian(splits[6], (CONV, DI), CONV ** -0.5, 3.0, ((1, 4),), jnp.float32),
        "conv_offset": gaussian(splits[7], (DI,), 0.3, 1.8, ((0, 4),), jnp.float32),
        "shared_kernel": gaussian(splits[8], (CONV, 2 * STATE), CONV ** -0.5, 3.0, (), jnp.float32),
        "shared_offset": gaussian(splits[9], (2 * STATE,), 0.3, 1.8, (), jnp.float32),
        "step_bias": jnp.clip(-7.0 + 4.7 * jax.random.uniform(splits[10], (HEADS,), jnp.float32) ** steps_of(splits[10], (HEADS,), ((0, 4),), -0.2, 0.2), -7.0, -2.3),
        "log_rate": jnp.clip(2.77 * jax.random.uniform(splits[11], (HEADS,), jnp.float32) ** steps_of(splits[11], (HEADS,), ((0, 4),), -0.2, 0.2), 0.0, 2.77),
        "skip_gain": jnp.clip(0.5 + 1.5 * jax.random.uniform(splits[12], (HEADS,), jnp.float32) ** steps_of(splits[12], (HEADS,), ((0, 4),), -0.2, 0.2), 0.5, 2.0),
        "gate_gain": jnp.clip(1.0 + 0.18 * jax.random.normal(splits[13], (DI,), jnp.float32), 0.1, 1.9),
        "weight_out": gaussian(splits[14], (DI, D), DI ** -0.5, 0.09375, ((0, 4),)),
        "cotangent": gaussian(splits[15], (SEQS, SEQ_LEN, D), 1.0, 6.0, ((0, 8), (1, 4))),
        "segments": jax.vmap(lambda own: jnp.searchsorted(jnp.cumsum(uneven(own, max(4, SEQ_LEN // 128), SEQ_LEN, SEQ_LEN // 2, 1)), jnp.arange(SEQ_LEN), side="right"))(jax.random.split(splits[16], SEQS)).reshape((SEQS, SEQ_LEN)).astype(jnp.int32),
        "image_span": draw_image_span(jax.random.fold_in(splits[18], 71), 0),
    }


EPSILON = 1e-05
HIGHEST = lax.Precision.HIGHEST

@jax.custom_vjp
def low(v):
    return lax.optimization_barrier(v.astype(jnp.bfloat16)).astype(jnp.float32)

@jax.custom_vjp
def low_back(v):
    return v

def low_keep(v):
    return (low(v), None)

def low_pass(kept, grad):
    return (grad,)

def back_keep(v):
    return (v, None)

def back_low(kept, grad):
    return (low(grad),)
low.defvjp(low_keep, low_pass)
low_back.defvjp(back_keep, back_low)

def matmul(left, right):
    return jnp.dot(left, right, precision=HIGHEST, preferred_element_type=jnp.float32)

def sigmoid_linear(values):
    return values * jax.nn.sigmoid(values)

def causal_conv(signal, kernel, offset):
    length = signal.shape[0]
    tap_count = kernel.shape[0]
    padded = jnp.pad(signal, ((tap_count - 1, 0), (0, 0)))
    summed = offset[None, :] + kernel[0][None, :] * padded[0:length]
    for tap_index in range(1, tap_count):
        summed = summed + kernel[tap_index][None, :] * padded[tap_index:tap_index + length]
    return summed

def piece_flags(span_row, pieces):
    piece_index = jnp.arange(pieces, dtype=jnp.int32)
    inside = (piece_index >= span_row[0]) & (piece_index < span_row[0] + span_row[1])
    return inside.astype(jnp.int32)

def state_scan(inputs_x, step_size, decay_rate, b_matrix, c_matrix, segment, is_image):
    length, head_count, head_width = inputs_x.shape
    pieces = is_image.shape[0]
    block_len = length // pieces
    log_step = (step_size * decay_rate[None, :]).reshape(pieces, block_len, head_count)
    cumulated = jnp.cumsum(log_step, axis=1)
    weighted_x = (inputs_x * step_size[:, :, None]).reshape(pieces, block_len, head_count, head_width)
    b_blocks = b_matrix.reshape(pieces, block_len, -1)
    c_blocks = c_matrix.reshape(pieces, block_len, -1)
    doc_blocks = segment.reshape(pieces, block_len)
    same_doc = doc_blocks[:, :, None] == doc_blocks[:, None, :]
    position = jnp.arange(block_len)
    causal = position[:, None] >= position[None, :]
    allowed = same_doc & (causal[None, :, :] | (is_image[:, None, None] > 0))
    spread = cumulated[:, :, None, :] - cumulated[:, None, :, :]
    decays = jnp.where(allowed[:, :, :, None], jnp.exp(-jnp.abs(spread)), jnp.zeros_like(spread))
    scores = jnp.einsum('ctn,csn->cts', c_blocks, b_blocks, precision=HIGHEST)
    mixing = scores[:, :, :, None] * decays
    within = jnp.einsum('ctsh,cshp->cthp', mixing, weighted_x, precision=HIGHEST)
    last_doc = doc_blocks[:, -1]
    to_end = (doc_blocks == last_doc[:, None]).astype(cumulated.dtype)[:, :, None] * jnp.exp(cumulated[:, -1:, :] - cumulated)
    fresh_state = jnp.einsum('cshp,csn->chpn', to_end[:, :, :, None] * weighted_x, b_blocks, precision=HIGHEST)
    before_doc = jnp.concatenate([doc_blocks[:1, 0], doc_blocks[:-1, -1]])
    keep_factor = (last_doc == before_doc).astype(cumulated.dtype)[:, None] * jnp.exp(cumulated[:, -1, :])

    def advance(carry_state, scan_item):
        factor, update = scan_item
        return (factor[:, None, None] * carry_state + update, carry_state)
    start_state = jnp.zeros((head_count, head_width, b_blocks.shape[2]), inputs_x.dtype)
    final_state, entering = lax.scan(advance, start_state, (keep_factor, fresh_state))
    reach_gate = (doc_blocks == before_doc[:, None]).astype(cumulated.dtype)[:, :, None] * jnp.exp(cumulated)
    carried = jnp.einsum('ctn,chpn->cthp', c_blocks, entering, precision=HIGHEST) * reach_gate[:, :, :, None]
    return (within + carried).reshape(length, head_count, head_width)

def state_mixer(gate_pre, inner_pre, step_pre, shared_pre, conv_kernel, conv_offset, shared_kernel, shared_offset, step_bias, log_rate, skip_gain, segment, is_image):
    activated = sigmoid_linear(causal_conv(inner_pre, conv_kernel, conv_offset))
    shared = sigmoid_linear(causal_conv(shared_pre, shared_kernel, shared_offset))
    state_width = shared.shape[1] // 2
    head_count = step_bias.shape[0]
    length = inner_pre.shape[0]
    inputs_x = activated.reshape(length, head_count, -1)
    step_size = jax.nn.softplus(step_pre + step_bias[None, :])
    decay_rate = -jnp.exp(log_rate)
    mixed_out = state_scan(inputs_x, step_size, decay_rate, shared[:, :state_width], shared[:, state_width:], segment, is_image)
    mixed_out = mixed_out + skip_gain[None, :, None] * inputs_x
    return mixed_out.reshape(length, -1) * sigmoid_linear(gate_pre)

def residual_block(tokens_in, pre_gain, weight_gate, weight_inner, weight_step, weight_shared, conv_kernel, conv_offset, shared_kernel, shared_offset, step_bias, log_rate, skip_gain, gate_gain, weight_out, segment, is_image):
    row_scale = lax.rsqrt(lax.optimization_barrier(jnp.mean(tokens_in * tokens_in, axis=1, keepdims=True)) + EPSILON)
    normed_in = low(tokens_in * row_scale * pre_gain[None, :])
    gate_pre = low_back(matmul(normed_in, weight_gate))
    inner_pre = low_back(matmul(normed_in, weight_inner))
    step_pre = low_back(matmul(normed_in, weight_step))
    shared_pre = low_back(matmul(normed_in, weight_shared))
    gated_out = state_mixer(gate_pre, inner_pre, step_pre, shared_pre, conv_kernel, conv_offset, shared_kernel, shared_offset, step_bias, log_rate, skip_gain, segment, is_image)
    gate_scale = lax.rsqrt(lax.optimization_barrier(jnp.mean(gated_out * gated_out, axis=1, keepdims=True)) + EPSILON)
    normed_out = low(gated_out * gate_scale * gate_gain[None, :])
    return tokens_in + matmul(normed_out, weight_out)

def reference(tokens, pre_gain, weight_gate, weight_inner, weight_step, weight_shared, conv_kernel, conv_offset, shared_kernel, shared_offset, step_bias, log_rate, skip_gain, gate_gain, weight_out, cotangent, segments, image_span):
    parameters = tuple((parameter.astype(jnp.float32) for parameter in (pre_gain, weight_gate, weight_inner, weight_step, weight_shared, conv_kernel, conv_offset, shared_kernel, shared_offset, step_bias, log_rate, skip_gain, gate_gain, weight_out)))
    pieces = segments.shape[1] // STRETCH

    def one_sequence(totals, scan_item):
        sequence_in, sequence_cot, segment, span_row = scan_item
        is_image = piece_flags(span_row, pieces)

        def forward(tokens_in, *weights):
            return residual_block(tokens_in, *weights, segment, is_image)
        result, pullback = jax.vjp(forward, sequence_in.astype(jnp.float32), *parameters)
        gradients = pullback(sequence_cot.astype(jnp.float32))
        totals = tuple((running + addend for running, addend in zip(totals, gradients[1:])))
        return (totals, (result.astype(jnp.bfloat16), gradients[0].astype(jnp.bfloat16)))
    initial = tuple((jnp.zeros_like(parameter) for parameter in parameters))
    totals, (block_out, tokens_grad) = lax.scan(one_sequence, initial, (tokens, cotangent, segments, image_span))
    return (block_out, tokens_grad, totals[0], totals[1], totals[2], totals[3], totals[4], totals[5], totals[6], totals[7], totals[8], totals[9], totals[10], totals[11], totals[12], totals[13])
```

```python
from functools import partial

import jax
import jax.numpy as jnp
from jax import lax
from jax.experimental import pallas as pl
from jax.experimental.pallas import tpu as pltpu
from jax.sharding import PartitionSpec as P

STRETCH = 256
HEAD = 64
LANES = 128
GROUPS = 2

EPSILON = 1e-05
LOG2E = 1.4426950408889634
BF16 = jnp.bfloat16
F32 = jnp.float32
NN = (((1,), (0,)), ((), ()))
NT = (((1,), (1,)), ((), ()))
TN = (((0,), (0,)), ((), ()))


def mm(left, right, dims=NN):
    return lax.dot_general(left.astype(BF16), right.astype(BF16), dims, preferred_element_type=F32)


def two_parts(values):
    high = values.astype(BF16)
    return high, (values - high.astype(F32)).astype(BF16)


def iota(shape, axis):
    return lax.broadcasted_iota(jnp.int32, shape, axis)


def expand(values, spread):
    high, low = two_parts(values)
    return mm(jnp.concatenate([high, low], axis=1), spread)


def head_sum(values, spread):
    high, low = two_parts(values)
    half = spread[:LANES]
    return mm(high, half, NT) + mm(low, half, NT)


def column_of(row, eye):
    return jnp.sum(jnp.where(eye, row, 0.0), axis=1, keepdims=True)


def shifted_rows(current, before):
    rows = current.shape[0]
    joined = jnp.concatenate([before, current], axis=0)
    return [joined[5 + tap : 5 + tap + rows] for tap in range(4)]


def conv_of(shifted, kernel, offset):
    total = offset + kernel[0:1] * shifted[0]
    for tap in range(1, 4):
        total = total + kernel[tap : tap + 1] * shifted[tap]
    return total


def conv_back(grad, after, kernel):
    rows = grad.shape[0]
    joined = jnp.concatenate([grad, after], axis=0)
    total = kernel[3:4] * grad
    for tap in range(3):
        total = total + kernel[tap : tap + 1] * joined[3 - tap : 3 - tap + rows]
    return total


def piece_context(seg_sm, span_sm, seg_row, step_pre, bias, rate, seq, piece):
    rows = STRETCH
    i0, i1 = iota((rows, rows), 0), iota((rows, rows), 1)
    eye = i0 == i1
    seg_r = seg_row[...]
    seg_c = column_of(seg_r, eye)
    first = span_sm[seq, 0]
    image = jnp.logical_and(piece >= first, piece < first + span_sm[seq, 1])
    reach_all = jnp.where(image, 2 * rows, 0)
    same = seg_c == seg_r
    order = i0 - i1
    allowed = jnp.logical_and(same, order + reach_all >= 0)
    start = piece * rows
    last_doc = seg_sm[seq, start + rows - 1].astype(F32)
    before_doc = seg_sm[seq, jnp.maximum(start - 1, 0)].astype(F32)
    pre = step_pre + bias
    tail = jnp.exp(-jnp.abs(pre))
    step = jnp.maximum(pre, 0.0) + jnp.log1p(tail)
    log_step = step * rate
    high, low = two_parts(log_step)
    lowest = (log_step - high.astype(F32) - low.astype(F32)).astype(BF16)
    ahead = (order >= 0).astype(F32)
    cum = mm(ahead, high) + mm(ahead, low) + mm(ahead, lowest)
    cum = cum * LOG2E
    end = cum[rows - 1 : rows]
    to_end = jnp.where(seg_c == last_doc, jnp.exp2(end - cum), 0.0)
    reach = jnp.where(seg_c == before_doc, jnp.exp2(cum), 0.0)
    keep = jnp.where(last_doc == before_doc, jnp.exp2(end), 0.0)
    return eye, order, reach_all, same, allowed, pre, step, log_step, cum, to_end, reach, keep


def forward_kernel(
    channels, seg_sm, span_sm, pre, ss, seg_row, spread, kernel, offset, skip, shared_kernel,
    shared_offset, bias, rate, y_out, state_out, square_out, before, shared_before, state,
):
    seq, piece = pl.program_id(0), pl.program_id(1)
    group = channels // GROUPS

    @pl.when(piece == 0)
    def _():
        before[...] = jnp.zeros_like(before)
        shared_before[...] = jnp.zeros_like(shared_before)
        state[...] = jnp.zeros_like(state)

    width = shared_kernel.shape[1]
    half = width // 2
    shared_pre = ss[:, :width]
    _, _, _, _, allowed, _, step, _, cum, to_end, reach, keep = piece_context(
        seg_sm, span_sm, seg_row, ss[:, width:], bias[...], rate[...], seq, piece
    )
    conv = conv_of(shifted_rows(shared_pre, shared_before[...]), shared_kernel[...], shared_offset[...])
    shared_before[...] = shared_pre[STRETCH - 8 :]
    act = conv * jax.nn.sigmoid(conv)
    b, c = act[:, :half].astype(BF16), act[:, half:].astype(BF16)
    scores = jnp.where(allowed, mm(c, b, NT), 0.0)
    cum_rows = cum.T
    b_cols = b.T
    lane = iota((STRETCH, LANES), 1)
    squares = jnp.zeros((8, STRETCH), F32)
    ones = jnp.ones((8, group), BF16)
    for g in range(GROUPS):
        cols = slice(g * group, (g + 1) * group)
        gate = pre[:, 2 * g * group : (2 * g + 1) * group].astype(F32)
        inner = pre[:, (2 * g + 1) * group : (2 * g + 2) * group].astype(F32)
        v = conv_of(shifted_rows(inner, before[:, cols]), kernel[:, cols], offset[:, cols])
        before[:, cols] = inner[STRETCH - 8 :]
        x = v * jax.nn.sigmoid(v)
        spread_g = spread[:, cols]
        u = x * expand(step, spread_g)
        entering = state[:, cols]
        state_out[0, 0, :, cols] = entering.astype(BF16)
        carried = mm(c, entering) * expand(reach, spread_g)
        keep_row = expand(jnp.broadcast_to(keep, (8, LANES)), spread_g)[0:1]
        state[:, cols] = keep_row * entering + mm(b_cols, u * expand(to_end, spread_g))
        u_low = u.astype(BF16)
        mixed = []
        for pair in range(group // LANES):
            pair_u = u_low[:, pair * LANES : (pair + 1) * LANES]
            halves = []
            for one in range(2):
                head = g * (group // HEAD) + 2 * pair + one
                gap = cum[:, head : head + 1] - cum_rows[head : head + 1]
                halves.append(mm(scores * jnp.exp2(-jnp.abs(gap)), pair_u))
            mixed.append(jnp.where(lane < HEAD, halves[0], halves[1]))
        y = jnp.concatenate(mixed, axis=1) + carried + skip[:, cols] * x
        y_out[:, cols] = y
        gated = y * (gate * jax.nn.sigmoid(gate))
        squares = squares + mm(ones, gated * gated, NT)
    square_out[...] = squares


def gate_kernel(channels, pre, y, grad, scale_row, gain, low_out, coupling_out, gain_grad):
    group = channels // GROUPS

    @pl.when(pl.program_id(0) == 0)
    def _():
        gain_grad[...] = jnp.zeros_like(gain_grad)

    rows = STRETCH
    eye = iota((rows, rows), 0) == iota((rows, rows), 1)
    scale = column_of(scale_row[...], eye)
    ones = jnp.ones((8, group), BF16)
    coupling = jnp.zeros((8, rows), F32)
    for g in range(GROUPS):
        cols = slice(g * group, (g + 1) * group)
        gate = pre[:, 2 * g * group : (2 * g + 1) * group].astype(F32)
        gated = y[:, cols].astype(F32) * (gate * jax.nn.sigmoid(gate))
        product = grad[:, cols].astype(F32) * gated
        scaled = gain[:, cols]
        low_out[:, cols] = (gated * scale * scaled).astype(BF16)
        high, low = two_parts(product * scaled)
        coupling = coupling + mm(ones, high, NT) + mm(ones, low, NT)
        gain_grad[0:1, cols] += jnp.sum(product * scale, axis=0, keepdims=True)
    coupling_out[...] = coupling


def backward_kernel(
    g, heads, first_group, last_group, seg_sm, span_sm, gate_in, inner_in, inner_halo, ss, ss_halo,
    grad_in, y_in, state_in, seg_row, scale_row, pull_row, spread, kernel, offset, skip, gain,
    shared_kernel, shared_offset, bias, rate, *rest,
):
    rest = list(rest)
    chain_in = None if first_group else rest.pop(0)
    low_out, chain_out, conv_grads, head_grads = rest[:4]
    rest = rest[4:]
    shared_grads = rest.pop(0) if last_group else None
    after, lam = rest[:2]
    shared_after = rest[2] if last_group else None
    seq = pl.program_id(0)
    backward_piece = pl.program_id(1)
    pieces = pl.num_programs(1)
    piece = pieces - 1 - backward_piece
    group = gate_in.shape[1]

    @pl.when(backward_piece == 0)
    def _():
        after[...] = jnp.zeros_like(after)
        lam[...] = jnp.zeros_like(lam)
        if last_group:
            shared_after[...] = jnp.zeros_like(shared_after)

    @pl.when(jnp.logical_and(backward_piece == 0, seq == 0))
    def _():
        conv_grads[...] = jnp.zeros_like(conv_grads)
        head_grads[...] = jnp.zeros_like(head_grads)
        if last_group:
            shared_grads[...] = jnp.zeros_like(shared_grads)

    rows = STRETCH
    width = shared_kernel.shape[1]
    half = width // 2
    inside = jnp.where(piece > 0, 1.0, 0.0)
    shared_pre = ss[:, :width]
    eye, order, reach_all, same, allowed, pre, step, log_step, cum, to_end, reach, keep = piece_context(
        seg_sm, span_sm, seg_row, ss[:, width:], bias[...], rate[...], seq, piece
    )
    allowed_t = jnp.logical_and(same, reach_all - order >= 0)
    shared_shifted = shifted_rows(shared_pre, ss_halo[:, :width] * inside)
    conv = conv_of(shared_shifted, shared_kernel[...], shared_offset[...])
    shared_sig = jax.nn.sigmoid(conv)
    act = conv * shared_sig
    b, c = act[:, :half].astype(BF16), act[:, half:].astype(BF16)
    scores = jnp.where(allowed, mm(c, b, NT), 0.0)
    scores_t = jnp.where(allowed_t, mm(b, c, NT), 0.0)
    signed = jnp.where(order > 0, scores, jnp.where(order < 0, -scores, 0.0))
    cum_rows = cum.T
    c_cols = c.T
    lane = iota((rows, LANES), 1)
    head_row = iota((LANES, rows), 0)

    scale = column_of(scale_row[...], eye)
    pull = column_of(pull_row[...], eye)
    gate = gate_in[...].astype(F32)
    y = y_in[...].astype(F32)
    gate_sig = jax.nn.sigmoid(gate)
    silu = gate * gate_sig
    d_gated = scale * (gain[...] * grad_in[...].astype(F32)) - pull * (y * silu)
    low_out[:, :group] = (d_gated * y * (gate_sig + silu * (1.0 - gate_sig))).astype(BF16)
    dy = d_gated * silu

    inner = inner_in[...].astype(F32)
    shifted = shifted_rows(inner, inner_halo[...] * inside)
    v = conv_of(shifted, kernel[...], offset[...])
    sig = jax.nn.sigmoid(v)
    x = v * sig
    spread_g = spread[...]
    step_x = expand(step, spread_g)
    reach_x = expand(reach, spread_g)
    to_end_x = expand(to_end, spread_g)
    keep_row = expand(jnp.broadcast_to(keep, (8, LANES)), spread_g)[0:1]
    u = x * step_x
    u_low = u.astype(BF16)
    dy_low = dy.astype(BF16)
    entering = state_in[0, 0]
    lam_now = lam[...]
    lam_low = lam_now.astype(BF16)
    reached = (dy * reach_x).astype(BF16)
    pulled = mm(b, lam_low) * to_end_x
    d_c = mm(reached, entering, NT)
    d_b = mm(u * to_end_x, lam_low, NT)
    from_start = dy * reach_x * mm(c, entering)
    from_end = u * pulled
    edge = jnp.sum(from_end, axis=0, keepdims=True) + keep_row * jnp.sum(
        lam_now * entering.astype(F32), axis=0, keepdims=True
    )
    lam[...] = keep_row * lam_now + mm(c_cols, reached)

    d_scores = jnp.zeros((rows, rows), F32)
    row_sums = jnp.zeros((rows, LANES), F32)
    col_sums = jnp.zeros((LANES, rows), F32)
    du_parts = []
    for pair in range(group // LANES):
        cols = slice(pair * LANES, (pair + 1) * LANES)
        pair_u, pair_dy = u_low[:, cols], dy_low[:, cols]
        halves = []
        for one in range(2):
            head = g * heads + 2 * pair + one
            own = lane < HEAD if one == 0 else lane >= HEAD
            gap = cum[:, head : head + 1] - cum_rows[head : head + 1]
            decay = jnp.exp2(-jnp.abs(gap))
            d_mix = mm(jnp.where(own, pair_dy, jnp.zeros_like(pair_dy)), pair_u, NT) * decay
            d_scores = d_scores + d_mix
            turned = d_mix * signed
            row_sums = row_sums + jnp.where(lane == head, jnp.sum(turned, axis=1, keepdims=True), 0.0)
            col_sums = col_sums + jnp.where(head_row == head, jnp.sum(turned, axis=0, keepdims=True), 0.0)
            halves.append(mm(scores_t * decay, pair_dy))
        du_parts.append(jnp.where(lane < HEAD, halves[0], halves[1]))
    du = jnp.concatenate(du_parts, axis=1) + pulled
    d_scores = jnp.where(allowed, d_scores, 0.0).astype(BF16)
    d_c = d_c + mm(d_scores, b)
    d_b = d_b + mm(d_scores, c, TN)

    d_cum = row_sums - col_sums.T + head_sum(from_start - from_end, spread_g)
    high, low = two_parts(d_cum)
    behind = (order <= 0).astype(F32)
    d_log = mm(behind, high) + mm(behind, low) + head_sum(jnp.broadcast_to(edge, (8, group)), spread_g)[0:1]
    d_step = (d_log * rate[...] + head_sum(x * du, spread_g)) * jax.nn.sigmoid(pre)
    own_heads = jnp.logical_and(lane >= g * heads, lane < (g + 1) * heads)
    d_step = jnp.where(own_heads, d_step, 0.0)
    head_grads[0:1] += jnp.sum(jnp.where(own_heads, d_log * log_step, 0.0), axis=0, keepdims=True)
    head_grads[1:2] += jnp.sum(d_step, axis=0, keepdims=True)

    dx = step_x * du + skip[...] * dy
    dv = dx * (sig + x * (1.0 - sig))
    low_out[:, group:] = conv_back(dv, after[...], kernel[...]).astype(BF16)
    after[...] = dv[:8]
    for tap in range(4):
        conv_grads[tap : tap + 1] += jnp.sum(dv * shifted[tap], axis=0, keepdims=True)
    conv_grads[4:5] += jnp.sum(dv, axis=0, keepdims=True)
    conv_grads[5:6] += jnp.sum(dy * x, axis=0, keepdims=True)

    d_act = jnp.concatenate([d_b, d_c], axis=1)
    if chain_in is not None:
        d_act = d_act + chain_in[:, :width]
        d_step = d_step + chain_in[:, width:]
    if last_group:
        d_conv = d_act * (shared_sig + act * (1.0 - shared_sig))
        chain_out[:, :width] = conv_back(d_conv, shared_after[...], shared_kernel[...]).astype(BF16)
        chain_out[:, width:] = d_step.astype(BF16)
        shared_after[...] = d_conv[:8]
        for tap in range(4):
            shared_grads[tap : tap + 1] += jnp.sum(d_conv * shared_shifted[tap], axis=0, keepdims=True)
        shared_grads[4:5] += jnp.sum(d_conv, axis=0, keepdims=True)
    else:
        chain_out[:, :width] = d_act
        chain_out[:, width:] = d_step


def whole(shape):
    return pl.BlockSpec(shape, lambda *_: (0,) * len(shape))


def cost(flops, moved):
    return pl.CostEstimate(flops=int(flops), bytes_accessed=int(moved), transcendentals=0)


def scan_forward(segments, spans, pre, ss, seg_row, spread, kernel, offset, skip, shared_kernel, shared_offset, bias, rate):
    seqs, length = segments.shape
    pieces = length // STRETCH
    channels = kernel.shape[1]
    width = shared_kernel.shape[1]
    at = lambda s, p, *_: (s * pieces + p, 0)
    row_at = lambda s, p, *_: (0, s * pieces + p)
    total = seqs * length
    return pl.pallas_call(
        partial(forward_kernel, channels),
        name="scan_forward",
        grid_spec=pltpu.PrefetchScalarGridSpec(
            num_scalar_prefetch=2,
            grid=(seqs, pieces),
            in_specs=[
                pl.BlockSpec((STRETCH, 2 * channels), at),
                pl.BlockSpec((STRETCH, ss.shape[1]), at),
                pl.BlockSpec((1, STRETCH), row_at),
                whole(spread.shape), whole(kernel.shape), whole(offset.shape), whole(skip.shape),
                whole(shared_kernel.shape), whole(shared_offset.shape), whole(bias.shape), whole(rate.shape),
            ],
            out_specs=[
                pl.BlockSpec((STRETCH, channels), at),
                pl.BlockSpec((1, 1, width // 2, channels), lambda s, p, *_: (s, p, 0, 0)),
                pl.BlockSpec((8, STRETCH), row_at),
            ],
            scratch_shapes=[
                pltpu.VMEM((8, channels), F32), pltpu.VMEM((8, width), F32), pltpu.VMEM((width // 2, channels), F32),
            ],
        ),
        out_shape=[
            jax.ShapeDtypeStruct((total, channels), F32),
            jax.ShapeDtypeStruct((seqs, pieces, width // 2, channels), BF16),
            jax.ShapeDtypeStruct((8, total), F32),
        ],
        compiler_params=pltpu.CompilerParams(dimension_semantics=("arbitrary", "arbitrary")),
        cost_estimate=cost(12e9, 24e6),
    )(segments, spans, pre, ss, seg_row, spread, kernel, offset, skip, shared_kernel, shared_offset, bias, rate)


def gate_step(pre, y, grad, scale_row, gain):
    total, channels = y.shape
    at = lambda i: (i, 0)
    row_at = lambda i: (0, i)
    return pl.pallas_call(
        partial(gate_kernel, channels),
        name="gate_norm",
        grid=(total // STRETCH,),
        in_specs=[
            pl.BlockSpec((STRETCH, 2 * channels), at),
            pl.BlockSpec((STRETCH, channels), at),
            pl.BlockSpec((STRETCH, channels), at),
            pl.BlockSpec((1, STRETCH), row_at),
            whole(gain.shape),
        ],
        out_specs=[pl.BlockSpec((STRETCH, channels), at), pl.BlockSpec((8, STRETCH), row_at), whole((8, channels))],
        out_shape=[
            jax.ShapeDtypeStruct((total, channels), BF16),
            jax.ShapeDtypeStruct((8, total), F32),
            jax.ShapeDtypeStruct((8, channels), F32),
        ],
        compiler_params=pltpu.CompilerParams(dimension_semantics=("arbitrary",)),
        cost_estimate=cost(4e9, 20e6),
    )(pre, y, grad, scale_row, gain)


def scan_backward(
    g, segments, spans, pre, ss, grad, y, states, seg_row, scale_row, pull_row, spread, kernel, offset, skip, gain,
    shared_kernel, shared_offset, bias, rate, chain,
):
    seqs, length = segments.shape
    pieces = length // STRETCH
    channels = kernel.shape[1]
    group = channels // GROUPS
    width = shared_kernel.shape[1]
    wide = ss.shape[1]
    total = seqs * length
    last = g == GROUPS - 1
    piece_at = lambda s, p: s * pieces + pieces - 1 - p
    at = lambda col: lambda s, p, *_: (piece_at(s, p), col)
    row_at = lambda s, p, *_: (0, piece_at(s, p))
    halo = lambda rows, col: lambda s, p, *_: (jnp.maximum(piece_at(s, p) * (STRETCH // rows) - 1, 0), col)
    cols = lambda rows: pl.BlockSpec((rows, group), lambda *_: (0, g))
    in_specs = [
        pl.BlockSpec((STRETCH, group), at(2 * g)),
        pl.BlockSpec((STRETCH, group), at(2 * g + 1)),
        pl.BlockSpec((8, group), halo(8, 2 * g + 1)),
        pl.BlockSpec((STRETCH, wide), at(0)),
        pl.BlockSpec((8, wide), halo(8, 0)),
        pl.BlockSpec((STRETCH, group), at(g)),
        pl.BlockSpec((STRETCH, group), at(g)),
        pl.BlockSpec((1, 1, width // 2, group), lambda s, p, *_: (s, pieces - 1 - p, 0, g)),
        pl.BlockSpec((1, STRETCH), row_at),
        pl.BlockSpec((1, STRETCH), row_at),
        pl.BlockSpec((1, STRETCH), row_at),
        cols(spread.shape[0]), cols(kernel.shape[0]), cols(1), cols(1), cols(1),
        whole(shared_kernel.shape), whole(shared_offset.shape), whole(bias.shape), whole(rate.shape),
    ]
    operands = [
        pre, pre, pre, ss, ss, grad, y, states, seg_row, scale_row, pull_row, spread, kernel, offset, skip, gain,
        shared_kernel, shared_offset, bias, rate,
    ]
    if chain is not None:
        in_specs.append(pl.BlockSpec((STRETCH, wide), at(0)))
        operands.append(chain)
    out_specs = [pl.BlockSpec((STRETCH, 2 * group), at(0)), pl.BlockSpec((STRETCH, wide), at(0)), whole((8, group)), whole((8, LANES))]
    out_shape = [
        jax.ShapeDtypeStruct((total, 2 * group), BF16),
        jax.ShapeDtypeStruct((total, wide), BF16 if last else F32),
        jax.ShapeDtypeStruct((8, group), F32),
        jax.ShapeDtypeStruct((8, LANES), F32),
    ]
    scratch = [pltpu.VMEM((8, group), F32), pltpu.VMEM((width // 2, group), F32)]
    if last:
        out_specs.append(whole((8, width)))
        out_shape.append(jax.ShapeDtypeStruct((8, width), F32))
        scratch.append(pltpu.VMEM((8, width), F32))
    return pl.pallas_call(
        partial(backward_kernel, g, group // HEAD, chain is None, last),
        name=f"scan_backward_{g}",
        grid_spec=pltpu.PrefetchScalarGridSpec(
            num_scalar_prefetch=2, grid=(seqs, pieces), in_specs=in_specs, out_specs=out_specs, scratch_shapes=scratch
        ),
        out_shape=out_shape,
        compiler_params=pltpu.CompilerParams(dimension_semantics=("arbitrary", "arbitrary")),
        cost_estimate=cost(14e9, 20e6),
    )(segments, spans, *operands)


def ring_order(devices, across):
    depth = devices // across
    if devices % across or across < 2 or depth < 2 or depth % 2 and across % 2:
        return list(range(devices))
    if across == 2:
        return [z * 2 for z in range(depth)] + [z * 2 + 1 for z in reversed(range(depth))]
    walk = [z * across for z in range(depth)]
    for turn, z in enumerate(reversed(range(depth))):
        xs = range(1, across)
        walk += [z * across + x for x in (xs if turn % 2 == 0 else reversed(xs))]
    return walk


def ring_steps(order, parts, puts):
    n = len(order)
    if n > 8:
        slab = lax.psum_scatter(parts, "dp", scatter_dimension=0, tiled=True)
        puts(0, lax.all_gather(slab, "dp", axis=0, tiled=True).astype(F32))
        return
    place = jnp.asarray([order.index(i) for i in range(n)], jnp.int32)[lax.axis_index("dp")]
    onward = [(order[i], order[(i + 1) % n]) for i in range(n)]
    pairs = {1: onward, -1: [(b, a) for a, b in onward]}
    block = parts.shape[0] // (2 * n)

    def row(way, index):
        return (0 if way > 0 else n * block) + jnp.mod(index, n) * block

    def own(way, index):
        return lax.dynamic_slice_in_dim(parts, row(way, index), block, 0)

    held = {way: own(way, place) for way in (1, -1)}
    for step in range(1, n):
        for way in (1, -1):
            arrived = lax.ppermute(held[way], "dp", pairs[way])
            held[way] = (arrived.astype(F32) + own(way, place - way * step).astype(F32)).astype(BF16)
    for step in range(n):
        for way in (1, -1):
            if step:
                held[way] = lax.ppermute(held[way], "dp", pairs[way])
            puts(row(way, place + way - way * step), held[way].astype(F32))


def tensor_pairs(size):
    core = [(i, i ^ 1) for i in range(size)]
    along = [(i, (i + 2) % size) for i in range(size)]
    return core, along


def gather_rows(rows, size):
    core, along = tensor_pairs(size)
    index = lax.axis_index("tensor")
    block = rows.shape[0]
    out = jnp.zeros((size * block,) + rows.shape[1:], rows.dtype)
    held = rows
    for step in range(size // 2):
        if step:
            held = lax.ppermute(held, "tensor", along)
        origin = jnp.mod(index - 2 * step, size)
        out = lax.dynamic_update_slice_in_dim(out, held, origin * block, 0)
        other = lax.ppermute(held, "tensor", core)
        out = lax.dynamic_update_slice_in_dim(out, other, (origin ^ 1) * block, 0)
    return out


def total_over(values, axis, size):
    step = 1
    while step < size:
        values = values + lax.ppermute(values, axis, [(i, i ^ step) for i in range(size)])
        step *= 2
    return values


def body(
    ranks, dps, tokens, pre_gain, weight_gate, weight_inner, weight_step, weight_shared, conv_kernel, conv_offset,
    shared_kernel, shared_offset, step_bias, log_rate, skip_gain, gate_gain, weight_out, cotangent, segments, image_span,
):
    seqs, rows, model = tokens.shape
    length = rows * ranks
    total = seqs * length
    channels = weight_gate.shape[1]
    group = channels // GROUPS
    heads = step_bias.shape[0]
    inner_width = channels * ranks
    width = weight_shared.shape[1]
    index = lax.axis_index("tensor")

    own = tokens.astype(F32)
    row_scale = lax.rsqrt(jnp.mean(own * own, axis=2, keepdims=True) + EPSILON)
    normed_rows = (own * row_scale * pre_gain[None, None, :]).astype(BF16)
    normed_in = jnp.concatenate([gather_rows(normed_rows[s], ranks) for s in range(seqs)], axis=0)
    cot_full = jnp.concatenate([gather_rows(cotangent[s], ranks) for s in range(seqs)], axis=0)

    columns = []
    for g in range(GROUPS):
        cols = slice(g * group, (g + 1) * group)
        columns += [weight_gate[:, cols], weight_inner[:, cols]]
    weight_pre = jnp.concatenate(columns, axis=1)
    weight_ss = jnp.concatenate(
        [weight_shared, weight_step, jnp.zeros((model, LANES - heads), BF16)], axis=1
    )
    pad_heads = lambda values: jnp.pad(values, (0, LANES - heads))[None, :]
    bias = pad_heads(step_bias)
    rate = pad_heads(-jnp.exp(log_rate))
    skip = jnp.repeat(skip_gain, HEAD)[None, :]
    heads_of = (jnp.arange(LANES)[:, None] == (jnp.arange(channels) // HEAD)[None, :]).astype(BF16)
    spread = jnp.concatenate([heads_of, heads_of], axis=0)
    seg_row = segments.astype(F32).reshape(1, total)
    offset_row, shared_offset_row = conv_offset[None, :], shared_offset[None, :]
    gain_row = gate_gain[None, :]

    pre = lax.dot_general(normed_in, weight_pre, NN, preferred_element_type=F32)
    ss = lax.dot_general(normed_in, weight_ss, NN, preferred_element_type=F32)
    y, states, squares = scan_forward(
        segments, image_span, pre, ss, seg_row, spread, conv_kernel, offset_row, skip, shared_kernel, shared_offset_row,
        bias, rate,
    )
    grad = lax.dot_general(cot_full, weight_out, NT, preferred_element_type=F32)
    square_sum = total_over(squares[0:1], "tensor", ranks)
    scale_row = lax.rsqrt(square_sum / inner_width + EPSILON)
    normed_out, coupling, gain_grad = gate_step(pre, y, grad, scale_row, gain_row)
    coupling_sum = total_over(coupling[0:1], "tensor", ranks)
    pull_row = scale_row * scale_row * scale_row / inner_width * coupling_sum

    order = ring_order(dps, ranks // 2)
    grads = {}

    def reduce_into(parts, targets):
        def put(row, values):
            for name, start, count, column in targets:
                grads[name] = lax.dynamic_update_slice(grads[name], values[:, start : start + count], (row, column))

        ring_steps(order, parts, put)

    grads["out"] = jnp.zeros((channels, model), F32)
    grads["gate"] = jnp.zeros((model, channels), F32)
    grads["inner"] = jnp.zeros((model, channels), F32)
    grads["ss"] = jnp.zeros((model, LANES), F32)
    out_part = lax.dot_general(normed_out, cot_full, TN, preferred_element_type=BF16)
    reduce_into(out_part, [("out", 0, model, 0)])
    mixed = lax.dot_general(normed_out, weight_out, NN, preferred_element_type=BF16)

    chain = None
    low_parts, conv_parts, head_grads = [], [], jnp.zeros((8, LANES), F32)
    for g in range(GROUPS):
        result = scan_backward(
            g, segments, image_span, pre, ss, grad, y, states, seg_row, scale_row, pull_row, spread, conv_kernel,
            offset_row, skip, gain_row, shared_kernel, shared_offset_row, bias, rate, chain,
        )
        low, chain = result[0], result[1]
        low_parts.append(low)
        conv_parts.append(result[2])
        head_grads = head_grads + result[3]
        part = lax.dot_general(normed_in, low, TN, preferred_element_type=BF16)
        reduce_into(part, [("gate", 0, group, g * group), ("inner", group, group, g * group)])
    shared_grads = result[4]

    slab = width // ranks
    shared_part = jnp.moveaxis(chain[:, :width].reshape(total, ranks, slab), 1, 0)
    shared_low = lax.psum_scatter(shared_part, "tensor", scatter_dimension=0, tiled=True)[0]
    side = jnp.concatenate(
        [shared_low, chain[:, width : width + heads], jnp.zeros((total, LANES - slab - heads), BF16)], axis=1
    )
    weight_side = jnp.concatenate(
        [
            lax.dynamic_slice_in_dim(weight_shared, index * slab, slab, 1),
            weight_step,
            jnp.zeros((model, LANES - slab - heads), BF16),
        ],
        axis=1,
    )
    side_part = lax.dot_general(normed_in, side, TN, preferred_element_type=BF16)
    reduce_into(side_part, [("ss", 0, LANES, 0)])
    grad_shared = lax.all_gather(grads["ss"][:, :slab].astype(BF16), "tensor", axis=1, tiled=True).astype(F32)
    grad_step = grads["ss"][:, slab : slab + heads]

    blocks, token_blocks = [], []
    pre_gain_grad = jnp.zeros((model,), F32)
    for s in range(seqs):
        part = slice(s * length, (s + 1) * length)
        mixed_rows = lax.psum_scatter(mixed[part], "tensor", scatter_dimension=0, tiled=True)
        blocks.append((own[s] + mixed_rows.astype(F32)).astype(BF16))
    for s in range(seqs):
        part = slice(s * length, (s + 1) * length)
        summed = lax.dot_general(side[part], weight_side, NT, preferred_element_type=F32)
        for g in range(GROUPS):
            weights = weight_pre[:, 2 * g * group : 2 * (g + 1) * group]
            summed = summed + lax.dot_general(low_parts[g][part], weights, NT, preferred_element_type=F32)
        normed_grad = lax.psum_scatter(summed.astype(BF16), "tensor", scatter_dimension=0, tiled=True).astype(F32)
        weighted = normed_grad * pre_gain[None, :]
        scale = row_scale[s]
        projection = jnp.sum(weighted * own[s], axis=1, keepdims=True)
        own_grad = scale * weighted - scale * scale * scale / model * own[s] * projection
        pre_gain_grad = pre_gain_grad + jnp.sum(normed_grad * own[s] * scale, axis=0)
        token_blocks.append((cotangent[s].astype(F32) + own_grad).astype(BF16))

    conv_grads = jnp.concatenate(conv_parts, axis=1)
    packed = jnp.concatenate([conv_grads[:6], gain_grad[0:1], jnp.pad(head_grads[:2], ((0, 0), (0, channels - LANES)))], axis=0)
    packed = total_over(packed, "dp", dps)
    shared_packed = total_over(total_over(shared_grads, "dp", dps), "tensor", ranks)
    gain_total = total_over(total_over(pre_gain_grad[None, :], "dp", dps), "tensor", ranks)[0]
    return (
        jnp.stack(blocks),
        jnp.stack(token_blocks),
        gain_total,
        grads["gate"],
        grads["inner"],
        grad_step,
        grad_shared,
        packed[0:4],
        packed[4],
        shared_packed[0:4],
        shared_packed[4],
        packed[8, :heads],
        packed[7, :heads],
        jnp.sum(packed[5].reshape(heads, HEAD), axis=1),
        packed[6],
        grads["out"],
    )


def solution(mesh):
    placed = (
        P("dp", "tensor", None),
        P(),
        P(None, "tensor"),
        P(None, "tensor"),
        P(None, "tensor"),
        P(),
        P(None, "tensor"),
        P("tensor"),
        P(),
        P(),
        P("tensor"),
        P("tensor"),
        P("tensor"),
        P("tensor"),
        P("tensor", None),
        P("dp", "tensor", None),
        P("dp", None),
        P("dp", None),
    )
    return jax.shard_map(
        partial(body, mesh.shape["tensor"], mesh.shape["dp"]),
        mesh=mesh,
        in_specs=placed,
        out_specs=(
            P("dp", "tensor", None),
            P("dp", "tensor", None),
            P(),
            P(None, "tensor"),
            P(None, "tensor"),
            P(None, "tensor"),
            P(),
            P(None, "tensor"),
            P("tensor"),
            P(),
            P(),
            P("tensor"),
            P("tensor"),
            P("tensor"),
            P("tensor"),
            P("tensor", None),
        ),
        check_vma=False,
    )
```

```python
from functools import partial

import jax
import jax.numpy as jnp
from jax import lax
from jax.experimental import pallas as pl
from jax.experimental.pallas import tpu as pltpu
from jax.sharding import PartitionSpec as P

STRETCH = 256
HEAD = 64
LANES = 128

EPSILON = 1e-05
LOG2E = 1.4426950408889634
BF16 = jnp.bfloat16
F32 = jnp.float32
NN = (((1,), (0,)), ((), ()))
NT = (((1,), (1,)), ((), ()))
TN = (((0,), (0,)), ((), ()))


def mm(left, right, dims=NN):
    return lax.dot_general(left.astype(BF16), right.astype(BF16), dims, preferred_element_type=F32)


def two_parts(values):
    high = values.astype(BF16)
    return high, (values - high.astype(F32)).astype(BF16)


def iota(shape, axis):
    return lax.broadcasted_iota(jnp.int32, shape, axis)


def expand(values, spread):
    high, low = two_parts(values)
    return mm(jnp.concatenate([high, low], axis=1), spread)


def head_sum(values, spread):
    high, low = two_parts(values)
    half = spread[:LANES]
    return mm(high, half, NT) + mm(low, half, NT)


def column_of(row, eye):
    return jnp.sum(jnp.where(eye, row, 0.0), axis=1, keepdims=True)


def token_of(rows):
    return (rows & 7) * (STRETCH // 8) + (rows >> 3)


def lagged(current, before):
    last = current[STRETCH - 24 :]
    top = iota(last.shape, 0) & 7
    first = jnp.where(top == 0, pltpu.roll(before, 17, 0), pltpu.roll(last, 1, 0))
    joined = jnp.concatenate([first, current], axis=0)
    return [joined[8 * tap : 8 * tap + STRETCH] for tap in range(4)]


def leading(current, after):
    first = current[:24]
    top = iota(first.shape, 0) & 7
    last = jnp.where(top == 7, pltpu.roll(after, 7, 0), pltpu.roll(first, 23, 0))
    joined = jnp.concatenate([current, last], axis=0)
    return [joined[24 - 8 * tap : 24 - 8 * tap + STRETCH] for tap in range(4)]


def taps(values, kernel):
    total = kernel[0:1] * values[0]
    for tap in range(1, 4):
        total = total + kernel[tap : tap + 1] * values[tap]
    return total


def column_sum(values):
    return jnp.sum(values, axis=0, keepdims=True)


def piece_context(seg_sm, span_sm, seg_row, step_pre, bias, rate, seq, piece):
    rows = STRETCH
    i0, i1 = token_of(iota((rows, rows), 0)), token_of(iota((rows, rows), 1))
    order = i0 - i1
    eye = order == 0
    seg_r = seg_row[...]
    seg_c = column_of(seg_r, eye)
    first = span_sm[seq, 0]
    image = jnp.logical_and(piece >= first, piece < first + span_sm[seq, 1])
    reach_all = jnp.where(image, 2 * rows, 0)
    same = seg_c == seg_r
    start = piece * rows
    last_doc = seg_sm[seq, start + rows - 1].astype(F32)
    before_doc = seg_sm[seq, jnp.maximum(start - 1, 0)].astype(F32)
    pre = step_pre + bias
    tail = jnp.exp(-jnp.abs(pre))
    step = jnp.maximum(pre, 0.0) + jnp.log1p(tail)
    log_step = step * rate
    high, low = two_parts(log_step)
    lowest = (log_step - high.astype(F32) - low.astype(F32)).astype(BF16)
    ahead = (order >= 0).astype(F32)
    cum = mm(ahead, high) + mm(ahead, low) + mm(ahead, lowest)
    cum = cum * LOG2E
    end = cum[rows - 1 : rows]
    to_end = jnp.where(seg_c == last_doc, jnp.exp2(end - cum), 0.0)
    reach = jnp.where(seg_c == before_doc, jnp.exp2(cum), 0.0)
    keep = jnp.where(last_doc == before_doc, jnp.exp2(end), 0.0)
    sign = jnp.where(order > 0, 1.0, jnp.where(order < 0, -1.0, 0.0))
    return eye, order, reach_all, same, sign, pre, step, log_step, cum, to_end, reach, keep


def forward_kernel(
    channels, slots, seg_sm, span_sm, pre, seg_row, spread, kernel, offset, skip, shared_kernel, shared_offset, bias, rate,
    y_out, gated_out, state_out, square_out, before, shared_before, state,
):
    seq, piece = pl.program_id(0), pl.program_id(1)
    width = shared_kernel.shape[1]
    half = width // 2

    @pl.when(piece == 0)
    def _():
        before[...] = jnp.zeros_like(before)
        shared_before[...] = jnp.zeros_like(shared_before)
        state[...] = jnp.zeros_like(state)

    shared_pre = pre[:, 2 * channels : 2 * channels + width]
    step_columns = pre[:, 2 * channels + width : 2 * channels + width + LANES]
    _, order, reach_all, same, sign, _, step, _, cum, to_end, reach, keep = piece_context(
        seg_sm, span_sm, seg_row, step_columns, bias[...], rate[...], seq, piece
    )
    allowed = jnp.logical_and(same, order + reach_all >= 0)
    conv = taps(lagged(shared_pre, shared_before[...]), shared_kernel) + shared_offset[...]
    shared_before[...] = shared_pre[STRETCH - 24 :]
    act = conv * jax.nn.sigmoid(conv)
    b, c = act[:, :half].astype(BF16), act[:, half:].astype(BF16)
    scores = jnp.where(allowed, mm(c, b, NT), 0.0)
    cum_rows = cum.T
    b_cols = b.T
    lane = iota((STRETCH, LANES), 1)
    spread_all = spread[...]

    gate = pre[:, :channels]
    inner = pre[:, channels : 2 * channels]
    v = taps(lagged(inner, before[...]), kernel) + offset[...]
    before[...] = inner[STRETCH - 24 :]
    x = v * jax.nn.sigmoid(v)
    u = x * expand(step, spread_all)
    entering = state[...]
    state_out[0, 0] = entering.astype(BF16)
    carried = mm(c, entering) * expand(reach, spread_all)
    keep_row = expand(jnp.broadcast_to(keep, (8, LANES)), spread_all)[0:1]
    state[...] = keep_row * entering + mm(b_cols, u * expand(to_end, spread_all))
    u_low = u.astype(BF16)
    mixed = []
    for pair in range(channels // LANES):
        pair_u = u_low[:, pair * LANES : (pair + 1) * LANES]
        halves = []
        for head in (2 * pair, 2 * pair + 1):
            gap = cum[:, head : head + 1] - cum_rows[head : head + 1]
            halves.append(mm(scores * jnp.exp2(gap * sign), pair_u))
        mixed.append(jnp.where(lane < HEAD, halves[0], halves[1]))
    y = jnp.concatenate(mixed, axis=1) + carried + skip[...] * x
    y_out[...] = y
    gated = y * (gate * jax.nn.sigmoid(gate))
    gated_out[...] = gated.astype(BF16)
    square_out[...] = mm(jnp.ones((8, channels), BF16), gated * gated, NT)


def coupling_kernel(slots, gated, grad, gain, coupling_out):
    product = grad[...] * (gated[...].astype(F32) * gain[...])
    coupling_out[...] = mm(jnp.ones((8, gain.shape[1]), BF16), product, NT)


def norm_kernel(slots, gated, scale_row, gain, low_out):
    eye = iota((STRETCH, STRETCH), 0) == iota((STRETCH, STRETCH), 1)
    scale = column_of(scale_row[...], eye)
    low_out[...] = (gated[...].astype(F32) * gain[...] * scale).astype(BF16)


def backward_kernel(
    channels, start, slots, seg_sm, span_sm, pre, halo, grad_in, y_in, state_in, seg_row, scale_row, pull_row, spread, kernel,
    offset, skip, gain, shared_kernel, shared_offset, bias, rate,
    *rest,
):
    earlier = rest[3:6] if start else None
    low_out, shared_out, step_out, channel_grads, head_grads, shared_grads, after, lam, shared_after = rest[-9:]
    seq = pl.program_id(0) + start
    backward_piece = pl.program_id(1)
    piece = pl.num_programs(1) - 1 - backward_piece
    width = shared_kernel.shape[1]
    half = width // 2
    rows = STRETCH

    @pl.when(backward_piece == 0)
    def _():
        after[...] = jnp.zeros_like(after)
        lam[...] = jnp.zeros_like(lam)
        shared_after[...] = jnp.zeros_like(shared_after)

    @pl.when(jnp.logical_and(backward_piece == 0, seq == start))
    def _():
        for i, total in enumerate((channel_grads, head_grads, shared_grads)):
            total[...] = earlier[i][...] if start else jnp.zeros_like(total)

    inside = jnp.where(piece > 0, 1.0, 0.0)
    shared_pre = pre[:, 2 * channels : 2 * channels + width]
    step_columns = pre[:, 2 * channels + width : 2 * channels + width + LANES]
    eye, order, reach_all, same, sign, step_pre, step, log_step, cum, to_end, reach, keep = piece_context(
        seg_sm, span_sm, seg_row, step_columns, bias[...], rate[...], seq, piece
    )
    allowed = jnp.logical_and(same, order + reach_all >= 0)
    allowed_t = jnp.logical_and(same, reach_all - order >= 0)
    conv = taps(lagged(shared_pre, halo[8:32, 2 * channels : 2 * channels + width] * inside), shared_kernel) + shared_offset[...]
    shared_sig = jax.nn.sigmoid(conv)
    act = conv * shared_sig
    b, c = act[:, :half].astype(BF16), act[:, half:].astype(BF16)
    scores = jnp.where(allowed, mm(c, b, NT), 0.0)
    scores_t = jnp.where(allowed_t, mm(b, c, NT), 0.0)
    signed = scores * sign
    cum_rows = cum.T
    c_cols = c.T
    lane = iota((rows, LANES), 1)
    head_row = iota((LANES, rows), 0)

    scale = column_of(scale_row[...], eye)
    pull = column_of(pull_row[...], eye)
    gate = pre[:, :channels]
    y = y_in[...]
    gate_sig = jax.nn.sigmoid(gate)
    silu = gate * gate_sig
    gated = y * silu
    scaled_grad = scale * grad_in[...]
    d_gated = gain[...] * scaled_grad - pull * gated
    low_out[:, :channels] = (d_gated * y * (gate_sig + silu * (1.0 - gate_sig))).astype(BF16)
    channel_grads[6:7] += column_sum(scaled_grad * gated)
    dy = d_gated * silu

    inner = pre[:, channels : 2 * channels]
    v = taps(lagged(inner, halo[8:32, channels : 2 * channels] * inside), kernel) + offset[...]
    sig = jax.nn.sigmoid(v)
    x = v * sig
    spread_all = spread[...]
    step_x = expand(step, spread_all)
    to_end_x = expand(to_end, spread_all)
    keep_row = expand(jnp.broadcast_to(keep, (8, LANES)), spread_all)[0:1]
    u = x * step_x
    u_low = u.astype(BF16)
    dy_low = dy.astype(BF16)
    entering = state_in[0, 0]
    lam_now = lam[...]
    lam_low = lam_now.astype(BF16)
    reached_full = dy * expand(reach, spread_all)
    reached = reached_full.astype(BF16)
    pulled = mm(b, lam_low) * to_end_x
    d_c = mm(reached, entering, NT)
    d_b = mm(u * to_end_x, lam_low, NT)
    from_start = reached_full * mm(c, entering)
    from_end = u * pulled
    edge = column_sum(from_end) + keep_row * column_sum(lam_now * entering.astype(F32))
    lam[...] = keep_row * lam_now + mm(c_cols, reached)

    d_scores = jnp.zeros((rows, rows), F32)
    row_sums = jnp.zeros((rows, LANES), F32)
    col_sums = jnp.zeros((LANES, rows), F32)
    du_parts = []
    for pair in range(channels // LANES):
        cols = slice(pair * LANES, (pair + 1) * LANES)
        pair_u, pair_dy = u_low[:, cols], dy_low[:, cols]
        halves = []
        for one in range(2):
            head = 2 * pair + one
            own = lane < HEAD if one == 0 else lane >= HEAD
            gap = cum[:, head : head + 1] - cum_rows[head : head + 1]
            decay = jnp.exp2(gap * sign)
            d_mix = mm(jnp.where(own, pair_dy, jnp.zeros_like(pair_dy)), pair_u, NT) * decay
            d_scores = d_scores + d_mix
            turned = d_mix * signed
            row_sums = row_sums + jnp.where(lane == head, jnp.sum(turned, axis=1, keepdims=True), 0.0)
            col_sums = col_sums + jnp.where(head_row == head, column_sum(turned), 0.0)
            halves.append(mm(scores_t * decay, pair_dy))
        du_parts.append(jnp.where(lane < HEAD, halves[0], halves[1]))
    du = jnp.concatenate(du_parts, axis=1) + pulled
    d_scores = jnp.where(allowed, d_scores, 0.0).astype(BF16)
    d_c = d_c + mm(d_scores, b)
    d_b = d_b + mm(d_scores, c, TN)

    d_cum = row_sums - col_sums.T + head_sum(from_start - from_end, spread_all)
    high, low = two_parts(d_cum)
    behind = (order <= 0).astype(F32)
    d_log = mm(behind, high) + mm(behind, low) + head_sum(jnp.broadcast_to(edge, (8, channels)), spread_all)[0:1]
    d_step = (d_log * rate[...] + head_sum(x * du, spread_all)) * jax.nn.sigmoid(step_pre)
    d_step = jnp.where(lane < channels // HEAD, d_step, 0.0)
    step_out[...] = d_step.astype(BF16)
    head_grads[0:1] += column_sum(d_log * log_step)
    head_grads[1:2] += column_sum(d_step)

    dx = step_x * du + skip[...] * dy
    dv = dx * (sig + x * (1.0 - sig))
    ahead = leading(dv, after[...])
    after[...] = dv[:24]
    low_out[:, channels:] = taps(ahead, kernel).astype(BF16)
    for tap in range(4):
        channel_grads[tap : tap + 1] += column_sum(ahead[tap] * inner)
    channel_grads[4:5] += column_sum(dv)
    channel_grads[5:6] += column_sum(dy * x)

    d_conv = jnp.concatenate([d_b, d_c], axis=1) * (shared_sig + act * (1.0 - shared_sig))
    ahead = leading(d_conv, shared_after[...])
    shared_after[...] = d_conv[:24]
    shared_out[...] = taps(ahead, shared_kernel).astype(BF16)
    for tap in range(4):
        shared_grads[tap : tap + 1] += column_sum(ahead[tap] * shared_pre)
    shared_grads[4:5] += column_sum(d_conv)


def whole(shape):
    return pl.BlockSpec(shape, lambda *_: (0,) * len(shape))


def limits(mebibytes):
    return pltpu.CompilerParams(vmem_limit_bytes=mebibytes << 20)


def cost(flops, moved):
    return pl.CostEstimate(flops=int(flops), bytes_accessed=int(moved), transcendentals=0)


def fill_kernel(dims, spans, first, own, other, *rest):
    weights = rest[: len(spans)]
    product, joined, held, sems = rest[-4:]
    rows = own.shape[0]
    tile = product.shape[1]
    part = min(tile, 256)
    index, step = pl.program_id(0), pl.program_id(1)
    copies = [
        pltpu.make_async_copy(block, joined.at[pl.ds((2 * i + first) * rows, rows)], sems.at[i])
        for i, block in enumerate((own, other))
    ]
    for i, block in enumerate((own, other)):

        @pl.when(jnp.logical_and(index == 0, step == i))
        def _():
            copies[i].start()
            held[i] = block[...]

    for (start, count), weight in zip(spans, weights):

        @pl.when(jnp.logical_and(index >= start, index < start + count))
        def _():
            @pl.loop(0, tile // part)
            def _(piece):
                cols = pl.ds(pl.multiple_of(piece * part, part), part)
                own_weight = weight[:, cols] if dims == NN else weight[cols, :]
                product[:, cols] = lax.dot_general(held[step], own_weight, dims, preferred_element_type=F32)

    @pl.when(jnp.logical_and(index == pl.num_programs(0) - 1, step == 1))
    def _():
        for copy in copies:
            copy.wait()


def fill_rows(own, other, weights, dims, filled):
    rows, depth = own.shape
    side = 1 if dims == NN else 0
    widths = [values.shape[side] for values in weights]
    tile = min(512, *widths)
    spans, first = [], 0
    for width in widths:
        spans.append((first, width // tile))
        first += width // tile
    second = filled is not None
    anywhere = pl.BlockSpec(memory_space=pl.ANY)

    def weight_spec(span):
        column = lambda j: jnp.clip(j - span[0], 0, span[1] - 1)
        if dims == NN:
            return pl.BlockSpec((depth, tile), lambda j, i: (0, column(j)))
        return pl.BlockSpec((tile, depth), lambda j, i: (column(j), 0))

    count = len(weights)
    block = lambda i: 2 * i + (1 if second else 0)
    return pl.pallas_call(
        partial(fill_kernel, dims, spans, 1 if second else 0),
        name="fill_rows",
        grid=(first, 2),
        in_specs=[whole(own.shape), whole(other.shape)]
        + [weight_spec(span) for span in spans]
        + ([anywhere] * 2 if second else []),
        out_specs=[
            pl.BlockSpec((rows, tile), lambda j, i: (block(i), j)),
            anywhere,
        ],
        out_shape=[jax.ShapeDtypeStruct((4 * rows, sum(widths)), F32), jax.ShapeDtypeStruct((4 * rows, depth), BF16)],
        scratch_shapes=[pltpu.VMEM((2, rows, depth), BF16), pltpu.SemaphoreType.DMA((2,))],
        input_output_aliases={2 + count: 0, 3 + count: 1} if second else {},
        compiler_params=limits(36),
        cost_estimate=cost(4 * rows * depth * sum(widths), 4 * rows * (depth + sum(widths))),
    )(own, other, *weights, *(filled if second else ()))


def blank(shape):
    return pl.pallas_call(
        lambda out: None, name="blank", out_specs=pl.BlockSpec(memory_space=pl.ANY), out_shape=jax.ShapeDtypeStruct(shape, F32)
    )()


def scan_forward(slots, segments, spans, pre, seg_row, spread, kernel, offset, skip, shared_kernel, shared_offset, bias, rate):
    seqs, length = segments.shape
    pieces = length // STRETCH
    channels = kernel.shape[1]
    width = shared_kernel.shape[1]
    at = lambda s, p, where, *_: (where[p] * seqs + s, 0)
    row_at = lambda s, p, *_: (0, s * pieces + p)
    total = seqs * length
    return pl.pallas_call(
        partial(forward_kernel, channels),
        name="scan_forward",
        grid_spec=pltpu.PrefetchScalarGridSpec(
            num_scalar_prefetch=3,
            grid=(seqs, pieces),
            in_specs=[
                pl.BlockSpec((STRETCH, pre.shape[1]), at),
                pl.BlockSpec((1, STRETCH), row_at),
                whole(spread.shape), whole(kernel.shape), whole(offset.shape), whole(skip.shape),
                whole(shared_kernel.shape), whole(shared_offset.shape), whole(bias.shape), whole(rate.shape),
            ],
            out_specs=[
                pl.BlockSpec((STRETCH, channels), at),
                pl.BlockSpec((STRETCH, channels), at),
                pl.BlockSpec((1, 1, width // 2, channels), lambda s, p, *_: (s, p, 0, 0)),
                pl.BlockSpec((8, STRETCH), row_at),
            ],
            scratch_shapes=[
                pltpu.VMEM((24, channels), F32), pltpu.VMEM((24, width), F32), pltpu.VMEM((width // 2, channels), F32),
            ],
        ),
        out_shape=[
            jax.ShapeDtypeStruct((total, channels), F32),
            jax.ShapeDtypeStruct((total, channels), BF16),
            jax.ShapeDtypeStruct((seqs, pieces, width // 2, channels), BF16),
            jax.ShapeDtypeStruct((8, total), F32),
        ],
        compiler_params=pltpu.CompilerParams(dimension_semantics=("arbitrary", "arbitrary")),
        cost_estimate=cost(20e9, 40e6),
    )(slots, segments, spans, pre, seg_row, spread, kernel, offset, skip, shared_kernel, shared_offset, bias, rate)


def coupling_step(slots, seqs, gated, grad, gain):
    total, channels = gated.shape
    pieces = total // STRETCH // seqs
    at = lambda s, p, where: (where[p] * seqs + s, 0)
    return pl.pallas_call(
        coupling_kernel,
        name="coupling",
        grid_spec=pltpu.PrefetchScalarGridSpec(
            num_scalar_prefetch=1,
            grid=(seqs, pieces),
            in_specs=[pl.BlockSpec((STRETCH, channels), at), pl.BlockSpec((STRETCH, channels), at), whole(gain.shape)],
            out_specs=pl.BlockSpec((8, STRETCH), lambda s, p, *_: (0, s * pieces + p)),
        ),
        out_shape=jax.ShapeDtypeStruct((8, total), F32),
        compiler_params=limits(8),
        cost_estimate=cost(2e9, 12e6),
    )(slots, gated, grad, gain)


def norm_step(slots, seqs, gated, scale_row, gain):
    total, channels = gated.shape
    pieces = total // STRETCH // seqs
    at = lambda s, p, where: (where[p] * seqs + s, 0)
    return pl.pallas_call(
        norm_kernel,
        name="norm_rows",
        grid_spec=pltpu.PrefetchScalarGridSpec(
            num_scalar_prefetch=1,
            grid=(seqs, pieces),
            in_specs=[
                pl.BlockSpec((STRETCH, channels), at),
                pl.BlockSpec((1, STRETCH), lambda s, p, *_: (0, s * pieces + p)),
                whole(gain.shape),
            ],
            out_specs=pl.BlockSpec((STRETCH, channels), at),
        ),
        out_shape=jax.ShapeDtypeStruct((total, channels), BF16),
        compiler_params=limits(8),
        cost_estimate=cost(1e9, 8e6),
    )(slots, gated, scale_row, gain)


def scan_backward(
    start, count, done, slots, segments, spans, pre, grad, y, states, seg_row, scale_row, pull_row, spread, kernel, offset, skip, gain,
    shared_kernel, shared_offset, bias, rate,
):
    seqs, length = segments.shape
    pieces = length // STRETCH
    channels = kernel.shape[1]
    width = shared_kernel.shape[1]
    total = seqs * length
    piece_at = lambda p: pieces - 1 - p
    at = lambda s, p, where, *_: (where[piece_at(p)] * seqs + s + start, 0)
    row_at = lambda s, p, *_: (0, (s + start) * pieces + piece_at(p))
    halo_at = lambda s, p, where, *_: (
        (where[jnp.maximum(piece_at(p) - 1, 0)] * seqs + s + start) * (STRETCH // 32) + STRETCH // 32 - 1, 0
    )
    plain_at = lambda s, p, *_: ((s + start) * pieces + piece_at(p), 0)
    return pl.pallas_call(
        partial(backward_kernel, channels, start),
        name="scan_backward",
        grid_spec=pltpu.PrefetchScalarGridSpec(
            num_scalar_prefetch=3,
            grid=(count, pieces),
            in_specs=[
                pl.BlockSpec((STRETCH, pre.shape[1]), at),
                pl.BlockSpec((32, pre.shape[1]), halo_at),
                pl.BlockSpec((STRETCH, channels), at),
                pl.BlockSpec((STRETCH, channels), at),
                pl.BlockSpec((1, 1, width // 2, channels), lambda s, p, *_: (s + start, piece_at(p), 0, 0)),
                pl.BlockSpec((1, STRETCH), row_at),
                pl.BlockSpec((1, STRETCH), row_at),
                pl.BlockSpec((1, STRETCH), row_at),
                whole(spread.shape), whole(kernel.shape), whole(offset.shape), whole(skip.shape), whole(gain.shape),
                whole(shared_kernel.shape), whole(shared_offset.shape), whole(bias.shape), whole(rate.shape),
            ]
            + ([pl.BlockSpec(memory_space=pl.ANY)] * 3 + [whole(values.shape) for values in done[3:]] if start else []),
            out_specs=[
                pl.BlockSpec((STRETCH, 2 * channels), at),
                pl.BlockSpec((STRETCH, width), plain_at),
                pl.BlockSpec((STRETCH, LANES), at),
                whole((8, channels)),
                whole((8, LANES)),
                whole((8, width)),
            ],
            scratch_shapes=[
                pltpu.VMEM((24, channels), F32), pltpu.VMEM((width // 2, channels), F32), pltpu.VMEM((24, width), F32),
            ],
        ),
        out_shape=[
            jax.ShapeDtypeStruct((total, 2 * channels), BF16),
            jax.ShapeDtypeStruct((total, width), BF16),
            jax.ShapeDtypeStruct((total, LANES), BF16),
            jax.ShapeDtypeStruct((8, channels), F32),
            jax.ShapeDtypeStruct((8, LANES), F32),
            jax.ShapeDtypeStruct((8, width), F32),
        ],
        input_output_aliases={20: 0, 21: 1, 22: 2} if start else {},
        compiler_params=pltpu.CompilerParams(dimension_semantics=("arbitrary", "arbitrary")),
        cost_estimate=cost(22e9 * count, 30e6 * count),
    )(
        slots, segments, spans, pre, pre, grad, y, states, seg_row, scale_row, pull_row, spread, kernel, offset, skip, gain,
        shared_kernel, shared_offset, bias, rate, *(done if start else ()),
    )


def ring_order(devices, across):
    depth = devices // across
    if devices % across or across < 2 or depth < 2 or depth % 2 and across % 2:
        return list(range(devices))
    if across == 2:
        return [z * 2 for z in range(depth)] + [z * 2 + 1 for z in reversed(range(depth))]
    walk = [z * across for z in range(depth)]
    for turn, z in enumerate(reversed(range(depth))):
        xs = range(1, across)
        walk += [z * across + x for x in (xs if turn % 2 == 0 else reversed(xs))]
    return walk


class Numbers:
    def __init__(self, axis, size, columns):
        self.names = {name: i for i, name in enumerate(columns)}
        table = jnp.asarray([[values(i) for values in columns.values()] for i in range(size)], jnp.int32)
        row = lax.dynamic_slice(table, (lax.axis_index(axis), 0), (1, len(columns)), allow_negative_indices=False)
        self.row = lax.optimization_barrier(row)

    def __getitem__(self, name):
        return self.row[0, self.names[name]]


def rows_at(values, start, count, axis=0):
    starts = [start if i == axis else 0 for i in range(values.ndim)]
    sizes = [count if i == axis else size for i, size in enumerate(values.shape)]
    return lax.dynamic_slice(values, starts, sizes, allow_negative_indices=False)


def put_at(values, update, row, column=0):
    return lax.dynamic_update_slice(values, update, (row, column), allow_negative_indices=False)


WAYS = (1, -1)


class Ring:
    def __init__(self, devices, across, height, halved):
        self.size = n = devices
        self.order = order = ring_order(devices, across)
        self.block = block = height // (2 * n)
        self.eighth = eighth = halved // 8
        onward = [(order[i], order[(i + 1) % n]) for i in range(n)]
        self.pairs = {1: onward, -1: [(b, a) for a, b in onward]}
        columns = {}
        for step in range(n):
            for kind, lead in (("add", 0), ("store", 1)):
                for way in WAYS:
                    columns[kind, step, way] = lambda i, w=way, s=step, d=lead: (0 if w > 0 else n) + (
                        order.index(i) + w * (d - s)
                    ) % n
            for way in WAYS:

                def eighth_of(i, w=way, s=step):
                    origin = order[(order.index(i) - w * s) % n]
                    return 2 * ((origin & 1) * 4 + (origin >> 1 & 1) * 2 + (origin >> 2 & 1)) + (0 if w > 0 else 1)

                columns["side", step, way] = eighth_of
        for way in WAYS:
            columns["first", way] = lambda i, w=way: (0 if w > 0 else n * block) + order.index(i) * block
        for bit in range(3):
            columns["keep", bit] = lambda i, k=bit: (i >> k & 1) * (halved >> k + 1)
            columns["give", bit] = lambda i, k=bit: (1 - (i >> k & 1)) * (halved >> k + 1)
        self.at = Numbers("dp", n, columns)

    def exchange(self, values, bit):
        return lax.ppermute(values, "dp", [(i, i ^ (1 << bit)) for i in range(self.size)])

    def add(self, parts, arrived, step):
        shape = (self.block, parts.shape[1])
        first = self.at.names["add", step, 1]

        def kernel(row, one, two, came_one, came_two, out_one, out_two):
            out_one[...] = (came_one[...].astype(F32) + one[...].astype(F32)).astype(BF16)
            out_two[...] = (came_two[...].astype(F32) + two[...].astype(F32)).astype(BF16)

        return pl.pallas_call(
            kernel,
            name="ring_add",
            grid_spec=pltpu.PrefetchScalarGridSpec(
                num_scalar_prefetch=1,
                grid=(1,),
                in_specs=[
                    pl.BlockSpec(shape, lambda i, row: (row[0, first], 0)),
                    pl.BlockSpec(shape, lambda i, row: (row[0, first + 1], 0)),
                    whole(shape),
                    whole(shape),
                ],
                out_specs=[whole(shape), whole(shape)],
            ),
            out_shape=[jax.ShapeDtypeStruct(shape, BF16)] * 2,
            compiler_params=limits(8),
            cost_estimate=cost(1e6, 4e6),
        )(self.at.row, parts, parts, *arrived)

    def store(self, sums, held, step):
        block, height = self.block, self.eighth // 2
        channels, model = sums[0].shape[1], sums[2].shape[1]
        first, side = self.at.names["store", step, 1], self.at.names["side", step, 1]

        def kernel(row, one, two, *rest):
            gate, inner, out = rest[3:]
            for way, source in enumerate((one, two)):

                @pl.when(pl.program_id(0) == way)
                def _():
                    gate[...] = source[:block, :channels].astype(F32)
                    inner[...] = source[:block, channels:].astype(F32)
                    out[...] = source[block:, :].astype(F32)

        low_spec = pl.BlockSpec((block, channels), lambda i, row: (row[0, first + i], 0))
        return pl.pallas_call(
            kernel,
            name="ring_store",
            grid_spec=pltpu.PrefetchScalarGridSpec(
                num_scalar_prefetch=1,
                grid=(2,),
                in_specs=[whole(held[0].shape), whole(held[1].shape)] + [pl.BlockSpec(memory_space=pl.ANY)] * 3,
                out_specs=[low_spec, low_spec, pl.BlockSpec((height, model), lambda i, row: (row[0, side + i], 0))],
            ),
            out_shape=[jax.ShapeDtypeStruct(values.shape, F32) for values in sums],
            input_output_aliases={3: 0, 4: 1, 5: 2},
            compiler_params=limits(12),
            cost_estimate=cost(1e6, 6e6),
        )(self.at.row, *held, *sums)

    def all_reduce(self, parts, sums, fillers, finished):
        n, fillers = self.size, list(fillers)

        def send(held):
            arrived = [lax.ppermute(values, "dp", self.pairs[way]) for way, values in zip(WAYS, held)]
            made = fillers.pop(0)(lambda values: after(values, *held)) if fillers else []
            return lax.optimization_barrier((*arrived, *made))[:2]

        held = [rows_at(parts, self.at["first", way], self.block) for way in WAYS]
        for step in range(1, n):
            held = self.add(parts, send(held), step)
        extra = finished()
        half = extra.shape[0] // 2
        held = [jnp.concatenate([held[0], extra[:half]], axis=0), jnp.concatenate([held[1], extra[half:]], axis=0)]
        for step in range(n):
            if step:
                held = send(held)
            sums = self.store(sums, held, step)
        for filler in fillers:
            filler(lambda values: values)
        return sums


class Ranks:
    def __init__(self, size, slab):
        self.size, self.along = size, size // 2
        along = self.along

        def owner(i, slot):
            other, place = divmod(slot, along)
            return ((i - 2 * place) % size) ^ other

        def slot(i, owner):
            other = (owner ^ i) & 1
            return other * along + (i - (owner ^ other)) % size // 2

        columns = {}
        for k in range(size):
            columns["owner", k] = lambda i, k=k: owner(i, k)
        for k in range(size):
            columns["slot", k] = lambda i, k=k: slot(i, k)
        columns["slab"] = lambda i: i * slab
        self.at = Numbers("tensor", size, columns)

    def core(self, values):
        return lax.ppermute(values, "tensor", [(i, i ^ 1) for i in range(self.size)])

    def shift(self, values, places):
        return lax.ppermute(values, "tensor", [(i, (i + 2 * places) % self.size) for i in range(self.size)])

    def gather(self, own):
        held = [own]
        for _ in range(1, self.along):
            held.append(self.shift(held[-1], 1))
        return jnp.concatenate(held + [self.core(values) for values in held], axis=0)


def total_over(values, axis, size):
    step = 1
    while step < size:
        values = values + lax.ppermute(values, axis, [(i, i ^ step) for i in range(size)])
        step *= 2
    return values


def after(values, *earlier):
    return lax.optimization_barrier((values, *earlier))[0]


def body(
    ranks, dps, tokens, pre_gain, weight_gate, weight_inner, weight_step, weight_shared, conv_kernel, conv_offset,
    shared_kernel, shared_offset, step_bias, log_rate, skip_gain, gate_gain, weight_out, cotangent, segments, image_span,
):
    seqs, rows, model = tokens.shape
    length = rows * ranks
    pieces = length // STRETCH
    total = seqs * length
    channels = weight_gate.shape[1]
    heads = step_bias.shape[0]
    inner_width = channels * ranks
    width = weight_shared.shape[1]
    slab = width // ranks
    group = Ranks(ranks, slab)
    local = rows == STRETCH

    mixer = (token_of(jnp.arange(STRETCH))[:, None] == jnp.arange(STRETCH)[None, :]).astype(BF16)

    def reorder(values, dims=NN):
        blocks = values.reshape(-1, STRETCH, values.shape[-1])
        moved = [lax.dot_general(mixer, blocks[i], dims, preferred_element_type=BF16) for i in range(blocks.shape[0])]
        return jnp.concatenate(moved, axis=0).reshape(values.shape)

    def gather(values):
        if local:
            return group.gather(values.reshape(seqs * rows, model))
        every = lax.all_gather(values, "tensor", axis=1, tiled=True).reshape(seqs, pieces, STRETCH, model)
        return reorder(jnp.moveaxis(every, 1, 0)).reshape(total, model)

    def scatter(values):
        every = jnp.moveaxis(reorder(values, TN).reshape(pieces, seqs, STRETCH, model), 0, 1).reshape(seqs, length, model)
        return lax.psum_scatter(every, "tensor", scatter_dimension=1, tiled=True).astype(F32)

    def slabs(values):
        blocks = values.reshape(seqs, pieces, STRETCH, values.shape[-1])
        if not local:
            return jnp.moveaxis(blocks, 1, 0).reshape(values.shape)
        return jnp.concatenate(
            [rows_at(blocks, group.at["owner", slot], 1, 1)[:, 0] for slot in range(ranks)], axis=0
        ).reshape(values.shape)

    slots = jnp.arange(pieces, dtype=jnp.int32)
    if local:
        first = group.at.names["slot", 0]
        slots = group.at.row[0, first : first + pieces]
    own_low = reorder(tokens) if local else tokens
    cot_low = reorder(cotangent) if local else cotangent
    own = own_low.astype(F32)
    row_scale = lax.rsqrt(jnp.mean(own * own, axis=2, keepdims=True) + EPSILON)
    normed_low = (own * row_scale * pre_gain[None, None, :]).astype(BF16)
    tail = min(512, channels) - width - heads
    weight_ss = jnp.concatenate([weight_shared, weight_step, jnp.zeros((model, tail), BF16)], axis=1)
    pad_heads = lambda values: jnp.pad(values, (0, LANES - heads))[None, :]
    bias = pad_heads(step_bias)
    rate = pad_heads(-jnp.exp(log_rate))
    skip = jnp.repeat(skip_gain, HEAD)[None, :]
    heads_of = (jnp.arange(LANES)[:, None] == (jnp.arange(channels) // HEAD)[None, :]).astype(BF16)
    spread = jnp.concatenate([heads_of, heads_of], axis=0)
    seg_row = jnp.swapaxes(segments.astype(F32).reshape(seqs, pieces, 8, STRETCH // 8), 2, 3).reshape(1, total)
    offset_row, shared_offset_row = conv_offset[None, :], shared_offset[None, :]
    gain_row = gate_gain[None, :]

    blocked = local and ranks == 4
    if blocked:
        own_rows, cot_rows = normed_low.reshape(seqs * rows, model), cot_low.reshape(seqs * rows, model)
        far_rows = group.shift(own_rows, 1)
        far_cot = group.shift(after(cot_rows, own_rows), 1)
        weights = (weight_gate, weight_inner, weight_ss)
        first = fill_rows(own_rows, group.core(own_rows), weights, NN, None)
        first_cot = fill_rows(cot_rows, group.core(cot_rows), (weight_out,), NT, None)
        far_rows = after(far_rows, first[0], first_cot[0])
        pre, normed_in = fill_rows(far_rows, group.core(far_rows), weights, NN, first)
    else:
        normed_in, cot_full = gather(normed_low), gather(cot_low)
        weights = jnp.concatenate([weight_gate, weight_inner, weight_ss], axis=1)
        pre = lax.dot_general(normed_in, weights, NN, preferred_element_type=F32)
        grad = lax.dot_general(cot_full, weight_out, NT, preferred_element_type=F32)
    y, gated, states, squares = scan_forward(
        slots, segments, image_span, pre, seg_row, spread, conv_kernel, offset_row, skip, shared_kernel, shared_offset_row,
        bias, rate,
    )
    if blocked:
        far_cot = after(far_cot, squares)
        grad, cot_full = fill_rows(far_cot, group.core(far_cot), (weight_out,), NT, first_cot)
    coupling = coupling_step(slots, seqs, gated, grad, gain_row)
    sums = total_over(jnp.concatenate([squares[0:1], coupling[0:1]], axis=0), "tensor", ranks)
    scale_row = lax.rsqrt(sums[0:1] / inner_width + EPSILON)
    pull_row = scale_row * scale_row * scale_row / inner_width * sums[1:2]
    normed_out = norm_step(slots, seqs, gated, scale_row, gain_row)

    def backward(start, count, done, pull):
        return scan_backward(
            start, count, done, slots, segments, image_span, pre, grad, y, states, seg_row, scale_row, pull, spread,
            conv_kernel, offset_row, skip, gain_row, shared_kernel, shared_offset_row, bias, rate,
        )

    out_product = lambda left: lax.dot_general(left, cot_full, TN, preferred_element_type=BF16)
    made = {}
    ringed = dps == 8 and seqs > 1 and model == 2 * channels
    if ringed:
        ring = Ring(dps, ranks // 2, model, channels)
        join = lambda mine, arrived: (mine.astype(F32) + arrived.astype(F32)).astype(BF16)
        part_of = lambda values, kind, bit, axis=0: rows_at(values, ring.at[kind, bit], channels >> bit + 1, axis)
        given = out_product(part_of(normed_out, "give", 0, 1))
        arrived = ring.exchange(given, 0)
        kept = out_product(after(part_of(normed_out, "keep", 0, 1), given))
        low, shared_part, step_low, channel_grads, head_grads, shared_grads = backward(0, seqs, None, after(pull_row, kept))
        kept = join(after(kept, low), arrived)
        given = part_of(kept, "give", 1)
        arrived = ring.exchange(given, 1)
        low_part = lax.dot_general(normed_in, after(low, given), TN, preferred_element_type=BF16)
        made["quarter"] = part_of(kept, "keep", 1), arrived
    else:
        out_sum = lax.psum(out_product(normed_out), "dp")
        low, shared_part, step_low, channel_grads, head_grads, shared_grads = backward(0, seqs, None, pull_row)
        low_part = lax.dot_general(normed_in, low, TN, preferred_element_type=BF16)

    cut = total // 2 if local else 0
    half = ranks // 2
    weight_low = jnp.concatenate([weight_gate, weight_inner], axis=1)
    weight_side = jnp.concatenate(
        [
            rows_at(weight_shared, group.at["slab"], slab, 1),
            weight_step,
            jnp.zeros((model, LANES - slab - heads), BF16),
        ],
        axis=1,
    )
    by_rank = lambda values: values.reshape(-1, seqs, rows, model)

    def quarter_join(hold):
        mine, other = made["quarter"]
        kept = join(hold(mine), other)
        given = part_of(kept, "give", 2)
        made["eighth"] = part_of(kept, "keep", 2), ring.exchange(given, 2)
        return [given]

    def finished(hold=lambda values: values):
        if "finished" not in made:
            made["finished"] = join(hold(made["eighth"][0]), made["eighth"][1])
        return made["finished"]

    def finish(hold):
        return [finished(hold)] if ringed else []

    def columns_out(hold):
        columns = jnp.moveaxis(hold(shared_part).reshape(total, ranks, slab), 1, 0)
        columns = jnp.concatenate([rows_at(columns, group.at["owner", slot], 1) for slot in range(ranks)], axis=0)
        made["columns"] = columns[:half], group.core(columns[half:])
        return [columns] + (quarter_join(hold) if ringed else [])

    def columns_in(hold):
        shared_low = slabs(take_rows("columns", hold).astype(BF16))
        made["side"] = jnp.concatenate([shared_low, step_low[:, :heads], jnp.zeros((total, LANES - slab - heads), BF16)], axis=1)
        return [made["side"]]

    def pass_on(name):
        def run(hold):
            mine, other = made[name]
            sent = [(hold(mine)[i].astype(F32) + other[i].astype(F32)).astype(BF16) for i in range(1, half)]
            made[name] = mine[0], [other[0]] + [group.shift(values, -1 - i) for i, values in enumerate(sent)]
            return sent

        return run if local or name == "columns" else lambda hold: []

    def take_rows(name, hold):
        mine, others = made[name]
        mine = hold(mine).astype(F32)
        for values in others:
            mine = mine + values.astype(F32)
        return mine

    def input_rows_of(slot):
        part = slice(slot * seqs * rows, (slot + 1) * seqs * rows) if local else slice(0, total)

        def run(hold):
            side, low_rows = lax.optimization_barrier((hold(made["side"]), low))
            summed = lax.dot_general(side[part], weight_side, NT, preferred_element_type=F32)
            summed = (summed + lax.dot_general(low_rows[part], weight_low, NT, preferred_element_type=F32)).astype(BF16)
            if local:
                made["input", slot] = by_rank(summed)[0]
                if slot >= half:
                    made["input", slot] = group.core(made["input", slot])
            else:
                made["input"] = scatter(summed), []
            return [summed]

        return run

    def input_pair(hold):
        if local:
            made["input"] = [made["input", slot] for slot in range(half)], [made["input", slot] for slot in range(half, ranks)]
        return []

    def mix_of(slots, far):
        part = slice(slots.start * seqs * rows, slots.stop * seqs * rows) if local else slice(0, total)

        def run(hold):
            product = lax.dot_general(hold(normed_out[part]), weight_out, NN, preferred_element_type=BF16)
            if not local:
                made["mixed"] = scatter(product), []
            elif far:
                made["mixed far"] = group.core(by_rank(product))
            else:
                made["mixed"] = by_rank(product), made["mixed far"]
            return [product]

        return run

    def side_product(hold):
        made["side_part"] = lax.dot_general(normed_in, hold(made["side"]), TN, preferred_element_type=BF16)
        return [made["side_part"]]

    def input_rows(hold):
        normed_grad = take_rows("input", hold)
        weighted = normed_grad * pre_gain[None, None, :]
        projection = jnp.sum(weighted * own, axis=2, keepdims=True)
        own_grad = row_scale * weighted - row_scale * row_scale * row_scale / model * own * projection
        made["pre_gain"] = jnp.sum(normed_grad * own * row_scale, axis=(0, 1))
        made["tokens_grad"] = (cot_low.astype(F32) + own_grad).astype(BF16)
        return [made["tokens_grad"], made["pre_gain"]]

    def input_order(hold):
        if local:
            made["tokens_grad"] = reorder(hold(made["tokens_grad"]), TN)
        return [made["tokens_grad"]]

    def block_rows(hold):
        made["block_out"] = (own + take_rows("mixed", hold)).astype(BF16)
        return [made["block_out"]]

    def block_order(hold):
        if local:
            made["block_out"] = reorder(hold(made["block_out"]), TN)
        return [made["block_out"]]

    def small_start(hold):
        made["small"] = jnp.concatenate(
            [jnp.pad(hold(shared_grads), ((0, 0), (0, channels - width))), made["pre_gain"].reshape(-1, channels)], axis=0
        )
        return []

    def pack(hold):
        made["small"] = jnp.concatenate(
            [channel_grads, jnp.pad(head_grads, ((0, 0), (0, channels - LANES))), made["small"]], axis=0
        )
        return []

    def spread_sum(name, axis, size, bits, kind=F32):
        partners = [0]
        for bit in bits:
            partners += [partner ^ (1 << bit) for partner in partners]

        def send(hold):
            values = hold(made[name])
            made[name] = values, [lax.ppermute(values, axis, [(i, i ^ k) for i in range(size)]) for k in partners[1:]]
            return [values]

        def receive(hold):
            values, others = made[name]
            terms = [hold(values).astype(F32)] + [other.astype(F32) for other in others]
            while len(terms) > 1:
                terms = [terms[i] + terms[i + 1] for i in range(0, len(terms), 2)]
            made[name] = terms[0].astype(kind)
            return [made[name]]

        return send, receive

    def together(*parts):
        def run(hold):
            return [value for part in parts for value in part(hold)]

        return run

    bits_of = lambda size: list(range((size - 1).bit_length()))
    tensor_send, tensor_take = spread_sum("small", "tensor", ranks, bits_of(ranks))
    small_dp = [spread_sum("small", "dp", dps, bits) for bits in (bits_of(dps)[:1], bits_of(dps)[1:])]
    if ringed:
        side_dp = [spread_sum("side_part", "dp", dps, [bit], BF16) for bit in range(3)]
    else:

        def side_whole(hold):
            made["side_part"] = lax.psum(made["side_part"], "dp")
            return []

        side_dp = [(side_whole, lambda hold: [])] + [(lambda hold: [], lambda hold: [])] * 2
    nothing = lambda hold: []
    far = [input_rows_of(slot) for slot in (range(half, ranks) if local else range(1))]
    near = [input_rows_of(slot) for slot in (range(half) if local else range(0))]
    def gather_near(hold):
        slabs_of = hold(made["side_part"])[:, :slab]
        made["gathered"] = [slabs_of]
        for _ in range(1, half):
            made["gathered"].append(group.shift(made["gathered"][-1], 1))
        return []

    def gather_far(hold):
        made["gathered"] = made["gathered"] + [group.core(hold(values)) for values in made["gathered"]]
        return []

    fillers = [
        columns_out,
        together(pass_on("columns"), mix_of(range(half, ranks), True) if local else nothing),
        together(columns_in, side_product),
        together(side_dp[0][0], *far[:1]),
        *far[1:],
        together(side_dp[0][1], side_dp[1][0], *near[:1], finish),
        *near[1:],
        together(input_pair, pass_on("input"), side_dp[1][1], side_dp[2][0], mix_of(range(half), False)),
        pass_on("mixed"),
        together(input_rows, side_dp[2][1]),
        together(small_start, tensor_send, input_order, gather_near),
        together(tensor_take, pack, small_dp[0][0], block_rows),
        together(small_dp[0][1], small_dp[1][0], block_order, gather_far),
    ]
    if ringed:
        sums = [blank((model, channels)), blank((model, channels)), blank((channels, model))]
        grads = dict(zip(("gate", "inner", "out"), ring.all_reduce(low_part, sums, fillers, finished)))
    else:
        low_sum = lax.psum(low_part, "dp").astype(F32)
        grads = {"gate": low_sum[:, :channels], "inner": low_sum[:, channels:], "out": out_sum.astype(F32)}
        for filler in fillers:
            filler(lambda values: values)
    plain = lambda values: values
    small_dp[1][1](plain)
    packed, side_sum = made["small"], made["side_part"]
    block_out, tokens_grad, grad_out = made["block_out"], made["tokens_grad"], grads["out"]
    gathered = jnp.stack(made["gathered"])
    grad_shared = jnp.concatenate(
        [rows_at(gathered, group.at["slot", owner], 1)[0] for owner in range(ranks)], axis=1
    ).astype(F32)
    grad_step = side_sum[:, slab : slab + heads].astype(F32)

    shared_sums = packed[16:24, :width]
    return (
        block_out,
        tokens_grad,
        packed[24:].reshape(model),
        grads["gate"],
        grads["inner"],
        grad_step,
        grad_shared,
        packed[0:4],
        packed[4],
        shared_sums[0:4],
        shared_sums[4],
        packed[9, :heads],
        packed[8, :heads],
        jnp.sum(packed[5].reshape(heads, HEAD), axis=1),
        packed[6],
        grad_out,
    )


def solution(mesh):
    placed = (
        P("dp", "tensor", None),
        P(),
        P(None, "tensor"),
        P(None, "tensor"),
        P(None, "tensor"),
        P(),
        P(None, "tensor"),
        P("tensor"),
        P(),
        P(),
        P("tensor"),
        P("tensor"),
        P("tensor"),
        P("tensor"),
        P("tensor", None),
        P("dp", "tensor", None),
        P("dp", None),
        P("dp", None),
    )
    return jax.shard_map(
        partial(body, mesh.shape["tensor"], mesh.shape["dp"]),
        mesh=mesh,
        in_specs=placed,
        out_specs=(
            P("dp", "tensor", None),
            P("dp", "tensor", None),
            P(),
            P(None, "tensor"),
            P(None, "tensor"),
            P(None, "tensor"),
            P(),
            P(None, "tensor"),
            P("tensor"),
            P(),
            P(),
            P("tensor"),
            P("tensor"),
            P("tensor"),
            P("tensor"),
            P("tensor", None),
        ),
        check_vma=False,
    )
```

```python
from functools import partial

import jax
import jax.numpy as jnp
from jax import lax
from jax.experimental import pallas as pl
from jax.experimental.pallas import tpu as pltpu
from jax.sharding import PartitionSpec as P

STRETCH = 256
HEAD = 64
LANES = 128

EPSILON = 1e-05
LOG2E = 1.4426950408889634
BF16 = jnp.bfloat16
F32 = jnp.float32
NN = (((1,), (0,)), ((), ()))
NT = (((1,), (1,)), ((), ()))
TN = (((0,), (0,)), ((), ()))


def mm(left, right, dims=NN):
    return lax.dot_general(left.astype(BF16), right.astype(BF16), dims, preferred_element_type=F32)


def two_parts(values):
    high = values.astype(BF16)
    return high, (values - high.astype(F32)).astype(BF16)


def iota(shape, axis):
    return lax.broadcasted_iota(jnp.int32, shape, axis)


def expand(values, spread):
    high, low = two_parts(values)
    return mm(jnp.concatenate([high, low], axis=1), spread)


def head_sum(values, spread):
    high, low = two_parts(values)
    half = spread[:LANES]
    return mm(high, half, NT) + mm(low, half, NT)


def column_of(row, eye):
    return jnp.sum(jnp.where(eye, row, 0.0), axis=1, keepdims=True)


def token_of(rows):
    return (rows & 7) * (STRETCH // 8) + (rows >> 3)


def lagged(current, before):
    last = current[STRETCH - 24 :]
    top = iota(last.shape, 0) & 7
    first = jnp.where(top == 0, pltpu.roll(before, 17, 0), pltpu.roll(last, 1, 0))
    joined = jnp.concatenate([first, current], axis=0)
    return [joined[8 * tap : 8 * tap + STRETCH] for tap in range(4)]


def leading(current, after):
    first = current[:24]
    top = iota(first.shape, 0) & 7
    last = jnp.where(top == 7, pltpu.roll(after, 7, 0), pltpu.roll(first, 23, 0))
    joined = jnp.concatenate([current, last], axis=0)
    return [joined[24 - 8 * tap : 24 - 8 * tap + STRETCH] for tap in range(4)]


def taps(values, kernel):
    total = kernel[0:1] * values[0]
    for tap in range(1, 4):
        total = total + kernel[tap : tap + 1] * values[tap]
    return total


def column_sum(values):
    return jnp.sum(values, axis=0, keepdims=True)


def piece_context(seg_sm, span_sm, seg_row, step_pre, bias, rate, seq, piece):
    rows = STRETCH
    i0, i1 = token_of(iota((rows, rows), 0)), token_of(iota((rows, rows), 1))
    order = i0 - i1
    eye = order == 0
    seg_r = seg_row[...]
    seg_c = column_of(seg_r, eye)
    first = span_sm[seq, 0]
    image = jnp.logical_and(piece >= first, piece < first + span_sm[seq, 1])
    reach_all = jnp.where(image, 2 * rows, 0)
    same = seg_c == seg_r
    start = piece * rows
    last_doc = seg_sm[seq, start + rows - 1].astype(F32)
    before_doc = seg_sm[seq, jnp.maximum(start - 1, 0)].astype(F32)
    pre = step_pre + bias
    tail = jnp.exp(-jnp.abs(pre))
    step = jnp.maximum(pre, 0.0) + jnp.log1p(tail)
    log_step = step * rate
    high, low = two_parts(log_step)
    lowest = (log_step - high.astype(F32) - low.astype(F32)).astype(BF16)
    ahead = (order >= 0).astype(F32)
    cum = mm(ahead, high) + mm(ahead, low) + mm(ahead, lowest)
    cum = cum * LOG2E
    end = cum[rows - 1 : rows]
    to_end = jnp.where(seg_c == last_doc, jnp.exp2(end - cum), 0.0)
    reach = jnp.where(seg_c == before_doc, jnp.exp2(cum), 0.0)
    keep = jnp.where(last_doc == before_doc, jnp.exp2(end), 0.0)
    sign = jnp.where(order > 0, 1.0, jnp.where(order < 0, -1.0, 0.0))
    return eye, order, reach_all, same, sign, pre, step, log_step, cum, to_end, reach, keep


def forward_kernel(
    channels, slots, seg_sm, span_sm, pre, seg_row, spread, kernel, offset, skip, shared_kernel, shared_offset, bias, rate,
    y_out, gated_out, state_out, square_out, before, shared_before, state,
):
    seq, piece = pl.program_id(0), pl.program_id(1)
    width = shared_kernel.shape[1]
    half = width // 2

    @pl.when(piece == 0)
    def _():
        before[...] = jnp.zeros_like(before)
        shared_before[...] = jnp.zeros_like(shared_before)
        state[...] = jnp.zeros_like(state)

    shared_pre = pre[:, 2 * channels : 2 * channels + width]
    step_columns = pre[:, 2 * channels + width : 2 * channels + width + LANES]
    _, order, reach_all, same, sign, _, step, _, cum, to_end, reach, keep = piece_context(
        seg_sm, span_sm, seg_row, step_columns, bias[...], rate[...], seq, piece
    )
    allowed = jnp.logical_and(same, order + reach_all >= 0)
    conv = taps(lagged(shared_pre, shared_before[...]), shared_kernel) + shared_offset[...]
    shared_before[...] = shared_pre[STRETCH - 24 :]
    act = conv * jax.nn.sigmoid(conv)
    b, c = act[:, :half].astype(BF16), act[:, half:].astype(BF16)
    scores = jnp.where(allowed, mm(c, b, NT), 0.0)
    cum_rows = cum.T
    b_cols = b.T
    lane = iota((STRETCH, LANES), 1)
    spread_all = spread[...]

    gate = pre[:, :channels]
    inner = pre[:, channels : 2 * channels]
    v = taps(lagged(inner, before[...]), kernel) + offset[...]
    before[...] = inner[STRETCH - 24 :]
    x = v * jax.nn.sigmoid(v)
    u = x * expand(step, spread_all)
    entering = state[...]
    state_out[0, 0] = entering.astype(BF16)
    carried = mm(c, entering) * expand(reach, spread_all)
    keep_row = expand(jnp.broadcast_to(keep, (8, LANES)), spread_all)[0:1]
    state[...] = keep_row * entering + mm(b_cols, u * expand(to_end, spread_all))
    u_low = u.astype(BF16)
    mixed = []
    for pair in range(channels // LANES):
        pair_u = u_low[:, pair * LANES : (pair + 1) * LANES]
        halves = []
        for head in (2 * pair, 2 * pair + 1):
            gap = cum[:, head : head + 1] - cum_rows[head : head + 1]
            halves.append(mm(scores * jnp.exp2(gap * sign), pair_u))
        mixed.append(jnp.where(lane < HEAD, halves[0], halves[1]))
    y = jnp.concatenate(mixed, axis=1) + carried + skip[...] * x
    y_out[...] = y
    gated = y * (gate * jax.nn.sigmoid(gate))
    gated_out[...] = gated.astype(BF16)
    square_out[...] = mm(jnp.ones((8, channels), BF16), gated * gated, NT)[0:1]


def coupling_kernel(slots, gated, grad, gain, coupling_out):
    product = grad[...].astype(F32) * (gated[...].astype(F32) * gain[...])
    coupling_out[...] = mm(jnp.ones((8, gain.shape[1]), BF16), product, NT)[0:1]


def norm_kernel(slots, gated, scale_row, gain, low_out):
    eye = iota((STRETCH, STRETCH), 0) == iota((STRETCH, STRETCH), 1)
    scale = column_of(scale_row[...], eye)
    low_out[...] = (gated[...].astype(F32) * gain[...] * scale).astype(BF16)


def backward_kernel(
    channels, start, slots, seg_sm, span_sm, pre, halo, grad_in, y_in, state_in, seg_row, scale_row, pull_row, spread, kernel,
    offset, skip, gain, shared_kernel, shared_offset, bias, rate,
    *rest,
):
    earlier = rest[3:6] if start else None
    low_out, shared_out, step_out, channel_grads, head_grads, shared_grads, after, lam, shared_after = rest[-9:]
    seq = pl.program_id(0) + start
    backward_piece = pl.program_id(1)
    piece = pl.num_programs(1) - 1 - backward_piece
    width = shared_kernel.shape[1]
    half = width // 2
    rows = STRETCH

    @pl.when(backward_piece == 0)
    def _():
        after[...] = jnp.zeros_like(after)
        lam[...] = jnp.zeros_like(lam)
        shared_after[...] = jnp.zeros_like(shared_after)

    @pl.when(jnp.logical_and(backward_piece == 0, seq == start))
    def _():
        for i, total in enumerate((channel_grads, head_grads, shared_grads)):
            total[...] = earlier[i][...] if start else jnp.zeros_like(total)

    inside = jnp.where(piece > 0, 1.0, 0.0)
    shared_pre = pre[:, 2 * channels : 2 * channels + width]
    step_columns = pre[:, 2 * channels + width : 2 * channels + width + LANES]
    eye, order, reach_all, same, sign, step_pre, step, log_step, cum, to_end, reach, keep = piece_context(
        seg_sm, span_sm, seg_row, step_columns, bias[...], rate[...], seq, piece
    )
    allowed = jnp.logical_and(same, order + reach_all >= 0)
    allowed_t = jnp.logical_and(same, reach_all - order >= 0)
    conv = taps(lagged(shared_pre, halo[8:32, 2 * channels : 2 * channels + width] * inside), shared_kernel) + shared_offset[...]
    shared_sig = jax.nn.sigmoid(conv)
    act = conv * shared_sig
    b, c = act[:, :half].astype(BF16), act[:, half:].astype(BF16)
    scores = jnp.where(allowed, mm(c, b, NT), 0.0)
    scores_t = jnp.where(allowed_t, mm(b, c, NT), 0.0)
    signed = scores * sign
    cum_rows = cum.T
    c_cols = c.T
    lane = iota((rows, LANES), 1)
    head_row = iota((LANES, rows), 0)

    scale = column_of(scale_row[...], eye)
    pull = column_of(pull_row[...], eye)
    gate = pre[:, :channels]
    y = y_in[...]
    gate_sig = jax.nn.sigmoid(gate)
    silu = gate * gate_sig
    gated = y * silu
    scaled_grad = scale * grad_in[...].astype(F32)
    d_gated = gain[...] * scaled_grad - pull * gated
    low_out[:, :channels] = (d_gated * y * (gate_sig + silu * (1.0 - gate_sig))).astype(BF16)
    channel_grads[6:7] += column_sum(scaled_grad * gated)
    dy = d_gated * silu

    inner = pre[:, channels : 2 * channels]
    v = taps(lagged(inner, halo[8:32, channels : 2 * channels] * inside), kernel) + offset[...]
    sig = jax.nn.sigmoid(v)
    x = v * sig
    spread_all = spread[...]
    step_x = expand(step, spread_all)
    to_end_x = expand(to_end, spread_all)
    keep_row = expand(jnp.broadcast_to(keep, (8, LANES)), spread_all)[0:1]
    u = x * step_x
    u_low = u.astype(BF16)
    dy_low = dy.astype(BF16)
    entering = state_in[0, 0]
    lam_now = lam[...]
    lam_low = lam_now.astype(BF16)
    reached_full = dy * expand(reach, spread_all)
    reached = reached_full.astype(BF16)
    pulled = mm(b, lam_low) * to_end_x
    d_c = mm(reached, entering, NT)
    d_b = mm(u * to_end_x, lam_low, NT)
    from_start = reached_full * mm(c, entering)
    from_end = u * pulled
    edge = column_sum(from_end) + keep_row * column_sum(lam_now * entering.astype(F32))
    lam[...] = keep_row * lam_now + mm(c_cols, reached)

    d_scores = jnp.zeros((rows, rows), F32)
    row_sums = jnp.zeros((rows, LANES), F32)
    col_sums = jnp.zeros((LANES, rows), F32)
    du_parts = []
    for pair in range(channels // LANES):
        cols = slice(pair * LANES, (pair + 1) * LANES)
        pair_u, pair_dy = u_low[:, cols], dy_low[:, cols]
        halves = []
        for one in range(2):
            head = 2 * pair + one
            own = lane < HEAD if one == 0 else lane >= HEAD
            gap = cum[:, head : head + 1] - cum_rows[head : head + 1]
            decay = jnp.exp2(gap * sign)
            d_mix = mm(jnp.where(own, pair_dy, jnp.zeros_like(pair_dy)), pair_u, NT) * decay
            d_scores = d_scores + d_mix
            turned = d_mix * signed
            row_sums = row_sums + jnp.where(lane == head, jnp.sum(turned, axis=1, keepdims=True), 0.0)
            col_sums = col_sums + jnp.where(head_row == head, column_sum(turned), 0.0)
            halves.append(mm(scores_t * decay, pair_dy))
        du_parts.append(jnp.where(lane < HEAD, halves[0], halves[1]))
    du = jnp.concatenate(du_parts, axis=1) + pulled
    d_scores = jnp.where(allowed, d_scores, 0.0).astype(BF16)
    d_c = d_c + mm(d_scores, b)
    d_b = d_b + mm(d_scores, c, TN)

    d_cum = row_sums - col_sums.T + head_sum(from_start - from_end, spread_all)
    high, low = two_parts(d_cum)
    behind = (order <= 0).astype(F32)
    d_log = mm(behind, high) + mm(behind, low) + head_sum(jnp.broadcast_to(edge, (8, channels)), spread_all)[0:1]
    d_step = (d_log * rate[...] + head_sum(x * du, spread_all)) * jax.nn.sigmoid(step_pre)
    d_step = jnp.where(lane < channels // HEAD, d_step, 0.0)
    step_out[...] = d_step.astype(BF16)
    head_grads[0:1] += column_sum(d_log * log_step)
    head_grads[1:2] += column_sum(d_step)

    dx = step_x * du + skip[...] * dy
    dv = dx * (sig + x * (1.0 - sig))
    ahead = leading(dv, after[...])
    after[...] = dv[:24]
    low_out[:, channels:] = taps(ahead, kernel).astype(BF16)
    for tap in range(4):
        channel_grads[tap : tap + 1] += column_sum(ahead[tap] * inner)
    channel_grads[4:5] += column_sum(dv)
    channel_grads[5:6] += column_sum(dy * x)

    d_conv = jnp.concatenate([d_b, d_c], axis=1) * (shared_sig + act * (1.0 - shared_sig))
    ahead = leading(d_conv, shared_after[...])
    shared_after[...] = d_conv[:24]
    shared_out[...] = taps(ahead, shared_kernel).astype(BF16)
    for tap in range(4):
        shared_grads[tap : tap + 1] += column_sum(ahead[tap] * shared_pre)
    shared_grads[4:5] += column_sum(d_conv)


def whole(shape):
    return pl.BlockSpec(shape, lambda *_: (0,) * len(shape))


def limits(mebibytes):
    return pltpu.CompilerParams(vmem_limit_bytes=mebibytes << 20)


def cost(flops, moved):
    return pl.CostEstimate(flops=int(flops), bytes_accessed=int(moved), transcendentals=0)


def fill_kernel(dims, spans, first, own, other, *rest):
    weights = rest[: len(spans)]
    product, joined, held, sems = rest[-4:]
    rows = own.shape[0]
    tile = product.shape[1]
    index, step = pl.program_id(0), pl.program_id(1)
    copies = [
        pltpu.make_async_copy(block, joined.at[pl.ds((2 * i + first) * rows, rows)], sems.at[i])
        for i, block in enumerate((own, other))
    ]
    for i, block in enumerate((own, other)):

        @pl.when(jnp.logical_and(index == 0, step == i))
        def _():
            copies[i].start()
            held[i] = block[...]

    for (start, count), weight in zip(spans, weights):

        @pl.when(jnp.logical_and(index >= start, index < start + count))
        def _():
            product[...] = lax.dot_general(held[step], weight[...], dims, preferred_element_type=F32).astype(product.dtype)

    @pl.when(jnp.logical_and(index == pl.num_programs(0) - 1, step == 1))
    def _():
        for copy in copies:
            copy.wait()


def fill_rows(own, other, weights, dims, filled, kind=F32):
    rows, depth = own.shape
    side = 1 if dims == NN else 0
    widths = [values.shape[side] for values in weights]
    tile = min(512, *widths)
    spans, first = [], 0
    for width in widths:
        spans.append((first, width // tile))
        first += width // tile
    second = filled is not None
    anywhere = pl.BlockSpec(memory_space=pl.ANY)

    def weight_spec(span):
        column = lambda j: jnp.clip(j - span[0], 0, span[1] - 1)
        if dims == NN:
            return pl.BlockSpec((depth, tile), lambda j, i: (0, column(j)))
        return pl.BlockSpec((tile, depth), lambda j, i: (column(j), 0))

    count = len(weights)
    block = lambda i: 2 * i + (1 if second else 0)
    return pl.pallas_call(
        partial(fill_kernel, dims, spans, 1 if second else 0),
        name="fill_rows",
        grid=(first, 2),
        in_specs=[whole(own.shape), whole(other.shape)]
        + [weight_spec(span) for span in spans]
        + ([anywhere] * 2 if second else []),
        out_specs=[
            pl.BlockSpec((rows, tile), lambda j, i: (block(i), j)),
            anywhere,
        ],
        out_shape=[jax.ShapeDtypeStruct((4 * rows, sum(widths)), kind), jax.ShapeDtypeStruct((4 * rows, depth), BF16)],
        scratch_shapes=[pltpu.VMEM((2, rows, depth), BF16), pltpu.SemaphoreType.DMA((2,))],
        input_output_aliases={2 + count: 0, 3 + count: 1} if second else {},
        compiler_params=pltpu.CompilerParams(dimension_semantics=("arbitrary", "arbitrary")),
        cost_estimate=cost(4 * rows * depth * sum(widths), 4 * rows * (depth + sum(widths))),
    )(own, other, *weights, *(filled if second else ()))


def blank(shape):
    return pl.pallas_call(
        lambda out: None, name="blank", out_specs=pl.BlockSpec(memory_space=pl.ANY), out_shape=jax.ShapeDtypeStruct(shape, F32)
    )()


def scan_forward(slots, segments, spans, pre, seg_row, spread, kernel, offset, skip, shared_kernel, shared_offset, bias, rate):
    seqs, length = segments.shape
    pieces = length // STRETCH
    channels = kernel.shape[1]
    width = shared_kernel.shape[1]
    at = lambda s, p, where, *_: (where[p] * seqs + s, 0)
    row_at = lambda s, p, *_: (0, s * pieces + p)
    total = seqs * length
    return pl.pallas_call(
        partial(forward_kernel, channels),
        name="scan_forward",
        grid_spec=pltpu.PrefetchScalarGridSpec(
            num_scalar_prefetch=3,
            grid=(seqs, pieces),
            in_specs=[
                pl.BlockSpec((STRETCH, pre.shape[1]), at),
                pl.BlockSpec((1, STRETCH), row_at),
                whole(spread.shape), whole(kernel.shape), whole(offset.shape), whole(skip.shape),
                whole(shared_kernel.shape), whole(shared_offset.shape), whole(bias.shape), whole(rate.shape),
            ],
            out_specs=[
                pl.BlockSpec((STRETCH, channels), at),
                pl.BlockSpec((STRETCH, channels), at),
                pl.BlockSpec((1, 1, width // 2, channels), lambda s, p, *_: (s, p, 0, 0)),
                pl.BlockSpec((1, STRETCH), row_at),
            ],
            scratch_shapes=[
                pltpu.VMEM((24, channels), F32), pltpu.VMEM((24, width), F32), pltpu.VMEM((width // 2, channels), F32),
            ],
        ),
        out_shape=[
            jax.ShapeDtypeStruct((total, channels), F32),
            jax.ShapeDtypeStruct((total, channels), BF16),
            jax.ShapeDtypeStruct((seqs, pieces, width // 2, channels), BF16),
            jax.ShapeDtypeStruct((1, total), F32),
        ],
        compiler_params=pltpu.CompilerParams(dimension_semantics=("arbitrary", "arbitrary")),
        cost_estimate=cost(20e9, 40e6),
    )(slots, segments, spans, pre, seg_row, spread, kernel, offset, skip, shared_kernel, shared_offset, bias, rate)


def coupling_step(slots, seqs, gated, grad, gain):
    total, channels = gated.shape
    pieces = total // STRETCH // seqs
    at = lambda s, p, where: (where[p] * seqs + s, 0)
    return pl.pallas_call(
        coupling_kernel,
        name="coupling",
        grid_spec=pltpu.PrefetchScalarGridSpec(
            num_scalar_prefetch=1,
            grid=(seqs, pieces),
            in_specs=[pl.BlockSpec((STRETCH, channels), at), pl.BlockSpec((STRETCH, channels), at), whole(gain.shape)],
            out_specs=pl.BlockSpec((1, STRETCH), lambda s, p, *_: (0, s * pieces + p)),
        ),
        out_shape=jax.ShapeDtypeStruct((1, total), F32),
        compiler_params=limits(8),
        cost_estimate=cost(2e9, 12e6),
    )(slots, gated, grad, gain)


def split_norm_step(owners, numbers, seqs, gated, scale_row, gain, row, give, keep):
    total, channels = gated.shape
    count = total // STRETCH
    pieces = count // seqs

    def kernel(owners, numbers, gated, scale_row, gain, given, kept, near, far, held):
        eye = iota((STRETCH, STRETCH), 0) == iota((STRETCH, STRETCH), 1)
        scale = column_of(scale_row[...], eye)
        low = (gated[...].astype(F32) * gain[...] * scale).astype(BF16)
        held[...] = low
        for out, name in ((given, give), (kept, keep)):
            start = pl.multiple_of(numbers[0, name] * (channels // 2), LANES)
            out[...] = held[:, pl.ds(start, channels // 2)]

        @pl.when(pl.program_id(0) < count // 2)
        def _():
            near[...] = low

        @pl.when(pl.program_id(0) >= count // 2)
        def _():
            far[...] = low

    at = lambda i, *_: (i, 0)
    half_block = pl.BlockSpec((STRETCH, channels // 2), at)
    return pl.pallas_call(
        kernel,
        name="norm_rows",
        grid_spec=pltpu.PrefetchScalarGridSpec(
            num_scalar_prefetch=2,
            grid=(count,),
            in_specs=[
                pl.BlockSpec((STRETCH, channels), at),
                pl.BlockSpec((1, STRETCH), lambda i, own, *_: (0, i % seqs * pieces + own[i // seqs])),
                whole(gain.shape),
            ],
            out_specs=[
                half_block,
                half_block,
                pl.BlockSpec((STRETCH, channels), lambda i, *_: (jnp.minimum(i, count // 2 - 1), 0)),
                pl.BlockSpec((STRETCH, channels), lambda i, *_: (jnp.maximum(i - count // 2, 0), 0)),
            ],
            scratch_shapes=[pltpu.VMEM((STRETCH, channels), BF16)],
        ),
        out_shape=[jax.ShapeDtypeStruct((total, channels // 2), BF16)] * 2
        + [jax.ShapeDtypeStruct((total // 2, channels), BF16)] * 2,
        compiler_params=limits(12),
        cost_estimate=cost(1e9, 12e6),
    )(owners, numbers, gated, scale_row, gain)


def norm_step(slots, seqs, gated, scale_row, gain):
    total, channels = gated.shape
    pieces = total // STRETCH // seqs
    at = lambda s, p, where: (where[p] * seqs + s, 0)
    return pl.pallas_call(
        norm_kernel,
        name="norm_rows",
        grid_spec=pltpu.PrefetchScalarGridSpec(
            num_scalar_prefetch=1,
            grid=(seqs, pieces),
            in_specs=[
                pl.BlockSpec((STRETCH, channels), at),
                pl.BlockSpec((1, STRETCH), lambda s, p, *_: (0, s * pieces + p)),
                whole(gain.shape),
            ],
            out_specs=pl.BlockSpec((STRETCH, channels), at),
        ),
        out_shape=jax.ShapeDtypeStruct((total, channels), BF16),
        compiler_params=limits(8),
        cost_estimate=cost(1e9, 8e6),
    )(slots, gated, scale_row, gain)


def scan_backward(
    start, count, done, slots, segments, spans, pre, grad, y, states, seg_row, scale_row, pull_row, spread, kernel, offset, skip, gain,
    shared_kernel, shared_offset, bias, rate,
):
    seqs, length = segments.shape
    pieces = length // STRETCH
    channels = kernel.shape[1]
    width = shared_kernel.shape[1]
    total = seqs * length
    piece_at = lambda p: pieces - 1 - p
    at = lambda s, p, where, *_: (where[piece_at(p)] * seqs + s + start, 0)
    row_at = lambda s, p, *_: (0, (s + start) * pieces + piece_at(p))
    halo_at = lambda s, p, where, *_: (
        (where[jnp.maximum(piece_at(p) - 1, 0)] * seqs + s + start) * (STRETCH // 32) + STRETCH // 32 - 1, 0
    )
    plain_at = lambda s, p, *_: ((s + start) * pieces + piece_at(p), 0)
    return pl.pallas_call(
        partial(backward_kernel, channels, start),
        name="scan_backward",
        grid_spec=pltpu.PrefetchScalarGridSpec(
            num_scalar_prefetch=3,
            grid=(count, pieces),
            in_specs=[
                pl.BlockSpec((STRETCH, pre.shape[1]), at),
                pl.BlockSpec((32, pre.shape[1]), halo_at),
                pl.BlockSpec((STRETCH, channels), at),
                pl.BlockSpec((STRETCH, channels), at),
                pl.BlockSpec((1, 1, width // 2, channels), lambda s, p, *_: (s + start, piece_at(p), 0, 0)),
                pl.BlockSpec((1, STRETCH), row_at),
                pl.BlockSpec((1, STRETCH), row_at),
                pl.BlockSpec((1, STRETCH), row_at),
                whole(spread.shape), whole(kernel.shape), whole(offset.shape), whole(skip.shape), whole(gain.shape),
                whole(shared_kernel.shape), whole(shared_offset.shape), whole(bias.shape), whole(rate.shape),
            ]
            + ([pl.BlockSpec(memory_space=pl.ANY)] * 3 + [whole(values.shape) for values in done[3:]] if start else []),
            out_specs=[
                pl.BlockSpec((STRETCH, 2 * channels), at),
                pl.BlockSpec((STRETCH, width), plain_at),
                pl.BlockSpec((STRETCH, LANES), at),
                whole((8, channels)),
                whole((8, LANES)),
                whole((8, width)),
            ],
            scratch_shapes=[
                pltpu.VMEM((24, channels), F32), pltpu.VMEM((width // 2, channels), F32), pltpu.VMEM((24, width), F32),
            ],
        ),
        out_shape=[
            jax.ShapeDtypeStruct((total, 2 * channels), BF16),
            jax.ShapeDtypeStruct((total, width), BF16),
            jax.ShapeDtypeStruct((total, LANES), BF16),
            jax.ShapeDtypeStruct((8, channels), F32),
            jax.ShapeDtypeStruct((8, LANES), F32),
            jax.ShapeDtypeStruct((8, width), F32),
        ],
        input_output_aliases={20: 0, 21: 1, 22: 2} if start else {},
        compiler_params=pltpu.CompilerParams(dimension_semantics=("arbitrary", "arbitrary")),
        cost_estimate=cost(22e9 * count, 30e6 * count),
    )(
        slots, segments, spans, pre, pre, grad, y, states, seg_row, scale_row, pull_row, spread, kernel, offset, skip, gain,
        shared_kernel, shared_offset, bias, rate, *(done if start else ()),
    )


def ring_order(devices, across):
    depth = devices // across
    if devices % across or across < 2 or depth < 2 or depth % 2 and across % 2:
        return list(range(devices))
    if across == 2:
        return [z * 2 for z in range(depth)] + [z * 2 + 1 for z in reversed(range(depth))]
    walk = [z * across for z in range(depth)]
    for turn, z in enumerate(reversed(range(depth))):
        xs = range(1, across)
        walk += [z * across + x for x in (xs if turn % 2 == 0 else reversed(xs))]
    return walk


class Numbers:
    def __init__(self, axis, size, columns):
        self.names = {name: i for i, name in enumerate(columns)}
        table = jnp.asarray([[values(i) for values in columns.values()] for i in range(size)], jnp.int32)
        row = lax.dynamic_slice(table, (lax.axis_index(axis), 0), (1, len(columns)), allow_negative_indices=False)
        self.row = lax.optimization_barrier(row)

    def __getitem__(self, name):
        return self.row[0, self.names[name]]


def rows_at(values, start, count, axis=0):
    starts = [start if i == axis else 0 for i in range(values.ndim)]
    sizes = [count if i == axis else size for i, size in enumerate(values.shape)]
    return lax.dynamic_slice(values, starts, sizes, allow_negative_indices=False)


def put_at(values, update, row, column=0):
    return lax.dynamic_update_slice(values, update, (row, column), allow_negative_indices=False)


WAYS = (1, -1)


class Ring:
    def __init__(self, devices, across, height, halved):
        self.size = n = devices
        self.order = order = ring_order(devices, across)
        self.block = block = height // (2 * n)
        self.eighth = eighth = halved // 8
        onward = [(order[i], order[(i + 1) % n]) for i in range(n)]
        self.pairs = {1: onward, -1: [(b, a) for a, b in onward]}
        columns = {}
        for step in range(n):
            for kind, lead in (("add", 0), ("store", 1)):
                for way in WAYS:
                    columns[kind, step, way] = lambda i, w=way, s=step, d=lead: (0 if w > 0 else n) + (
                        order.index(i) + w * (d - s)
                    ) % n
            for way in WAYS:

                def eighth_of(i, w=way, s=step):
                    origin = order[(order.index(i) - w * s) % n]
                    return 2 * ((origin & 1) * 4 + (origin >> 1 & 1) * 2 + (origin >> 2 & 1)) + (0 if w > 0 else 1)

                columns["side", step, way] = eighth_of
        for bit in range(3):
            columns["give", bit] = lambda i, k=bit: 1 - (i >> k & 1)
            columns["keep", bit] = lambda i, k=bit: i >> k & 1
        self.at = Numbers("dp", n, columns)

    def exchange(self, values, bit):
        return lax.ppermute(values, "dp", [(i, i ^ (1 << bit)) for i in range(self.size)])

    def halve(self, kept, arrived, bit):
        rows, columns = kept.shape
        first = self.at.names["give", bit]

        def kernel(row, mine, other, given, held):
            total = (mine[...].astype(F32) + other[...].astype(F32)).astype(BF16)

            @pl.when(pl.program_id(0) == 0)
            def _():
                given[...] = total

            @pl.when(pl.program_id(0) == 1)
            def _():
                held[...] = total

        half = (rows // 2, columns)
        at = pl.BlockSpec(half, lambda i, row: (row[0, first + i], 0))
        return pl.pallas_call(
            kernel,
            name="halve",
            grid_spec=pltpu.PrefetchScalarGridSpec(
                num_scalar_prefetch=1, grid=(2,), in_specs=[at, at], out_specs=[whole(half), whole(half)]
            ),
            out_shape=[jax.ShapeDtypeStruct(half, BF16)] * 2,
            compiler_params=limits(12),
            cost_estimate=cost(1e6, 4e6),
        )(self.at.row, kept, arrived)

    def add(self, parts, arrived, step, extra=None):
        block, columns = self.block, parts.shape[1]
        shape = (block, columns)
        half = 0 if extra is None else extra.shape[0] // 2
        full = (block + half, columns)
        first = self.at.names["add", step, 1]

        def kernel(row, one, two, *rest):
            out_one, out_two = rest[-2:]
            sources = [one[...].astype(F32), two[...].astype(F32)]
            for i in range(len(arrived)):
                sources[i] = sources[i] + rest[i][...].astype(F32)
            out_one[:block] = sources[0].astype(BF16)
            out_two[:block] = sources[1].astype(BF16)
            if half:
                out_one[block:] = rest[2][:half]
                out_two[block:] = rest[2][half:]

        return pl.pallas_call(
            kernel,
            name="ring_add",
            grid_spec=pltpu.PrefetchScalarGridSpec(
                num_scalar_prefetch=1,
                grid=(1,),
                in_specs=[
                    pl.BlockSpec(shape, lambda i, row: (row[0, first], 0)),
                    pl.BlockSpec(shape, lambda i, row: (row[0, first + 1], 0)),
                ]
                + [whole(shape)] * len(arrived)
                + ([whole(extra.shape)] if half else []),
                out_specs=[whole(full), whole(full)],
            ),
            out_shape=[jax.ShapeDtypeStruct(full, BF16)] * 2,
            compiler_params=limits(10),
            cost_estimate=cost(1e6, 4e6),
        )(self.at.row, parts, parts, *arrived, *([extra] if half else []))

    def store(self, sums, held, step):
        block, height = self.block, self.eighth // 2
        channels, model = sums[0].shape[1], sums[2].shape[1]
        first, side = self.at.names["store", step, 1], self.at.names["side", step, 1]

        def kernel(row, one, two, *rest):
            gate, inner, out = rest[3:]
            for way, source in enumerate((one, two)):

                @pl.when(pl.program_id(0) == way)
                def _():
                    gate[...] = source[:block, :channels].astype(F32)
                    inner[...] = source[:block, channels:].astype(F32)
                    out[...] = source[block:, :].astype(F32)

        low_spec = pl.BlockSpec((block, channels), lambda i, row: (row[0, first + i], 0))
        return pl.pallas_call(
            kernel,
            name="ring_store",
            grid_spec=pltpu.PrefetchScalarGridSpec(
                num_scalar_prefetch=1,
                grid=(2,),
                in_specs=[whole(held[0].shape), whole(held[1].shape)] + [pl.BlockSpec(memory_space=pl.ANY)] * 3,
                out_specs=[low_spec, low_spec, pl.BlockSpec((height, model), lambda i, row: (row[0, side + i], 0))],
            ),
            out_shape=[jax.ShapeDtypeStruct(values.shape, F32) for values in sums],
            input_output_aliases={3: 0, 4: 1, 5: 2},
            compiler_params=limits(12),
            cost_estimate=cost(1e6, 6e6),
        )(self.at.row, *held, *sums)

    def all_reduce(self, parts, sums, fillers, finished):
        n, fillers = self.size, list(fillers)

        def send(held, earlier=()):
            arrived = [lax.ppermute(values, "dp", self.pairs[way]) for way, values in zip(WAYS, held)]
            made = fillers.pop(0)(lambda values: after(values, *held)) if fillers else []
            return lax.optimization_barrier((*arrived, *made, *earlier))[:2]

        held = self.add(parts, (), 0)
        for step in range(1, n):
            held = self.add(parts, send(held), step, finished() if step == n - 1 else None)
        for step in range(n):
            if step:
                held = send(held, sums[:1])
            sums = self.store(sums, held, step)
        for filler in fillers:
            filler(lambda values: values)
        return sums, held


class Ranks:
    def __init__(self, size, slab):
        self.size, self.along = size, size // 2
        along = self.along

        def owner(i, slot):
            other, place = divmod(slot, along)
            return ((i - 2 * place) % size) ^ other

        def slot(i, owner):
            other = (owner ^ i) & 1
            return other * along + (i - (owner ^ other)) % size // 2

        columns = {}
        for k in range(size):
            columns["owner", k] = lambda i, k=k: owner(i, k)
        for k in range(size):
            columns["slot", k] = lambda i, k=k: slot(i, k)
        columns["slab"] = lambda i: i * slab
        self.at = Numbers("tensor", size, columns)

    def core(self, values):
        return lax.ppermute(values, "tensor", [(i, i ^ 1) for i in range(self.size)])

    def shift(self, values, places):
        return lax.ppermute(values, "tensor", [(i, (i + 2 * places) % self.size) for i in range(self.size)])

    def gather(self, own):
        held = [own]
        for _ in range(1, self.along):
            held.append(self.shift(held[-1], 1))
        return jnp.concatenate(held + [self.core(values) for values in held], axis=0)


def total_over(values, axis, size):
    step = 1
    while step < size:
        values = values + lax.ppermute(values, axis, [(i, i ^ step) for i in range(size)])
        step *= 2
    return values


def after(values, *earlier):
    return lax.optimization_barrier((values, *earlier))[0]


def body(
    ranks, dps, tokens, pre_gain, weight_gate, weight_inner, weight_step, weight_shared, conv_kernel, conv_offset,
    shared_kernel, shared_offset, step_bias, log_rate, skip_gain, gate_gain, weight_out, cotangent, segments, image_span,
):
    seqs, rows, model = tokens.shape
    length = rows * ranks
    pieces = length // STRETCH
    total = seqs * length
    channels = weight_gate.shape[1]
    heads = step_bias.shape[0]
    inner_width = channels * ranks
    width = weight_shared.shape[1]
    slab = width // ranks
    group = Ranks(ranks, slab)
    local = rows == STRETCH

    mixer = (token_of(jnp.arange(STRETCH))[:, None] == jnp.arange(STRETCH)[None, :]).astype(BF16)

    def reorder(values, dims=NN):
        blocks = values.reshape(-1, STRETCH, values.shape[-1])
        moved = [lax.dot_general(mixer, blocks[i], dims, preferred_element_type=BF16) for i in range(blocks.shape[0])]
        return jnp.concatenate(moved, axis=0).reshape(values.shape)

    def gather(values):
        if local:
            return group.gather(values.reshape(seqs * rows, model))
        every = lax.all_gather(values, "tensor", axis=1, tiled=True).reshape(seqs, pieces, STRETCH, model)
        return reorder(jnp.moveaxis(every, 1, 0)).reshape(total, model)

    def scatter(values):
        every = jnp.moveaxis(reorder(values, TN).reshape(pieces, seqs, STRETCH, model), 0, 1).reshape(seqs, length, model)
        return lax.psum_scatter(every, "tensor", scatter_dimension=1, tiled=True).astype(F32)

    def slabs(values):
        blocks = values.reshape(seqs, pieces, STRETCH, values.shape[-1])
        if not local:
            return jnp.moveaxis(blocks, 1, 0).reshape(values.shape)
        return jnp.concatenate(
            [rows_at(blocks, group.at["owner", slot], 1, 1)[:, 0] for slot in range(ranks)], axis=0
        ).reshape(values.shape)

    slots = jnp.arange(pieces, dtype=jnp.int32)
    if local:
        first = group.at.names["slot", 0]
        slots = group.at.row[0, first : first + pieces]
    own_low = reorder(tokens) if local else tokens
    cot_low = reorder(cotangent) if local else cotangent
    own = own_low.astype(F32)
    row_scale = lax.rsqrt(jnp.mean(own * own, axis=2, keepdims=True) + EPSILON)
    normed_low = (own * row_scale * pre_gain[None, None, :]).astype(BF16)
    tail = min(512, channels) - width - heads
    weight_ss = jnp.concatenate([weight_shared, weight_step, jnp.zeros((model, tail), BF16)], axis=1)
    pad_heads = lambda values: jnp.pad(values, (0, LANES - heads))[None, :]
    bias = pad_heads(step_bias)
    rate = pad_heads(-jnp.exp(log_rate))
    skip = jnp.repeat(skip_gain, HEAD)[None, :]
    heads_of = (jnp.arange(LANES)[:, None] == (jnp.arange(channels) // HEAD)[None, :]).astype(BF16)
    spread = jnp.concatenate([heads_of, heads_of], axis=0)
    seg_row = jnp.swapaxes(segments.astype(F32).reshape(seqs, pieces, 8, STRETCH // 8), 2, 3).reshape(1, total)
    offset_row, shared_offset_row = conv_offset[None, :], shared_offset[None, :]
    gain_row = gate_gain[None, :]

    slab = width // ranks
    weight_low = jnp.concatenate([weight_gate, weight_inner], axis=1)
    weight_side = jnp.concatenate(
        [
            rows_at(weight_shared, group.at["slab"], slab, 1),
            weight_step,
            jnp.zeros((model, LANES - slab - heads), BF16),
        ],
        axis=1,
    )
    blocked = local and ranks == 4
    if blocked:
        own_rows, cot_rows = normed_low.reshape(seqs * rows, model), cot_low.reshape(seqs * rows, model)
        far_rows = group.shift(own_rows, 1)
        far_cot = group.shift(after(cot_rows, own_rows), 1)
        weights = (weight_gate, weight_inner, weight_ss)
        first = fill_rows(own_rows, group.core(own_rows), weights, NN, None)
        first_cot = fill_rows(cot_rows, group.core(cot_rows), (weight_out,), NT, None, BF16)
        far_rows = after(far_rows, first[0], first_cot[0], weight_low, weight_side)
        pre, normed_in = fill_rows(far_rows, group.core(far_rows), weights, NN, first)
    else:
        normed_in, cot_full = gather(normed_low), gather(cot_low)
        weights = jnp.concatenate([weight_gate, weight_inner, weight_ss], axis=1)
        pre = lax.dot_general(normed_in, weights, NN, preferred_element_type=F32)
        grad = lax.dot_general(cot_full, weight_out, NT, preferred_element_type=BF16)
    y, gated, states, squares = scan_forward(
        slots, segments, image_span, pre, seg_row, spread, conv_kernel, offset_row, skip, shared_kernel, shared_offset_row,
        bias, rate,
    )
    if blocked:
        far_cot = after(far_cot, squares)
        grad, cot_full = fill_rows(far_cot, group.core(far_cot), (weight_out,), NT, first_cot, BF16)
    coupling = coupling_step(slots, seqs, gated, grad, gain_row)
    sums = total_over(jnp.concatenate([squares, coupling], axis=0), "tensor", ranks)
    scale_row = lax.rsqrt(sums[0:1] / inner_width + EPSILON)
    pull_row = scale_row * scale_row * scale_row / inner_width * sums[1:2]

    def backward(start, count, done, pull):
        return scan_backward(
            start, count, done, slots, segments, image_span, pre, grad, y, states, seg_row, scale_row, pull, spread,
            conv_kernel, offset_row, skip, gain_row, shared_kernel, shared_offset_row, bias, rate,
        )

    out_product = lambda left: lax.dot_general(left, cot_full, TN, preferred_element_type=BF16)
    made = {}
    ringed = local and dps == 8 and ranks == 4 and seqs > 1 and model == 2 * channels
    if ringed:
        ring = Ring(dps, ranks // 2, model, channels)
        join = lambda mine, arrived: (mine.astype(F32) + arrived.astype(F32)).astype(BF16)
        first = group.at.names["owner", 0]
        to_give, to_keep, norm_near, norm_far = split_norm_step(
            group.at.row[0, first : first + ranks], ring.at.row, seqs, gated, scale_row, gain_row, None,
            ring.at.names["give", 0], ring.at.names["keep", 0],
        )
        given = out_product(to_give)
        arrived = ring.exchange(given, 0)
        kept = out_product(after(to_keep, given))
        done = backward(0, seqs // 2, None, after(pull_row, kept))
        mixed_far = lax.dot_general(after(norm_far, done[0]), weight_out, NN, preferred_element_type=BF16)
        given, kept = ring.halve(after(kept, done[0], mixed_far), arrived, 1)
        arrived = ring.exchange(given, 1)
        done = backward(seqs // 2, seqs - seqs // 2, done, after(pull_row, given))
        given, kept = ring.halve(after(kept, done[0]), arrived, 2)
        low, shared_part, step_low, channel_grads, head_grads, shared_grads = done
        low_part = lax.dot_general(normed_in, after(low, given), TN, preferred_element_type=BF16)
        made["eighth"] = kept, ring.exchange(given, 2)
        low_part = after(low_part, made["eighth"][1])
    else:
        normed_out = norm_step(slots, seqs, gated, scale_row, gain_row)
        norm_near, norm_far = (normed_out[: total // 2], normed_out[total // 2 :]) if local else (normed_out, None)
        out_sum = lax.psum(out_product(normed_out), "dp")
        low, shared_part, step_low, channel_grads, head_grads, shared_grads = backward(0, seqs, None, pull_row)
        low_part = lax.dot_general(normed_in, low, TN, preferred_element_type=BF16)

    cut = total // 2 if local else 0
    half = ranks // 2
    by_rank = lambda values: values.reshape(-1, seqs, rows, model)

    def finished(hold=lambda values: values):
        if "finished" not in made:
            made["finished"] = join(hold(made["eighth"][0]), made["eighth"][1])
        return made["finished"]

    def finish(hold):
        return [finished(hold)] if ringed else []

    def columns_out(hold):
        columns = jnp.moveaxis(hold(shared_part).reshape(total, ranks, slab), 1, 0)
        columns = jnp.concatenate([rows_at(columns, group.at["owner", slot], 1) for slot in range(ranks)], axis=0)
        made["columns"] = columns[:half], group.core(columns[half:])
        return [columns]

    def columns_in(hold):
        shared_low = slabs(take_rows("columns", hold).astype(BF16))
        made["side"] = jnp.concatenate([shared_low, step_low[:, :heads], jnp.zeros((total, LANES - slab - heads), BF16)], axis=1)
        return [made["side"]]

    def pass_on(name):
        def run(hold):
            mine, other = made[name]
            sent = [(hold(mine)[i].astype(F32) + other[i].astype(F32)).astype(BF16) for i in range(1, half)]
            made[name] = mine[0], [other[0]] + [group.shift(values, -1 - i) for i, values in enumerate(sent)]
            return sent

        return run if local or name == "columns" else lambda hold: []

    def take_rows(name, hold):
        mine, others = made[name]
        mine = hold(mine).astype(F32)
        for values in others:
            mine = mine + values.astype(F32)
        return mine

    def input_rows_of(slot):
        part = slice(slot * seqs * rows, (slot + 1) * seqs * rows) if local else slice(0, total)

        def run(hold):
            side, low_rows = lax.optimization_barrier((hold(made["side"]), low))
            summed = lax.dot_general(side[part], weight_side, NT, preferred_element_type=F32)
            summed = (summed + lax.dot_general(low_rows[part], weight_low, NT, preferred_element_type=F32)).astype(BF16)
            if local:
                made["input", slot] = by_rank(summed)[0]
                if slot >= half:
                    made["input", slot] = group.core(made["input", slot])
            else:
                made["input"] = scatter(summed), []
            return [summed]

        return run

    def input_pair(hold):
        if local:
            made["input"] = [made["input", slot] for slot in range(half)], [made["input", slot] for slot in range(half, ranks)]
        return []

    def mix_of(far):
        def run(hold):
            if far and ringed:
                made["mixed far"] = group.core(by_rank(hold(mixed_far)))
                return []
            product = lax.dot_general(hold(norm_far if far else norm_near), weight_out, NN, preferred_element_type=BF16)
            if not local:
                made["mixed"] = scatter(product), []
            elif far:
                made["mixed far"] = group.core(by_rank(product))
            else:
                made["mixed"] = by_rank(product), made["mixed far"]
            return [product]

        return run

    def side_product(hold):
        product = lax.dot_general(hold(made["side"]), normed_in, TN, preferred_element_type=BF16)
        made["side_part"] = product[: slab + heads]
        return [made["side_part"]]

    def input_rows(hold):
        normed_grad = take_rows("input", hold)
        own = hold(own_low).astype(F32)
        weighted = normed_grad * pre_gain[None, None, :]
        projection = jnp.sum(weighted * own, axis=2, keepdims=True)
        own_grad = row_scale * weighted - row_scale * row_scale * row_scale / model * own * projection
        made["pre_gain"] = jnp.sum(normed_grad * own * row_scale, axis=(0, 1))
        made["tokens_grad"] = (cot_low.astype(F32) + own_grad).astype(BF16)
        return [made["tokens_grad"], made["pre_gain"]]

    def input_order(hold):
        if local:
            made["tokens_grad"] = reorder(hold(made["tokens_grad"]), TN)
        return [made["tokens_grad"]]

    def block_rows(hold):
        made["block_out"] = (hold(own_low).astype(F32) + take_rows("mixed", hold)).astype(BF16)
        return [made["block_out"]]

    def block_order(hold):
        if local:
            made["block_out"] = reorder(hold(made["block_out"]), TN)
        return [made["block_out"]]

    def small_start(hold):
        made["small"] = jnp.concatenate(
            [jnp.pad(hold(shared_grads), ((0, 0), (0, channels - width))), made["pre_gain"].reshape(-1, channels)], axis=0
        )
        return []

    def pack(hold):
        made["small"] = jnp.concatenate(
            [channel_grads, jnp.pad(head_grads, ((0, 0), (0, channels - LANES))), made["small"]], axis=0
        )
        return []

    def spread_sum(name, axis, size, bits, kind=F32):
        partners = [0]
        for bit in bits:
            partners += [partner ^ (1 << bit) for partner in partners]

        def send(hold):
            values = hold(made[name])
            made[name] = values, [lax.ppermute(values, axis, [(i, i ^ k) for i in range(size)]) for k in partners[1:]]
            return [values]

        def receive(hold):
            values, others = made[name]
            terms = [hold(values).astype(F32)] + [other.astype(F32) for other in others]
            while len(terms) > 1:
                terms = [terms[i] + terms[i + 1] for i in range(0, len(terms), 2)]
            made[name] = terms[0].astype(kind)
            return [made[name]]

        return send, receive

    def together(*parts):
        def run(hold):
            return [value for part in parts for value in part(hold)]

        return run

    bits_of = lambda size: list(range((size - 1).bit_length()))
    tensor_send, tensor_take = spread_sum("small", "tensor", ranks, bits_of(ranks))
    small_dp = [spread_sum("small", "dp", dps, bits) for bits in (bits_of(dps)[:1], bits_of(dps)[1:])]
    if ringed:
        side_dp = [spread_sum("side_part", "dp", dps, [bit], BF16) for bit in range(3)]
    else:

        def side_whole(hold):
            made["side_part"] = lax.psum(made["side_part"], "dp")
            return []

        side_dp = [(side_whole, lambda hold: [])] + [(lambda hold: [], lambda hold: [])] * 2
    nothing = lambda hold: []
    far = [input_rows_of(slot) for slot in (range(half, ranks) if local else range(1))]
    near = [input_rows_of(slot) for slot in (range(half) if local else range(0))]
    def gather_near(hold):
        slabs_of = hold(made["side_part"])[:slab]
        made["gathered"] = [slabs_of]
        for _ in range(1, half):
            made["gathered"].append(group.shift(made["gathered"][-1], 1))
        return []

    def gather_far(hold):
        made["gathered"] = made["gathered"] + [group.core(hold(values)) for values in made["gathered"]]
        return []

    def side_outputs(hold):
        gathered = jnp.stack([hold(values) for values in made["gathered"]])
        shared = jnp.concatenate([rows_at(gathered, group.at["slot", owner], 1)[0] for owner in range(ranks)], axis=0)
        made["shared"] = shared.T.astype(F32)
        made["step"] = hold(made["side_part"])[slab : slab + heads].T.astype(F32)
        return [made["shared"], made["step"]]

    def small_outputs(hold):
        packed = hold(made["small"])
        shared_sums = packed[16:24, :width]
        made["outputs"] = [
            packed[24:].reshape(model), packed[0:4], packed[4], shared_sums[0:4], shared_sums[4], packed[9, :heads],
            packed[8, :heads], jnp.sum(packed[5].reshape(heads, HEAD), axis=1), packed[6],
        ]
        return []

    fillers = [
        together(mix_of(True) if local else nothing, columns_out),
        together(pass_on("columns"), mix_of(False)),
        together(columns_in, side_product),
        together(side_dp[0][0], *far[:1]),
        together(side_dp[0][1], side_dp[1][0], *far[1:2]),
        *far[2:],
        together(*near[:1], finish),
        together(side_dp[1][1], side_dp[2][0], *near[1:2]),
        *near[2:],
        together(input_pair, pass_on("input")),
        together(pass_on("mixed"), side_dp[2][1]),
        input_rows,
        together(small_start, tensor_send, input_order, gather_near),
        together(tensor_take, pack, small_dp[0][0], block_rows),
        together(small_dp[0][1], small_dp[1][0], block_order, gather_far),
        together(small_dp[1][1], small_outputs, side_outputs),
    ]
    if ringed:
        sums = [blank((model, channels)), blank((model, channels)), blank((channels, model))]
        sums, _ = ring.all_reduce(low_part, sums, fillers, finished)
        grads = dict(zip(("gate", "inner", "out"), sums))
    else:
        low_sum = lax.psum(low_part, "dp").astype(F32)
        grads = {"gate": low_sum[:, :channels], "inner": low_sum[:, channels:], "out": out_sum.astype(F32)}
        for filler in fillers:
            filler(lambda values: values)
    gain, kernel_grad, offset_grad, shared_kernel_grad, shared_offset_grad, bias_grad, rate_grad, skip_grad, gate_gain_grad = made[
        "outputs"
    ]
    return (
        made["block_out"],
        made["tokens_grad"],
        gain,
        grads["gate"],
        grads["inner"],
        made["step"],
        made["shared"],
        kernel_grad,
        offset_grad,
        shared_kernel_grad,
        shared_offset_grad,
        bias_grad,
        rate_grad,
        skip_grad,
        gate_gain_grad,
        grads["out"],
    )


def solution(mesh):
    placed = (
        P("dp", "tensor", None),
        P(),
        P(None, "tensor"),
        P(None, "tensor"),
        P(None, "tensor"),
        P(),
        P(None, "tensor"),
        P("tensor"),
        P(),
        P(),
        P("tensor"),
        P("tensor"),
        P("tensor"),
        P("tensor"),
        P("tensor", None),
        P("dp", "tensor", None),
        P("dp", None),
        P("dp", None),
    )
    return jax.shard_map(
        partial(body, mesh.shape["tensor"], mesh.shape["dp"]),
        mesh=mesh,
        in_specs=placed,
        out_specs=(
            P("dp", "tensor", None),
            P("dp", "tensor", None),
            P(),
            P(None, "tensor"),
            P(None, "tensor"),
            P(None, "tensor"),
            P(),
            P(None, "tensor"),
            P("tensor"),
            P(),
            P(),
            P("tensor"),
            P("tensor"),
            P("tensor"),
            P("tensor"),
            P("tensor", None),
        ),
        check_vma=False,
    )
```

```python
from functools import partial

import jax
import jax.numpy as jnp
from jax import lax
from jax.experimental import pallas as pl
from jax.experimental.pallas import tpu as pltpu
from jax.sharding import PartitionSpec as P

STRETCH = 256
HEAD = 64
LANES = 128

EPSILON = 1e-05
LOG2E = 1.4426950408889634
BF16 = jnp.bfloat16
F32 = jnp.float32
NN = (((1,), (0,)), ((), ()))
NT = (((1,), (1,)), ((), ()))
TN = (((0,), (0,)), ((), ()))


def mm(left, right, dims=NN):
    return lax.dot_general(left.astype(BF16), right.astype(BF16), dims, preferred_element_type=F32)


def two_parts(values):
    high = values.astype(BF16)
    return high, (values - high.astype(F32)).astype(BF16)


def iota(shape, axis):
    return lax.broadcasted_iota(jnp.int32, shape, axis)


def expand(values, spread):
    high, low = two_parts(values)
    return mm(jnp.concatenate([high, low], axis=1), spread)


def head_sum(values, spread):
    high, low = two_parts(values)
    half = spread[:LANES]
    return mm(high, half, NT) + mm(low, half, NT)


def column_of(row, eye):
    return jnp.sum(jnp.where(eye, row, 0.0), axis=1, keepdims=True)


def token_of(rows):
    return (rows & 7) * (STRETCH // 8) + (rows >> 3)


def lagged(current, before):
    last = current[STRETCH - 24 :]
    top = iota(last.shape, 0) & 7
    first = jnp.where(top == 0, pltpu.roll(before, 17, 0), pltpu.roll(last, 1, 0))
    joined = jnp.concatenate([first, current], axis=0)
    return [joined[8 * tap : 8 * tap + STRETCH] for tap in range(4)]


def leading(current, after):
    first = current[:24]
    top = iota(first.shape, 0) & 7
    last = jnp.where(top == 7, pltpu.roll(after, 7, 0), pltpu.roll(first, 23, 0))
    joined = jnp.concatenate([current, last], axis=0)
    return [joined[24 - 8 * tap : 24 - 8 * tap + STRETCH] for tap in range(4)]


def taps(values, kernel):
    total = kernel[0:1] * values[0]
    for tap in range(1, 4):
        total = total + kernel[tap : tap + 1] * values[tap]
    return total


def column_sum(values):
    return jnp.sum(values, axis=0, keepdims=True)


def piece_context(seg_sm, span_sm, seg_row, step_pre, bias, rate, seq, piece):
    rows = STRETCH
    i0, i1 = token_of(iota((rows, rows), 0)), token_of(iota((rows, rows), 1))
    order = i0 - i1
    eye = order == 0
    seg_r = seg_row[...]
    seg_c = column_of(seg_r, eye)
    first = span_sm[seq, 0]
    image = jnp.logical_and(piece >= first, piece < first + span_sm[seq, 1])
    reach_all = jnp.where(image, 2 * rows, 0)
    same = seg_c == seg_r
    start = piece * rows
    last_doc = seg_sm[seq, start + rows - 1].astype(F32)
    before_doc = seg_sm[seq, jnp.maximum(start - 1, 0)].astype(F32)
    pre = step_pre + bias
    tail = jnp.exp(-jnp.abs(pre))
    step = jnp.maximum(pre, 0.0) + jnp.log1p(tail)
    log_step = step * rate
    high, low = two_parts(log_step)
    lowest = (log_step - high.astype(F32) - low.astype(F32)).astype(BF16)
    ahead = (order >= 0).astype(F32)
    cum = mm(ahead, high) + mm(ahead, low) + mm(ahead, lowest)
    cum = cum * LOG2E
    end = cum[rows - 1 : rows]
    to_end = jnp.where(seg_c == last_doc, jnp.exp2(end - cum), 0.0)
    reach = jnp.where(seg_c == before_doc, jnp.exp2(cum), 0.0)
    keep = jnp.where(last_doc == before_doc, jnp.exp2(end), 0.0)
    sign = jnp.where(order > 0, 1.0, jnp.where(order < 0, -1.0, 0.0))
    return eye, order, reach_all, same, sign, pre, step, log_step, cum, to_end, reach, keep


def forward_kernel(
    channels, slots, seg_sm, span_sm, pre, seg_row, spread, kernel, offset, skip, shared_kernel, shared_offset, bias, rate,
    y_out, gated_out, state_out, square_out, before, shared_before, state,
):
    seq, piece = pl.program_id(0), pl.program_id(1)
    width = shared_kernel.shape[1]
    half = width // 2

    @pl.when(piece == 0)
    def _():
        before[...] = jnp.zeros_like(before)
        shared_before[...] = jnp.zeros_like(shared_before)
        state[...] = jnp.zeros_like(state)

    shared_pre = pre[:, 2 * channels : 2 * channels + width]
    step_columns = pre[:, 2 * channels + width : 2 * channels + width + LANES]
    _, order, reach_all, same, sign, _, step, _, cum, to_end, reach, keep = piece_context(
        seg_sm, span_sm, seg_row, step_columns, bias[...], rate[...], seq, piece
    )
    allowed = jnp.logical_and(same, order + reach_all >= 0)
    conv = taps(lagged(shared_pre, shared_before[...]), shared_kernel) + shared_offset[...]
    shared_before[...] = shared_pre[STRETCH - 24 :]
    act = conv * jax.nn.sigmoid(conv)
    b, c = act[:, :half].astype(BF16), act[:, half:].astype(BF16)
    scores = jnp.where(allowed, mm(c, b, NT), 0.0)
    cum_rows = cum.T
    b_cols = b.T
    lane = iota((STRETCH, LANES), 1)
    spread_all = spread[...]

    gate = pre[:, :channels]
    inner = pre[:, channels : 2 * channels]
    v = taps(lagged(inner, before[...]), kernel) + offset[...]
    before[...] = inner[STRETCH - 24 :]
    x = v * jax.nn.sigmoid(v)
    u = x * expand(step, spread_all)
    entering = state[...]
    state_out[0, 0] = entering.astype(BF16)
    carried = mm(c, entering) * expand(reach, spread_all)
    keep_row = expand(jnp.broadcast_to(keep, (8, LANES)), spread_all)[0:1]
    state[...] = keep_row * entering + mm(b_cols, u * expand(to_end, spread_all))
    u_low = u.astype(BF16)
    mixed = []
    for pair in range(channels // LANES):
        pair_u = u_low[:, pair * LANES : (pair + 1) * LANES]
        halves = []
        for head in (2 * pair, 2 * pair + 1):
            gap = cum[:, head : head + 1] - cum_rows[head : head + 1]
            halves.append(mm(scores * jnp.exp2(gap * sign), pair_u))
        mixed.append(jnp.where(lane < HEAD, halves[0], halves[1]))
    y = jnp.concatenate(mixed, axis=1) + carried + skip[...] * x
    y_out[...] = y
    gated = y * (gate * jax.nn.sigmoid(gate))
    gated_out[...] = gated.astype(BF16)
    square_out[...] = mm(jnp.ones((8, channels), BF16), gated * gated, NT)[0:1]


def coupling_kernel(slots, gated, grad, gain, coupling_out):
    product = grad[...].astype(F32) * (gated[...].astype(F32) * gain[...])
    coupling_out[...] = mm(jnp.ones((8, gain.shape[1]), BF16), product, NT)[0:1]


def norm_kernel(slots, gated, scale_row, gain, low_out):
    eye = iota((STRETCH, STRETCH), 0) == iota((STRETCH, STRETCH), 1)
    scale = column_of(scale_row[...], eye)
    low_out[...] = (gated[...].astype(F32) * gain[...] * scale).astype(BF16)


def backward_kernel(
    channels, start, slots, seg_sm, span_sm, pre, halo, grad_in, y_in, state_in, seg_row, scale_row, pull_row, spread, kernel,
    offset, skip, gain, shared_kernel, shared_offset, bias, rate,
    *rest,
):
    earlier = rest[3:6] if start else None
    low_out, shared_out, step_out, channel_grads, head_grads, shared_grads, after, lam, shared_after = rest[-9:]
    seq = pl.program_id(0) + start
    backward_piece = pl.program_id(1)
    piece = pl.num_programs(1) - 1 - backward_piece
    width = shared_kernel.shape[1]
    half = width // 2
    rows = STRETCH

    @pl.when(backward_piece == 0)
    def _():
        after[...] = jnp.zeros_like(after)
        lam[...] = jnp.zeros_like(lam)
        shared_after[...] = jnp.zeros_like(shared_after)

    @pl.when(jnp.logical_and(backward_piece == 0, seq == start))
    def _():
        for i, total in enumerate((channel_grads, head_grads, shared_grads)):
            total[...] = earlier[i][...] if start else jnp.zeros_like(total)

    inside = jnp.where(piece > 0, 1.0, 0.0)
    shared_pre = pre[:, 2 * channels : 2 * channels + width]
    step_columns = pre[:, 2 * channels + width : 2 * channels + width + LANES]
    eye, order, reach_all, same, sign, step_pre, step, log_step, cum, to_end, reach, keep = piece_context(
        seg_sm, span_sm, seg_row, step_columns, bias[...], rate[...], seq, piece
    )
    allowed = jnp.logical_and(same, order + reach_all >= 0)
    allowed_t = jnp.logical_and(same, reach_all - order >= 0)
    conv = taps(lagged(shared_pre, halo[8:32, 2 * channels : 2 * channels + width] * inside), shared_kernel) + shared_offset[...]
    shared_sig = jax.nn.sigmoid(conv)
    act = conv * shared_sig
    b, c = act[:, :half].astype(BF16), act[:, half:].astype(BF16)
    scores = jnp.where(allowed, mm(c, b, NT), 0.0)
    scores_t = jnp.where(allowed_t, mm(b, c, NT), 0.0)
    signed = scores * sign
    cum_rows = cum.T
    c_cols = c.T
    lane = iota((rows, LANES), 1)
    head_row = iota((LANES, rows), 0)

    scale = column_of(scale_row[...], eye)
    pull = column_of(pull_row[...], eye)
    gate = pre[:, :channels]
    y = y_in[...]
    gate_sig = jax.nn.sigmoid(gate)
    silu = gate * gate_sig
    gated = y * silu
    scaled_grad = scale * grad_in[...].astype(F32)
    d_gated = gain[...] * scaled_grad - pull * gated
    low_out[:, :channels] = (d_gated * y * (gate_sig + silu * (1.0 - gate_sig))).astype(BF16)
    channel_grads[6:7] += column_sum(scaled_grad * gated)
    dy = d_gated * silu

    inner = pre[:, channels : 2 * channels]
    v = taps(lagged(inner, halo[8:32, channels : 2 * channels] * inside), kernel) + offset[...]
    sig = jax.nn.sigmoid(v)
    x = v * sig
    spread_all = spread[...]
    step_x = expand(step, spread_all)
    to_end_x = expand(to_end, spread_all)
    keep_row = expand(jnp.broadcast_to(keep, (8, LANES)), spread_all)[0:1]
    u = x * step_x
    u_low = u.astype(BF16)
    dy_low = dy.astype(BF16)
    entering = state_in[0, 0]
    lam_now = lam[...]
    lam_low = lam_now.astype(BF16)
    reached_full = dy * expand(reach, spread_all)
    reached = reached_full.astype(BF16)
    pulled = mm(b, lam_low) * to_end_x
    d_c = mm(reached, entering, NT)
    d_b = mm(u * to_end_x, lam_low, NT)
    from_start = reached_full * mm(c, entering)
    from_end = u * pulled
    edge = column_sum(from_end) + keep_row * column_sum(lam_now * entering.astype(F32))
    lam[...] = keep_row * lam_now + mm(c_cols, reached)

    d_scores = jnp.zeros((rows, rows), F32)
    row_sums = jnp.zeros((rows, LANES), F32)
    col_sums = jnp.zeros((LANES, rows), F32)
    du_parts = []
    for pair in range(channels // LANES):
        cols = slice(pair * LANES, (pair + 1) * LANES)
        pair_u, pair_dy = u_low[:, cols], dy_low[:, cols]
        halves = []
        for one in range(2):
            head = 2 * pair + one
            own = lane < HEAD if one == 0 else lane >= HEAD
            gap = cum[:, head : head + 1] - cum_rows[head : head + 1]
            decay = jnp.exp2(gap * sign)
            d_mix = mm(jnp.where(own, pair_dy, jnp.zeros_like(pair_dy)), pair_u, NT) * decay
            d_scores = d_scores + d_mix
            turned = d_mix * signed
            row_sums = row_sums + jnp.where(lane == head, jnp.sum(turned, axis=1, keepdims=True), 0.0)
            col_sums = col_sums + jnp.where(head_row == head, column_sum(turned), 0.0)
            halves.append(mm(scores_t * decay, pair_dy))
        du_parts.append(jnp.where(lane < HEAD, halves[0], halves[1]))
    du = jnp.concatenate(du_parts, axis=1) + pulled
    d_scores = jnp.where(allowed, d_scores, 0.0).astype(BF16)
    d_c = d_c + mm(d_scores, b)
    d_b = d_b + mm(d_scores, c, TN)

    d_cum = row_sums - col_sums.T + head_sum(from_start - from_end, spread_all)
    high, low = two_parts(d_cum)
    behind = (order <= 0).astype(F32)
    d_log = mm(behind, high) + mm(behind, low) + head_sum(jnp.broadcast_to(edge, (8, channels)), spread_all)[0:1]
    d_step = (d_log * rate[...] + head_sum(x * du, spread_all)) * jax.nn.sigmoid(step_pre)
    d_step = jnp.where(lane < channels // HEAD, d_step, 0.0)
    step_out[...] = d_step.astype(BF16)
    head_grads[0:1] += column_sum(d_log * log_step)
    head_grads[1:2] += column_sum(d_step)

    dx = step_x * du + skip[...] * dy
    dv = dx * (sig + x * (1.0 - sig))
    ahead = leading(dv, after[...])
    after[...] = dv[:24]
    low_out[:, channels:] = taps(ahead, kernel).astype(BF16)
    for tap in range(4):
        channel_grads[tap : tap + 1] += column_sum(ahead[tap] * inner)
    channel_grads[4:5] += column_sum(dv)
    channel_grads[5:6] += column_sum(dy * x)

    d_conv = jnp.concatenate([d_b, d_c], axis=1) * (shared_sig + act * (1.0 - shared_sig))
    ahead = leading(d_conv, shared_after[...])
    shared_after[...] = d_conv[:24]
    shared_out[...] = taps(ahead, shared_kernel).astype(BF16)
    for tap in range(4):
        shared_grads[tap : tap + 1] += column_sum(ahead[tap] * shared_pre)
    shared_grads[4:5] += column_sum(d_conv)


def whole(shape):
    return pl.BlockSpec(shape, lambda *_: (0,) * len(shape))


def limits(mebibytes):
    return pltpu.CompilerParams(vmem_limit_bytes=mebibytes << 20)


def cost(flops, moved):
    return pl.CostEstimate(flops=int(flops), bytes_accessed=int(moved), transcendentals=0)


def fill_kernel(dims, spans, first, own, other, *rest):
    weights = rest[: len(spans)]
    product, joined, held, sems = rest[-4:]
    rows = own.shape[0]
    tile = product.shape[1]
    index, step = pl.program_id(0), pl.program_id(1)
    copies = [
        pltpu.make_async_copy(block, joined.at[pl.ds((2 * i + first) * rows, rows)], sems.at[i])
        for i, block in enumerate((own, other))
    ]
    for i, block in enumerate((own, other)):

        @pl.when(jnp.logical_and(index == 0, step == i))
        def _():
            copies[i].start()
            held[i] = block[...]

    for (start, count), weight in zip(spans, weights):

        @pl.when(jnp.logical_and(index >= start, index < start + count))
        def _():
            product[...] = lax.dot_general(held[step], weight[...], dims, preferred_element_type=F32).astype(product.dtype)

    @pl.when(jnp.logical_and(index == pl.num_programs(0) - 1, step == 1))
    def _():
        for copy in copies:
            copy.wait()


def fill_rows(own, other, weights, dims, filled, kind=F32):
    rows, depth = own.shape
    side = 1 if dims == NN else 0
    widths = [values.shape[side] for values in weights]
    tile = min(512, *widths)
    spans, first = [], 0
    for width in widths:
        spans.append((first, width // tile))
        first += width // tile
    second = filled is not None
    anywhere = pl.BlockSpec(memory_space=pl.ANY)

    def weight_spec(span):
        column = lambda j: jnp.clip(j - span[0], 0, span[1] - 1)
        if dims == NN:
            return pl.BlockSpec((depth, tile), lambda j, i: (0, column(j)))
        return pl.BlockSpec((tile, depth), lambda j, i: (column(j), 0))

    count = len(weights)
    block = lambda i: 2 * i + (1 if second else 0)
    return pl.pallas_call(
        partial(fill_kernel, dims, spans, 1 if second else 0),
        name="fill_rows",
        grid=(first, 2),
        in_specs=[whole(own.shape), whole(other.shape)]
        + [weight_spec(span) for span in spans]
        + ([anywhere] * 2 if second else []),
        out_specs=[
            pl.BlockSpec((rows, tile), lambda j, i: (block(i), j)),
            anywhere,
        ],
        out_shape=[jax.ShapeDtypeStruct((4 * rows, sum(widths)), kind), jax.ShapeDtypeStruct((4 * rows, depth), BF16)],
        scratch_shapes=[pltpu.VMEM((2, rows, depth), BF16), pltpu.SemaphoreType.DMA((2,))],
        input_output_aliases={2 + count: 0, 3 + count: 1} if second else {},
        compiler_params=pltpu.CompilerParams(dimension_semantics=("arbitrary", "arbitrary")),
        cost_estimate=cost(4 * rows * depth * sum(widths), 4 * rows * (depth + sum(widths))),
    )(own, other, *weights, *(filled if second else ()))


def blank(shape):
    return pl.pallas_call(
        lambda out: None, name="blank", out_specs=pl.BlockSpec(memory_space=pl.ANY), out_shape=jax.ShapeDtypeStruct(shape, F32)
    )()


def scan_forward(slots, segments, spans, pre, seg_row, spread, kernel, offset, skip, shared_kernel, shared_offset, bias, rate):
    seqs, length = segments.shape
    pieces = length // STRETCH
    channels = kernel.shape[1]
    width = shared_kernel.shape[1]
    at = lambda s, p, where, *_: (where[p] * seqs + s, 0)
    row_at = lambda s, p, *_: (0, s * pieces + p)
    total = seqs * length
    return pl.pallas_call(
        partial(forward_kernel, channels),
        name="scan_forward",
        grid_spec=pltpu.PrefetchScalarGridSpec(
            num_scalar_prefetch=3,
            grid=(seqs, pieces),
            in_specs=[
                pl.BlockSpec((STRETCH, pre.shape[1]), at),
                pl.BlockSpec((1, STRETCH), row_at),
                whole(spread.shape), whole(kernel.shape), whole(offset.shape), whole(skip.shape),
                whole(shared_kernel.shape), whole(shared_offset.shape), whole(bias.shape), whole(rate.shape),
            ],
            out_specs=[
                pl.BlockSpec((STRETCH, channels), at),
                pl.BlockSpec((STRETCH, channels), at),
                pl.BlockSpec((1, 1, width // 2, channels), lambda s, p, *_: (s, p, 0, 0)),
                pl.BlockSpec((1, STRETCH), row_at),
            ],
            scratch_shapes=[
                pltpu.VMEM((24, channels), F32), pltpu.VMEM((24, width), F32), pltpu.VMEM((width // 2, channels), F32),
            ],
        ),
        out_shape=[
            jax.ShapeDtypeStruct((total, channels), F32),
            jax.ShapeDtypeStruct((total, channels), BF16),
            jax.ShapeDtypeStruct((seqs, pieces, width // 2, channels), BF16),
            jax.ShapeDtypeStruct((1, total), F32),
        ],
        compiler_params=pltpu.CompilerParams(dimension_semantics=("arbitrary", "arbitrary")),
        cost_estimate=cost(20e9, 40e6),
    )(slots, segments, spans, pre, seg_row, spread, kernel, offset, skip, shared_kernel, shared_offset, bias, rate)


def coupling_step(slots, seqs, gated, grad, gain):
    total, channels = gated.shape
    pieces = total // STRETCH // seqs
    at = lambda s, p, where: (where[p] * seqs + s, 0)
    return pl.pallas_call(
        coupling_kernel,
        name="coupling",
        grid_spec=pltpu.PrefetchScalarGridSpec(
            num_scalar_prefetch=1,
            grid=(seqs, pieces),
            in_specs=[pl.BlockSpec((STRETCH, channels), at), pl.BlockSpec((STRETCH, channels), at), whole(gain.shape)],
            out_specs=pl.BlockSpec((1, STRETCH), lambda s, p, *_: (0, s * pieces + p)),
        ),
        out_shape=jax.ShapeDtypeStruct((1, total), F32),
        compiler_params=limits(8),
        cost_estimate=cost(2e9, 12e6),
    )(slots, gated, grad, gain)


def split_norm_step(owners, numbers, seqs, gated, scale_row, gain, row, give, keep):
    total, channels = gated.shape
    count = total // STRETCH
    pieces = count // seqs

    def kernel(owners, numbers, gated, scale_row, gain, given, kept, near, far, held):
        eye = iota((STRETCH, STRETCH), 0) == iota((STRETCH, STRETCH), 1)
        scale = column_of(scale_row[...], eye)
        low = (gated[...].astype(F32) * gain[...] * scale).astype(BF16)
        held[...] = low
        for out, name in ((given, give), (kept, keep)):
            start = pl.multiple_of(numbers[0, name] * (channels // 2), LANES)
            out[...] = held[:, pl.ds(start, channels // 2)]

        @pl.when(pl.program_id(0) < count // 2)
        def _():
            near[...] = low

        @pl.when(pl.program_id(0) >= count // 2)
        def _():
            far[...] = low

    at = lambda i, *_: (i, 0)
    half_block = pl.BlockSpec((STRETCH, channels // 2), at)
    return pl.pallas_call(
        kernel,
        name="norm_rows",
        grid_spec=pltpu.PrefetchScalarGridSpec(
            num_scalar_prefetch=2,
            grid=(count,),
            in_specs=[
                pl.BlockSpec((STRETCH, channels), at),
                pl.BlockSpec((1, STRETCH), lambda i, own, *_: (0, i % seqs * pieces + own[i // seqs])),
                whole(gain.shape),
            ],
            out_specs=[
                half_block,
                half_block,
                pl.BlockSpec((STRETCH, channels), lambda i, *_: (jnp.minimum(i, count // 2 - 1), 0)),
                pl.BlockSpec((STRETCH, channels), lambda i, *_: (jnp.maximum(i - count // 2, 0), 0)),
            ],
            scratch_shapes=[pltpu.VMEM((STRETCH, channels), BF16)],
        ),
        out_shape=[jax.ShapeDtypeStruct((total, channels // 2), BF16)] * 2
        + [jax.ShapeDtypeStruct((total // 2, channels), BF16)] * 2,
        compiler_params=limits(12),
        cost_estimate=cost(1e9, 12e6),
    )(owners, numbers, gated, scale_row, gain)


def norm_step(slots, seqs, gated, scale_row, gain):
    total, channels = gated.shape
    pieces = total // STRETCH // seqs
    at = lambda s, p, where: (where[p] * seqs + s, 0)
    return pl.pallas_call(
        norm_kernel,
        name="norm_rows",
        grid_spec=pltpu.PrefetchScalarGridSpec(
            num_scalar_prefetch=1,
            grid=(seqs, pieces),
            in_specs=[
                pl.BlockSpec((STRETCH, channels), at),
                pl.BlockSpec((1, STRETCH), lambda s, p, *_: (0, s * pieces + p)),
                whole(gain.shape),
            ],
            out_specs=pl.BlockSpec((STRETCH, channels), at),
        ),
        out_shape=jax.ShapeDtypeStruct((total, channels), BF16),
        compiler_params=limits(8),
        cost_estimate=cost(1e9, 8e6),
    )(slots, gated, scale_row, gain)


def scan_backward(
    start, count, done, slots, segments, spans, pre, grad, y, states, seg_row, scale_row, pull_row, spread, kernel, offset, skip, gain,
    shared_kernel, shared_offset, bias, rate,
):
    seqs, length = segments.shape
    pieces = length // STRETCH
    channels = kernel.shape[1]
    width = shared_kernel.shape[1]
    total = seqs * length
    piece_at = lambda p: pieces - 1 - p
    at = lambda s, p, where, *_: (where[piece_at(p)] * seqs + s + start, 0)
    row_at = lambda s, p, *_: (0, (s + start) * pieces + piece_at(p))
    halo_at = lambda s, p, where, *_: (
        (where[jnp.maximum(piece_at(p) - 1, 0)] * seqs + s + start) * (STRETCH // 32) + STRETCH // 32 - 1, 0
    )
    plain_at = lambda s, p, *_: ((s + start) * pieces + piece_at(p), 0)
    return pl.pallas_call(
        partial(backward_kernel, channels, start),
        name="scan_backward",
        grid_spec=pltpu.PrefetchScalarGridSpec(
            num_scalar_prefetch=3,
            grid=(count, pieces),
            in_specs=[
                pl.BlockSpec((STRETCH, pre.shape[1]), at),
                pl.BlockSpec((32, pre.shape[1]), halo_at),
                pl.BlockSpec((STRETCH, channels), at),
                pl.BlockSpec((STRETCH, channels), at),
                pl.BlockSpec((1, 1, width // 2, channels), lambda s, p, *_: (s + start, piece_at(p), 0, 0)),
                pl.BlockSpec((1, STRETCH), row_at),
                pl.BlockSpec((1, STRETCH), row_at),
                pl.BlockSpec((1, STRETCH), row_at),
                whole(spread.shape), whole(kernel.shape), whole(offset.shape), whole(skip.shape), whole(gain.shape),
                whole(shared_kernel.shape), whole(shared_offset.shape), whole(bias.shape), whole(rate.shape),
            ]
            + ([pl.BlockSpec(memory_space=pl.ANY)] * 3 + [whole(values.shape) for values in done[3:]] if start else []),
            out_specs=[
                pl.BlockSpec((STRETCH, 2 * channels), at),
                pl.BlockSpec((STRETCH, width), plain_at),
                pl.BlockSpec((STRETCH, LANES), at),
                whole((8, channels)),
                whole((8, LANES)),
                whole((8, width)),
            ],
            scratch_shapes=[
                pltpu.VMEM((24, channels), F32), pltpu.VMEM((width // 2, channels), F32), pltpu.VMEM((24, width), F32),
            ],
        ),
        out_shape=[
            jax.ShapeDtypeStruct((total, 2 * channels), BF16),
            jax.ShapeDtypeStruct((total, width), BF16),
            jax.ShapeDtypeStruct((total, LANES), BF16),
            jax.ShapeDtypeStruct((8, channels), F32),
            jax.ShapeDtypeStruct((8, LANES), F32),
            jax.ShapeDtypeStruct((8, width), F32),
        ],
        input_output_aliases={20: 0, 21: 1, 22: 2} if start else {},
        compiler_params=pltpu.CompilerParams(dimension_semantics=("arbitrary", "arbitrary")),
        cost_estimate=cost(22e9 * count, 30e6 * count),
    )(
        slots, segments, spans, pre, pre, grad, y, states, seg_row, scale_row, pull_row, spread, kernel, offset, skip, gain,
        shared_kernel, shared_offset, bias, rate, *(done if start else ()),
    )


def ring_order(devices, across):
    depth = devices // across
    if devices % across or across < 2 or depth < 2 or depth % 2 and across % 2:
        return list(range(devices))
    if across == 2:
        return [z * 2 for z in range(depth)] + [z * 2 + 1 for z in reversed(range(depth))]
    walk = [z * across for z in range(depth)]
    for turn, z in enumerate(reversed(range(depth))):
        xs = range(1, across)
        walk += [z * across + x for x in (xs if turn % 2 == 0 else reversed(xs))]
    return walk


class Numbers:
    def __init__(self, axis, size, columns):
        self.names = {name: i for i, name in enumerate(columns)}
        table = jnp.asarray([[values(i) for values in columns.values()] for i in range(size)], jnp.int32)
        row = lax.dynamic_slice(table, (lax.axis_index(axis), 0), (1, len(columns)), allow_negative_indices=False)
        self.row = lax.optimization_barrier(row)

    def __getitem__(self, name):
        return self.row[0, self.names[name]]


def rows_at(values, start, count, axis=0):
    starts = [start if i == axis else 0 for i in range(values.ndim)]
    sizes = [count if i == axis else size for i, size in enumerate(values.shape)]
    return lax.dynamic_slice(values, starts, sizes, allow_negative_indices=False)


def put_at(values, update, row, column=0):
    return lax.dynamic_update_slice(values, update, (row, column), allow_negative_indices=False)


WAYS = (1, -1)


class Ring:
    def __init__(self, devices, across, height, halved):
        self.size = n = devices
        self.order = order = ring_order(devices, across)
        self.block = block = height // (2 * n)
        self.eighth = eighth = halved // 8
        onward = [(order[i], order[(i + 1) % n]) for i in range(n)]
        self.pairs = {1: onward, -1: [(b, a) for a, b in onward]}
        columns = {}
        for step in range(n):
            for kind, lead in (("add", 0), ("store", 1)):
                for way in WAYS:
                    columns[kind, step, way] = lambda i, w=way, s=step, d=lead: (0 if w > 0 else n) + (
                        order.index(i) + w * (d - s)
                    ) % n
            for way in WAYS:

                def eighth_of(i, w=way, s=step):
                    origin = order[(order.index(i) - w * s) % n]
                    return 2 * ((origin & 1) * 4 + (origin >> 1 & 1) * 2 + (origin >> 2 & 1)) + (0 if w > 0 else 1)

                columns["side", step, way] = eighth_of
        for bit in range(3):
            columns["give", bit] = lambda i, k=bit: 1 - (i >> k & 1)
            columns["keep", bit] = lambda i, k=bit: i >> k & 1
        self.at = Numbers("dp", n, columns)

    def exchange(self, values, bit):
        return lax.ppermute(values, "dp", [(i, i ^ (1 << bit)) for i in range(self.size)])

    def halve(self, kept, arrived, bit):
        rows, columns = kept.shape
        first = self.at.names["give", bit]

        def kernel(row, mine, other, given, held):
            total = (mine[...].astype(F32) + other[...].astype(F32)).astype(BF16)

            @pl.when(pl.program_id(0) == 0)
            def _():
                given[...] = total

            @pl.when(pl.program_id(0) == 1)
            def _():
                held[...] = total

        half = (rows // 2, columns)
        at = pl.BlockSpec(half, lambda i, row: (row[0, first + i], 0))
        return pl.pallas_call(
            kernel,
            name="halve",
            grid_spec=pltpu.PrefetchScalarGridSpec(
                num_scalar_prefetch=1, grid=(2,), in_specs=[at, at], out_specs=[whole(half), whole(half)]
            ),
            out_shape=[jax.ShapeDtypeStruct(half, BF16)] * 2,
            compiler_params=limits(12),
            cost_estimate=cost(1e6, 4e6),
        )(self.at.row, kept, arrived)

    def add(self, parts, arrived, step, extra=None):
        block, columns = self.block, parts.shape[1]
        shape = (block, columns)
        half = 0 if extra is None else extra.shape[0] // 2
        full = (block + half, columns)
        first = self.at.names["add", step, 1]

        def kernel(row, one, two, *rest):
            out_one, out_two = rest[-2:]
            sources = [one[...].astype(F32), two[...].astype(F32)]
            for i in range(len(arrived)):
                sources[i] = sources[i] + rest[i][...].astype(F32)
            out_one[:block] = sources[0].astype(BF16)
            out_two[:block] = sources[1].astype(BF16)
            if half:
                out_one[block:] = rest[2][:half]
                out_two[block:] = rest[2][half:]

        return pl.pallas_call(
            kernel,
            name="ring_add",
            grid_spec=pltpu.PrefetchScalarGridSpec(
                num_scalar_prefetch=1,
                grid=(1,),
                in_specs=[
                    pl.BlockSpec(shape, lambda i, row: (row[0, first], 0)),
                    pl.BlockSpec(shape, lambda i, row: (row[0, first + 1], 0)),
                ]
                + [whole(shape)] * len(arrived)
                + ([whole(extra.shape)] if half else []),
                out_specs=[whole(full), whole(full)],
            ),
            out_shape=[jax.ShapeDtypeStruct(full, BF16)] * 2,
            compiler_params=limits(10),
            cost_estimate=cost(1e6, 4e6),
        )(self.at.row, parts, parts, *arrived, *([extra] if half else []))

    def store(self, sums, held, step):
        block, height = self.block, self.eighth // 2
        channels, model = sums[0].shape[1], sums[2].shape[1]
        first, side = self.at.names["store", step, 1], self.at.names["side", step, 1]

        def kernel(row, one, two, *rest):
            gate, inner, out = rest[3:]
            for way, source in enumerate((one, two)):

                @pl.when(pl.program_id(0) == way)
                def _():
                    gate[...] = source[:block, :channels].astype(F32)
                    inner[...] = source[:block, channels:].astype(F32)
                    out[...] = source[block:, :].astype(F32)

        low_spec = pl.BlockSpec((block, channels), lambda i, row: (row[0, first + i], 0))
        return pl.pallas_call(
            kernel,
            name="ring_store",
            grid_spec=pltpu.PrefetchScalarGridSpec(
                num_scalar_prefetch=1,
                grid=(2,),
                in_specs=[whole(held[0].shape), whole(held[1].shape)] + [pl.BlockSpec(memory_space=pl.ANY)] * 3,
                out_specs=[low_spec, low_spec, pl.BlockSpec((height, model), lambda i, row: (row[0, side + i], 0))],
            ),
            out_shape=[jax.ShapeDtypeStruct(values.shape, F32) for values in sums],
            input_output_aliases={3: 0, 4: 1, 5: 2},
            compiler_params=limits(12),
            cost_estimate=cost(1e6, 6e6),
        )(self.at.row, *held, *sums)

    def all_reduce(self, parts, sums, fillers, finished):
        n, fillers = self.size, list(fillers)

        def send(held, earlier=()):
            arrived = [lax.ppermute(values, "dp", self.pairs[way]) for way, values in zip(WAYS, held)]
            made = fillers.pop(0)(lambda values: after(values, *held)) if fillers else []
            return lax.optimization_barrier((*arrived, *made, *earlier))[:2]

        held = self.add(parts, (), 0)
        for step in range(1, n):
            held = self.add(parts, send(held), step, finished() if step == n - 1 else None)
        for step in range(n):
            if step:
                held = send(held, sums[:1])
            sums = self.store(sums, held, step)
        for filler in fillers:
            filler(lambda values: values)
        return sums, held


class Ranks:
    def __init__(self, size, slab):
        self.size, self.along = size, size // 2
        along = self.along

        def owner(i, slot):
            other, place = divmod(slot, along)
            return ((i - 2 * place) % size) ^ other

        def slot(i, owner):
            other = (owner ^ i) & 1
            return other * along + (i - (owner ^ other)) % size // 2

        columns = {}
        for k in range(size):
            columns["owner", k] = lambda i, k=k: owner(i, k)
        for k in range(size):
            columns["slot", k] = lambda i, k=k: slot(i, k)
        columns["slab"] = lambda i: i * slab
        self.at = Numbers("tensor", size, columns)

    def core(self, values):
        return lax.ppermute(values, "tensor", [(i, i ^ 1) for i in range(self.size)])

    def shift(self, values, places):
        return lax.ppermute(values, "tensor", [(i, (i + 2 * places) % self.size) for i in range(self.size)])

    def gather(self, own):
        held = [own]
        for _ in range(1, self.along):
            held.append(self.shift(held[-1], 1))
        return jnp.concatenate(held + [self.core(values) for values in held], axis=0)


def total_over(values, axis, size):
    step = 1
    while step < size:
        values = values + lax.ppermute(values, axis, [(i, i ^ step) for i in range(size)])
        step *= 2
    return values


def after(values, *earlier):
    return lax.optimization_barrier((values, *earlier))[0]


def body(
    ranks, dps, tokens, pre_gain, weight_gate, weight_inner, weight_step, weight_shared, conv_kernel, conv_offset,
    shared_kernel, shared_offset, step_bias, log_rate, skip_gain, gate_gain, weight_out, cotangent, segments, image_span,
):
    seqs, rows, model = tokens.shape
    length = rows * ranks
    pieces = length // STRETCH
    total = seqs * length
    channels = weight_gate.shape[1]
    heads = step_bias.shape[0]
    inner_width = channels * ranks
    width = weight_shared.shape[1]
    slab = width // ranks
    group = Ranks(ranks, slab)
    local = rows == STRETCH

    mixer = (token_of(jnp.arange(STRETCH))[:, None] == jnp.arange(STRETCH)[None, :]).astype(BF16)

    def reorder(values, dims=NN):
        blocks = values.reshape(-1, STRETCH, values.shape[-1])
        moved = [lax.dot_general(mixer, blocks[i], dims, preferred_element_type=BF16) for i in range(blocks.shape[0])]
        return jnp.concatenate(moved, axis=0).reshape(values.shape)

    def gather(values):
        if local:
            return group.gather(values.reshape(seqs * rows, model))
        every = lax.all_gather(values, "tensor", axis=1, tiled=True).reshape(seqs, pieces, STRETCH, model)
        return reorder(jnp.moveaxis(every, 1, 0)).reshape(total, model)

    def scatter(values):
        every = jnp.moveaxis(reorder(values, TN).reshape(pieces, seqs, STRETCH, model), 0, 1).reshape(seqs, length, model)
        return lax.psum_scatter(every, "tensor", scatter_dimension=1, tiled=True).astype(F32)

    def slabs(values):
        blocks = values.reshape(seqs, pieces, STRETCH, values.shape[-1])
        if not local:
            return jnp.moveaxis(blocks, 1, 0).reshape(values.shape)
        return jnp.concatenate(
            [rows_at(blocks, group.at["owner", slot], 1, 1)[:, 0] for slot in range(ranks)], axis=0
        ).reshape(values.shape)

    slots = jnp.arange(pieces, dtype=jnp.int32)
    if local:
        first = group.at.names["slot", 0]
        slots = group.at.row[0, first : first + pieces]
    own_low = reorder(tokens) if local else tokens
    cot_low = reorder(cotangent) if local else cotangent
    own = own_low.astype(F32)
    row_scale = lax.rsqrt(jnp.mean(own * own, axis=2, keepdims=True) + EPSILON)
    normed_low = (own * row_scale * pre_gain[None, None, :]).astype(BF16)
    tail = min(512, channels) - width - heads
    weight_ss = jnp.concatenate([weight_shared, weight_step, jnp.zeros((model, tail), BF16)], axis=1)
    pad_heads = lambda values: jnp.pad(values, (0, LANES - heads))[None, :]
    bias = pad_heads(step_bias)
    rate = pad_heads(-jnp.exp(log_rate))
    skip = jnp.repeat(skip_gain, HEAD)[None, :]
    heads_of = (jnp.arange(LANES)[:, None] == (jnp.arange(channels) // HEAD)[None, :]).astype(BF16)
    spread = jnp.concatenate([heads_of, heads_of], axis=0)
    seg_row = jnp.swapaxes(segments.astype(F32).reshape(seqs, pieces, 8, STRETCH // 8), 2, 3).reshape(1, total)
    offset_row, shared_offset_row = conv_offset[None, :], shared_offset[None, :]
    gain_row = gate_gain[None, :]

    slab = width // ranks
    weight_low = jnp.concatenate([weight_gate, weight_inner], axis=1)
    weight_side = jnp.concatenate(
        [
            rows_at(weight_shared, group.at["slab"], slab, 1),
            weight_step,
            jnp.zeros((model, LANES - slab - heads), BF16),
        ],
        axis=1,
    )
    blocked = local and ranks == 4
    if blocked:
        own_rows, cot_rows = normed_low.reshape(seqs * rows, model), cot_low.reshape(seqs * rows, model)
        far_rows = group.shift(own_rows, 1)
        far_cot = group.shift(after(cot_rows, own_rows), 1)
        weights = (weight_gate, weight_inner, weight_ss)
        first = fill_rows(own_rows, group.core(own_rows), weights, NN, None)
        first_cot = fill_rows(cot_rows, group.core(cot_rows), (weight_out,), NT, None, BF16)
        far_rows = after(far_rows, first[0], first_cot[0], weight_low, weight_side)
        pre, normed_in = fill_rows(far_rows, group.core(far_rows), weights, NN, first)
    else:
        normed_in, cot_full = gather(normed_low), gather(cot_low)
        weights = jnp.concatenate([weight_gate, weight_inner, weight_ss], axis=1)
        pre = lax.dot_general(normed_in, weights, NN, preferred_element_type=F32)
        grad = lax.dot_general(cot_full, weight_out, NT, preferred_element_type=BF16)
    y, gated, states, squares = scan_forward(
        slots, segments, image_span, pre, seg_row, spread, conv_kernel, offset_row, skip, shared_kernel, shared_offset_row,
        bias, rate,
    )
    if blocked:
        far_cot = after(far_cot, squares)
        grad, cot_full = fill_rows(far_cot, group.core(far_cot), (weight_out,), NT, first_cot, BF16)
    coupling = coupling_step(slots, seqs, gated, grad, gain_row)
    sums = total_over(jnp.concatenate([squares, coupling], axis=0), "tensor", ranks)
    scale_row = lax.rsqrt(sums[0:1] / inner_width + EPSILON)
    pull_row = scale_row * scale_row * scale_row / inner_width * sums[1:2]

    def backward(start, count, done, pull):
        return scan_backward(
            start, count, done, slots, segments, image_span, pre, grad, y, states, seg_row, scale_row, pull, spread,
            conv_kernel, offset_row, skip, gain_row, shared_kernel, shared_offset_row, bias, rate,
        )

    out_product = lambda left: lax.dot_general(left, cot_full, TN, preferred_element_type=BF16)
    made = {}
    ringed = local and dps == 8 and ranks == 4 and seqs > 1 and model == 2 * channels
    if ringed:
        ring = Ring(dps, ranks // 2, model, channels)
        join = lambda mine, arrived: (mine.astype(F32) + arrived.astype(F32)).astype(BF16)
        first = group.at.names["owner", 0]
        to_give, to_keep, norm_near, norm_far = split_norm_step(
            group.at.row[0, first : first + ranks], ring.at.row, seqs, gated, scale_row, gain_row, None,
            ring.at.names["give", 0], ring.at.names["keep", 0],
        )
        given = out_product(to_give)
        arrived = ring.exchange(given, 0)
        kept = out_product(after(to_keep, given))
        done = backward(0, seqs // 2, None, after(pull_row, kept))
        mixed_far = lax.dot_general(after(norm_far, done[0]), weight_out, NN, preferred_element_type=BF16)
        given, kept = ring.halve(after(kept, done[0], mixed_far), arrived, 1)
        arrived = ring.exchange(given, 1)
        done = backward(seqs // 2, seqs - seqs // 2, done, after(pull_row, given))
        given, kept = ring.halve(after(kept, done[0]), arrived, 2)
        low, shared_part, step_low, channel_grads, head_grads, shared_grads = done
        low_part = lax.dot_general(normed_in, after(low, given), TN, preferred_element_type=BF16)
        made["eighth"] = kept, ring.exchange(given, 2)
        low_part = after(low_part, made["eighth"][1])
    else:
        normed_out = norm_step(slots, seqs, gated, scale_row, gain_row)
        norm_near, norm_far = (normed_out[: total // 2], normed_out[total // 2 :]) if local else (normed_out, None)
        out_sum = lax.psum(out_product(normed_out), "dp")
        low, shared_part, step_low, channel_grads, head_grads, shared_grads = backward(0, seqs, None, pull_row)
        low_part = lax.dot_general(normed_in, low, TN, preferred_element_type=BF16)

    cut = total // 2 if local else 0
    half = ranks // 2
    by_rank = lambda values: values.reshape(-1, seqs, rows, model)

    def finished(hold=lambda values: values):
        if "finished" not in made:
            made["finished"] = join(hold(made["eighth"][0]), made["eighth"][1])
        return made["finished"]

    def finish(hold):
        return [finished(hold)] if ringed else []

    def columns_out(hold):
        columns = jnp.moveaxis(hold(shared_part).reshape(total, ranks, slab), 1, 0)
        columns = jnp.concatenate([rows_at(columns, group.at["owner", slot], 1) for slot in range(ranks)], axis=0)
        made["columns"] = columns[:half], group.core(columns[half:])
        return [columns]

    def columns_in(hold):
        shared_low = slabs(take_rows("columns", hold).astype(BF16))
        made["side"] = jnp.concatenate([shared_low, step_low[:, :heads], jnp.zeros((total, LANES - slab - heads), BF16)], axis=1)
        return [made["side"]]

    def pass_on(name):
        def run(hold):
            mine, other = made[name]
            sent = [(hold(mine)[i].astype(F32) + other[i].astype(F32)).astype(BF16) for i in range(1, half)]
            made[name] = mine[0], [other[0]] + [group.shift(values, -1 - i) for i, values in enumerate(sent)]
            return sent

        return run if local or name == "columns" else lambda hold: []

    def take_rows(name, hold):
        mine, others = made[name]
        mine = hold(mine).astype(F32)
        for values in others:
            mine = mine + values.astype(F32)
        return mine

    def input_rows_of(slot):
        part = slice(slot * seqs * rows, (slot + 1) * seqs * rows) if local else slice(0, total)

        def run(hold):
            side, low_rows = lax.optimization_barrier((hold(made["side"]), low))
            summed = lax.dot_general(side[part], weight_side, NT, preferred_element_type=F32)
            summed = (summed + lax.dot_general(low_rows[part], weight_low, NT, preferred_element_type=F32)).astype(BF16)
            if local:
                made["input", slot] = by_rank(summed)[0]
                if slot >= half:
                    made["input", slot] = group.core(made["input", slot])
            else:
                made["input"] = scatter(summed), []
            return [summed]

        return run

    def input_pair(hold):
        if local:
            made["input"] = [made["input", slot] for slot in range(half)], [made["input", slot] for slot in range(half, ranks)]
        return []

    def mix_of(far):
        def run(hold):
            if far and ringed:
                made["mixed far"] = group.core(by_rank(hold(mixed_far)))
                return []
            product = lax.dot_general(hold(norm_far if far else norm_near), weight_out, NN, preferred_element_type=BF16)
            if not local:
                made["mixed"] = scatter(product), []
            elif far:
                made["mixed far"] = group.core(by_rank(product))
            else:
                made["mixed"] = by_rank(product), made["mixed far"]
            return [product]

        return run

    def side_product(hold):
        product = lax.dot_general(hold(made["side"]), normed_in, TN, preferred_element_type=BF16)
        made["side_part"] = product[: slab + heads]
        return [made["side_part"]]

    def input_rows(hold):
        normed_grad = take_rows("input", hold)
        own = hold(own_low).astype(F32)
        weighted = normed_grad * pre_gain[None, None, :]
        projection = jnp.sum(weighted * own, axis=2, keepdims=True)
        own_grad = row_scale * weighted - row_scale * row_scale * row_scale / model * own * projection
        made["pre_gain"] = jnp.sum(normed_grad * own * row_scale, axis=(0, 1))
        made["tokens_grad"] = (cot_low.astype(F32) + own_grad).astype(BF16)
        return [made["tokens_grad"], made["pre_gain"]]

    def input_order(hold):
        if local:
            made["tokens_grad"] = reorder(hold(made["tokens_grad"]), TN)
        return [made["tokens_grad"]]

    def block_rows(hold):
        made["block_out"] = (hold(own_low).astype(F32) + take_rows("mixed", hold)).astype(BF16)
        return [made["block_out"]]

    def block_order(hold):
        if local:
            made["block_out"] = reorder(hold(made["block_out"]), TN)
        return [made["block_out"]]

    def small_start(hold):
        made["small"] = jnp.concatenate(
            [jnp.pad(hold(shared_grads), ((0, 0), (0, channels - width))), made["pre_gain"].reshape(-1, channels)], axis=0
        )
        return []

    def pack(hold):
        made["small"] = jnp.concatenate(
            [channel_grads, jnp.pad(head_grads, ((0, 0), (0, channels - LANES))), made["small"]], axis=0
        )
        return []

    def spread_sum(name, axis, size, bits, kind=F32):
        partners = [0]
        for bit in bits:
            partners += [partner ^ (1 << bit) for partner in partners]

        def send(hold):
            values = hold(made[name])
            made[name] = values, [lax.ppermute(values, axis, [(i, i ^ k) for i in range(size)]) for k in partners[1:]]
            return [values]

        def receive(hold):
            values, others = hold(made[name])
            terms = [values.astype(F32)] + [other.astype(F32) for other in others]
            while len(terms) > 1:
                terms = [terms[i] + terms[i + 1] for i in range(0, len(terms), 2)]
            made[name] = terms[0].astype(kind)
            return [made[name]]

        return send, receive

    def together(*parts):
        def run(hold):
            return [value for part in parts for value in part(hold)]

        return run

    bits_of = lambda size: list(range((size - 1).bit_length()))
    tensor_send, tensor_take = spread_sum("small", "tensor", ranks, bits_of(ranks))
    small_dp = [spread_sum("small", "dp", dps, bits) for bits in (bits_of(dps)[1:], bits_of(dps)[:1])]
    if ringed:
        side_dp = [spread_sum("side_part", "dp", dps, [bit], BF16) for bit in range(3)]
    else:

        def side_whole(hold):
            made["side_part"] = lax.psum(made["side_part"], "dp")
            return []

        side_dp = [(side_whole, lambda hold: [])] + [(lambda hold: [], lambda hold: [])] * 2
    nothing = lambda hold: []
    far = [input_rows_of(slot) for slot in (range(half, ranks) if local else range(1))]
    near = [input_rows_of(slot) for slot in (range(half) if local else range(0))]
    def gather_near(hold):
        slabs_of = hold(made["side_part"])[:slab]
        made["gathered"] = [slabs_of]
        for _ in range(1, half):
            made["gathered"].append(group.shift(made["gathered"][-1], 1))
        return []

    def gather_far(hold):
        made["gathered"] = made["gathered"] + [group.core(hold(values)) for values in made["gathered"]]
        return []

    def side_outputs(hold):
        gathered = jnp.stack([hold(values) for values in made["gathered"]])
        shared = jnp.concatenate([rows_at(gathered, group.at["slot", owner], 1)[0] for owner in range(ranks)], axis=0)
        made["shared"] = shared.T.astype(F32)
        made["step"] = hold(made["side_part"])[slab : slab + heads].T.astype(F32)
        return [made["shared"], made["step"]]

    def small_outputs(hold):
        packed = hold(made["small"])
        shared_sums = packed[16:24, :width]
        made["outputs"] = [
            packed[24:].reshape(model), packed[0:4], packed[4], shared_sums[0:4], shared_sums[4], packed[9, :heads],
            packed[8, :heads], jnp.sum(packed[5].reshape(heads, HEAD), axis=1), packed[6],
        ]
        return []

    fillers = [
        together(mix_of(True) if local else nothing, columns_out),
        together(pass_on("columns"), mix_of(False)),
        together(columns_in, side_product),
        together(side_dp[0][0], *far[:1]),
        together(side_dp[0][1], side_dp[1][0], *far[1:2]),
        *far[2:],
        together(*near[:1], finish),
        together(side_dp[1][1], *near[1:2]),
        *near[2:],
        together(input_pair, pass_on("input")),
        together(pass_on("mixed"), side_dp[2][0]),
        together(input_rows, side_dp[2][1]),
        together(small_start, tensor_send, input_order, gather_near),
        together(tensor_take, pack, small_dp[0][0], block_rows),
        together(block_order, gather_far),
        together(small_dp[0][1], small_dp[1][0], side_outputs),
    ]
    if ringed:
        sums = [blank((model, channels)), blank((model, channels)), blank((channels, model))]
        sums, last = ring.all_reduce(low_part, sums, fillers, finished)
        grads = dict(zip(("gate", "inner", "out"), sums))
    else:
        low_sum = lax.psum(low_part, "dp").astype(F32)
        grads = {"gate": low_sum[:, :channels], "inner": low_sum[:, channels:], "out": out_sum.astype(F32)}
        for filler in fillers:
            filler(lambda values: values)
    finish_small = together(small_dp[1][1], small_outputs)
    finish_small((lambda values: after(values, *last)) if ringed else (lambda values: values))
    gain, kernel_grad, offset_grad, shared_kernel_grad, shared_offset_grad, bias_grad, rate_grad, skip_grad, gate_gain_grad = made[
        "outputs"
    ]
    return (
        made["block_out"],
        made["tokens_grad"],
        gain,
        grads["gate"],
        grads["inner"],
        made["step"],
        made["shared"],
        kernel_grad,
        offset_grad,
        shared_kernel_grad,
        shared_offset_grad,
        bias_grad,
        rate_grad,
        skip_grad,
        gate_gain_grad,
        grads["out"],
    )


def solution(mesh):
    placed = (
        P("dp", "tensor", None),
        P(),
        P(None, "tensor"),
        P(None, "tensor"),
        P(None, "tensor"),
        P(),
        P(None, "tensor"),
        P("tensor"),
        P(),
        P(),
        P("tensor"),
        P("tensor"),
        P("tensor"),
        P("tensor"),
        P("tensor", None),
        P("dp", "tensor", None),
        P("dp", None),
        P("dp", None),
    )
    return jax.shard_map(
        partial(body, mesh.shape["tensor"], mesh.shape["dp"]),
        mesh=mesh,
        in_specs=placed,
        out_specs=(
            P("dp", "tensor", None),
            P("dp", "tensor", None),
            P(),
            P(None, "tensor"),
            P(None, "tensor"),
            P(None, "tensor"),
            P(),
            P(None, "tensor"),
            P("tensor"),
            P(),
            P(),
            P("tensor"),
            P("tensor"),
            P("tensor"),
            P("tensor"),
            P("tensor", None),
        ),
        check_vma=False,
    )
```

```python
from functools import partial

import jax
import jax.numpy as jnp
from jax import lax
from jax.experimental import pallas as pl
from jax.experimental.pallas import tpu as pltpu
from jax.sharding import PartitionSpec as P

STRETCH = 256
HEAD = 64
LANES = 128

EPSILON = 1e-05
LOG2E = 1.4426950408889634
BF16 = jnp.bfloat16
F32 = jnp.float32
NN = (((1,), (0,)), ((), ()))
NT = (((1,), (1,)), ((), ()))
TN = (((0,), (0,)), ((), ()))


def mm(left, right, dims=NN):
    return lax.dot_general(left.astype(BF16), right.astype(BF16), dims, preferred_element_type=F32)


def two_parts(values):
    high = values.astype(BF16)
    return high, (values - high.astype(F32)).astype(BF16)


def iota(shape, axis):
    return lax.broadcasted_iota(jnp.int32, shape, axis)


def expand(values, spread):
    high, low = two_parts(values)
    return mm(jnp.concatenate([high, low], axis=1), spread)


def head_sum(values, spread):
    high, low = two_parts(values)
    half = spread[:LANES]
    return mm(high, half, NT) + mm(low, half, NT)


def column_of(row, eye):
    return jnp.sum(jnp.where(eye, row, 0.0), axis=1, keepdims=True)


def token_of(rows):
    return (rows & 7) * (STRETCH // 8) + (rows >> 3)


def lagged(current, before):
    last = current[STRETCH - 24 :]
    top = iota(last.shape, 0) & 7
    first = jnp.where(top == 0, pltpu.roll(before, 17, 0), pltpu.roll(last, 1, 0))
    joined = jnp.concatenate([first, current], axis=0)
    return [joined[8 * tap : 8 * tap + STRETCH] for tap in range(4)]


def leading(current, after):
    first = current[:24]
    top = iota(first.shape, 0) & 7
    last = jnp.where(top == 7, pltpu.roll(after, 7, 0), pltpu.roll(first, 23, 0))
    joined = jnp.concatenate([current, last], axis=0)
    return [joined[24 - 8 * tap : 24 - 8 * tap + STRETCH] for tap in range(4)]


def taps(values, kernel):
    total = kernel[0:1] * values[0]
    for tap in range(1, 4):
        total = total + kernel[tap : tap + 1] * values[tap]
    return total


def column_sum(values):
    return jnp.sum(values, axis=0, keepdims=True)


def piece_context(seg_sm, span_sm, seg_row, step_pre, bias, rate, seq, piece):
    rows = STRETCH
    i0, i1 = token_of(iota((rows, rows), 0)), token_of(iota((rows, rows), 1))
    order = i0 - i1
    eye = order == 0
    seg_r = seg_row[...]
    seg_c = column_of(seg_r, eye)
    first = span_sm[seq, 0]
    image = jnp.logical_and(piece >= first, piece < first + span_sm[seq, 1])
    reach_all = jnp.where(image, 2 * rows, 0)
    same = seg_c == seg_r
    start = piece * rows
    last_doc = seg_sm[seq, start + rows - 1].astype(F32)
    before_doc = seg_sm[seq, jnp.maximum(start - 1, 0)].astype(F32)
    pre = step_pre + bias
    tail = jnp.exp(-jnp.abs(pre))
    step = jnp.maximum(pre, 0.0) + jnp.log1p(tail)
    log_step = step * rate
    high, low = two_parts(log_step)
    lowest = (log_step - high.astype(F32) - low.astype(F32)).astype(BF16)
    ahead = (order >= 0).astype(F32)
    cum = mm(ahead, high) + mm(ahead, low) + mm(ahead, lowest)
    cum = cum * LOG2E
    end = cum[rows - 1 : rows]
    to_end = jnp.where(seg_c == last_doc, jnp.exp2(end - cum), 0.0)
    reach = jnp.where(seg_c == before_doc, jnp.exp2(cum), 0.0)
    keep = jnp.where(last_doc == before_doc, jnp.exp2(end), 0.0)
    sign = jnp.where(order > 0, 1.0, jnp.where(order < 0, -1.0, 0.0))
    return eye, order, reach_all, same, sign, pre, step, log_step, cum, to_end, reach, keep


def forward_kernel(
    channels, slots, seg_sm, span_sm, pre, seg_row, spread, kernel, offset, skip, shared_kernel, shared_offset, bias, rate,
    y_out, gated_out, state_out, square_out, before, shared_before, state,
):
    seq, piece = pl.program_id(0), pl.program_id(1)
    width = shared_kernel.shape[1]
    half = width // 2

    @pl.when(piece == 0)
    def _():
        before[...] = jnp.zeros_like(before)
        shared_before[...] = jnp.zeros_like(shared_before)
        state[...] = jnp.zeros_like(state)

    shared_pre = pre[:, 2 * channels : 2 * channels + width]
    step_columns = pre[:, 2 * channels + width : 2 * channels + width + LANES]
    _, order, reach_all, same, sign, _, step, _, cum, to_end, reach, keep = piece_context(
        seg_sm, span_sm, seg_row, step_columns, bias[...], rate[...], seq, piece
    )
    allowed = jnp.logical_and(same, order + reach_all >= 0)
    conv = taps(lagged(shared_pre, shared_before[...]), shared_kernel) + shared_offset[...]
    shared_before[...] = shared_pre[STRETCH - 24 :]
    act = conv * jax.nn.sigmoid(conv)
    b, c = act[:, :half].astype(BF16), act[:, half:].astype(BF16)
    scores = jnp.where(allowed, mm(c, b, NT), 0.0)
    cum_rows = cum.T
    b_cols = b.T
    lane = iota((STRETCH, LANES), 1)
    spread_all = spread[...]

    gate = pre[:, :channels]
    inner = pre[:, channels : 2 * channels]
    v = taps(lagged(inner, before[...]), kernel) + offset[...]
    before[...] = inner[STRETCH - 24 :]
    x = v * jax.nn.sigmoid(v)
    u = x * expand(step, spread_all)
    entering = state[...]
    state_out[0, 0] = entering.astype(BF16)
    carried = mm(c, entering) * expand(reach, spread_all)
    keep_row = expand(jnp.broadcast_to(keep, (8, LANES)), spread_all)[0:1]
    state[...] = keep_row * entering + mm(b_cols, u * expand(to_end, spread_all))
    u_low = u.astype(BF16)
    mixed = []
    for pair in range(channels // LANES):
        pair_u = u_low[:, pair * LANES : (pair + 1) * LANES]
        halves = []
        for head in (2 * pair, 2 * pair + 1):
            gap = cum[:, head : head + 1] - cum_rows[head : head + 1]
            halves.append(mm(scores * jnp.exp2(gap * sign), pair_u))
        mixed.append(jnp.where(lane < HEAD, halves[0], halves[1]))
    y = jnp.concatenate(mixed, axis=1) + carried + skip[...] * x
    y_out[...] = y
    gated = y * (gate * jax.nn.sigmoid(gate))
    gated_out[...] = gated.astype(BF16)
    square_out[...] = mm(jnp.ones((8, channels), BF16), gated * gated, NT)[0:1]


def coupling_kernel(slots, gated, grad, gain, coupling_out):
    product = grad[...].astype(F32) * (gated[...].astype(F32) * gain[...])
    coupling_out[...] = mm(jnp.ones((8, gain.shape[1]), BF16), product, NT)[0:1]


def norm_kernel(slots, gated, scale_row, gain, low_out):
    eye = iota((STRETCH, STRETCH), 0) == iota((STRETCH, STRETCH), 1)
    scale = column_of(scale_row[...], eye)
    low_out[...] = (gated[...].astype(F32) * gain[...] * scale).astype(BF16)


def backward_kernel(
    channels, start, slots, seg_sm, span_sm, pre, halo, grad_in, y_in, state_in, seg_row, scale_row, pull_row, spread, kernel,
    offset, skip, gain, shared_kernel, shared_offset, bias, rate,
    *rest,
):
    earlier = rest[3:6] if start else None
    low_out, shared_out, step_out, channel_grads, head_grads, shared_grads, after, lam, shared_after = rest[-9:]
    seq = pl.program_id(0) + start
    backward_piece = pl.program_id(1)
    piece = pl.num_programs(1) - 1 - backward_piece
    width = shared_kernel.shape[1]
    half = width // 2
    rows = STRETCH

    @pl.when(backward_piece == 0)
    def _():
        after[...] = jnp.zeros_like(after)
        lam[...] = jnp.zeros_like(lam)
        shared_after[...] = jnp.zeros_like(shared_after)

    @pl.when(jnp.logical_and(backward_piece == 0, seq == start))
    def _():
        for i, total in enumerate((channel_grads, head_grads, shared_grads)):
            total[...] = earlier[i][...] if start else jnp.zeros_like(total)

    inside = jnp.where(piece > 0, 1.0, 0.0)
    shared_pre = pre[:, 2 * channels : 2 * channels + width]
    step_columns = pre[:, 2 * channels + width : 2 * channels + width + LANES]
    eye, order, reach_all, same, sign, step_pre, step, log_step, cum, to_end, reach, keep = piece_context(
        seg_sm, span_sm, seg_row, step_columns, bias[...], rate[...], seq, piece
    )
    allowed = jnp.logical_and(same, order + reach_all >= 0)
    allowed_t = jnp.logical_and(same, reach_all - order >= 0)
    conv = taps(lagged(shared_pre, halo[8:32, 2 * channels : 2 * channels + width] * inside), shared_kernel) + shared_offset[...]
    shared_sig = jax.nn.sigmoid(conv)
    act = conv * shared_sig
    b, c = act[:, :half].astype(BF16), act[:, half:].astype(BF16)
    scores = jnp.where(allowed, mm(c, b, NT), 0.0)
    scores_t = jnp.where(allowed_t, mm(b, c, NT), 0.0)
    signed = scores * sign
    cum_rows = cum.T
    c_cols = c.T
    lane = iota((rows, LANES), 1)
    head_row = iota((LANES, rows), 0)

    scale = column_of(scale_row[...], eye)
    pull = column_of(pull_row[...], eye)
    gate = pre[:, :channels]
    y = y_in[...]
    gate_sig = jax.nn.sigmoid(gate)
    silu = gate * gate_sig
    gated = y * silu
    scaled_grad = scale * grad_in[...].astype(F32)
    d_gated = gain[...] * scaled_grad - pull * gated
    low_out[:, :channels] = (d_gated * y * (gate_sig + silu * (1.0 - gate_sig))).astype(BF16)
    channel_grads[6:7] += column_sum(scaled_grad * gated)
    dy = d_gated * silu

    inner = pre[:, channels : 2 * channels]
    v = taps(lagged(inner, halo[8:32, channels : 2 * channels] * inside), kernel) + offset[...]
    sig = jax.nn.sigmoid(v)
    x = v * sig
    spread_all = spread[...]
    step_x = expand(step, spread_all)
    to_end_x = expand(to_end, spread_all)
    keep_row = expand(jnp.broadcast_to(keep, (8, LANES)), spread_all)[0:1]
    u = x * step_x
    u_low = u.astype(BF16)
    dy_low = dy.astype(BF16)
    entering = state_in[0, 0]
    lam_now = lam[...]
    lam_low = lam_now.astype(BF16)
    reached_full = dy * expand(reach, spread_all)
    reached = reached_full.astype(BF16)
    pulled = mm(b, lam_low) * to_end_x
    d_c = mm(reached, entering, NT)
    d_b = mm(u * to_end_x, lam_low, NT)
    from_start = reached_full * mm(c, entering)
    from_end = u * pulled
    edge = column_sum(from_end) + keep_row * column_sum(lam_now * entering.astype(F32))
    lam[...] = keep_row * lam_now + mm(c_cols, reached)

    d_scores = jnp.zeros((rows, rows), F32)
    row_sums = jnp.zeros((rows, LANES), F32)
    col_sums = jnp.zeros((LANES, rows), F32)
    du_parts = []
    for pair in range(channels // LANES):
        cols = slice(pair * LANES, (pair + 1) * LANES)
        pair_u, pair_dy = u_low[:, cols], dy_low[:, cols]
        halves = []
        for one in range(2):
            head = 2 * pair + one
            own = lane < HEAD if one == 0 else lane >= HEAD
            gap = cum[:, head : head + 1] - cum_rows[head : head + 1]
            decay = jnp.exp2(gap * sign)
            d_mix = mm(jnp.where(own, pair_dy, jnp.zeros_like(pair_dy)), pair_u, NT) * decay
            d_scores = d_scores + d_mix
            turned = d_mix * signed
            row_sums = row_sums + jnp.where(lane == head, jnp.sum(turned, axis=1, keepdims=True), 0.0)
            col_sums = col_sums + jnp.where(head_row == head, column_sum(turned), 0.0)
            halves.append(mm(scores_t * decay, pair_dy))
        du_parts.append(jnp.where(lane < HEAD, halves[0], halves[1]))
    du = jnp.concatenate(du_parts, axis=1) + pulled
    d_scores = jnp.where(allowed, d_scores, 0.0).astype(BF16)
    d_c = d_c + mm(d_scores, b)
    d_b = d_b + mm(d_scores, c, TN)

    d_cum = row_sums - col_sums.T + head_sum(from_start - from_end, spread_all)
    high, low = two_parts(d_cum)
    behind = (order <= 0).astype(F32)
    d_log = mm(behind, high) + mm(behind, low) + head_sum(jnp.broadcast_to(edge, (8, channels)), spread_all)[0:1]
    d_step = (d_log * rate[...] + head_sum(x * du, spread_all)) * jax.nn.sigmoid(step_pre)
    d_step = jnp.where(lane < channels // HEAD, d_step, 0.0)
    step_out[...] = d_step.astype(BF16)
    head_grads[0:1] += column_sum(d_log * log_step)
    head_grads[1:2] += column_sum(d_step)

    dx = step_x * du + skip[...] * dy
    dv = dx * (sig + x * (1.0 - sig))
    ahead = leading(dv, after[...])
    after[...] = dv[:24]
    low_out[:, channels:] = taps(ahead, kernel).astype(BF16)
    for tap in range(4):
        channel_grads[tap : tap + 1] += column_sum(ahead[tap] * inner)
    channel_grads[4:5] += column_sum(dv)
    channel_grads[5:6] += column_sum(dy * x)

    d_conv = jnp.concatenate([d_b, d_c], axis=1) * (shared_sig + act * (1.0 - shared_sig))
    ahead = leading(d_conv, shared_after[...])
    shared_after[...] = d_conv[:24]
    shared_out[...] = taps(ahead, shared_kernel).astype(BF16)
    for tap in range(4):
        shared_grads[tap : tap + 1] += column_sum(ahead[tap] * shared_pre)
    shared_grads[4:5] += column_sum(d_conv)


def whole(shape):
    return pl.BlockSpec(shape, lambda *_: (0,) * len(shape))


def limits(mebibytes):
    return pltpu.CompilerParams(vmem_limit_bytes=mebibytes << 20)


def cost(flops, moved):
    return pl.CostEstimate(flops=int(flops), bytes_accessed=int(moved), transcendentals=0)


def fill_kernel(dims, spans, first, own, other, *rest):
    weights = rest[: len(spans)]
    product, joined, held, sems = rest[-4:]
    rows = own.shape[0]
    tile = product.shape[1]
    index, step = pl.program_id(0), pl.program_id(1)
    copies = [
        pltpu.make_async_copy(block, joined.at[pl.ds((2 * i + first) * rows, rows)], sems.at[i])
        for i, block in enumerate((own, other))
    ]
    for i, block in enumerate((own, other)):

        @pl.when(jnp.logical_and(index == 0, step == i))
        def _():
            copies[i].start()
            held[i] = block[...]

    for (start, count), weight in zip(spans, weights):

        @pl.when(jnp.logical_and(index >= start, index < start + count))
        def _():
            product[...] = lax.dot_general(held[step], weight[...], dims, preferred_element_type=F32).astype(product.dtype)

    @pl.when(jnp.logical_and(index == pl.num_programs(0) - 1, step == 1))
    def _():
        for copy in copies:
            copy.wait()


def fill_rows(own, other, weights, dims, filled, kind=F32):
    rows, depth = own.shape
    side = 1 if dims == NN else 0
    widths = [values.shape[side] for values in weights]
    tile = min(512, *widths)
    spans, first = [], 0
    for width in widths:
        spans.append((first, width // tile))
        first += width // tile
    second = filled is not None
    anywhere = pl.BlockSpec(memory_space=pl.ANY)

    def weight_spec(span):
        column = lambda j: jnp.clip(j - span[0], 0, span[1] - 1)
        if dims == NN:
            return pl.BlockSpec((depth, tile), lambda j, i: (0, column(j)))
        return pl.BlockSpec((tile, depth), lambda j, i: (column(j), 0))

    count = len(weights)
    block = lambda i: 2 * i + (1 if second else 0)
    return pl.pallas_call(
        partial(fill_kernel, dims, spans, 1 if second else 0),
        name="fill_rows",
        grid=(first, 2),
        in_specs=[whole(own.shape), whole(other.shape)]
        + [weight_spec(span) for span in spans]
        + ([anywhere] * 2 if second else []),
        out_specs=[
            pl.BlockSpec((rows, tile), lambda j, i: (block(i), j)),
            anywhere,
        ],
        out_shape=[jax.ShapeDtypeStruct((4 * rows, sum(widths)), kind), jax.ShapeDtypeStruct((4 * rows, depth), BF16)],
        scratch_shapes=[pltpu.VMEM((2, rows, depth), BF16), pltpu.SemaphoreType.DMA((2,))],
        input_output_aliases={2 + count: 0, 3 + count: 1} if second else {},
        compiler_params=pltpu.CompilerParams(dimension_semantics=("arbitrary", "arbitrary")),
        cost_estimate=cost(4 * rows * depth * sum(widths), 4 * rows * (depth + sum(widths))),
    )(own, other, *weights, *(filled if second else ()))


def blank(shape):
    return pl.pallas_call(
        lambda out: None, name="blank", out_specs=pl.BlockSpec(memory_space=pl.ANY), out_shape=jax.ShapeDtypeStruct(shape, F32)
    )()


def scan_forward(slots, segments, spans, pre, seg_row, spread, kernel, offset, skip, shared_kernel, shared_offset, bias, rate):
    seqs, length = segments.shape
    pieces = length // STRETCH
    channels = kernel.shape[1]
    width = shared_kernel.shape[1]
    at = lambda s, p, where, *_: (where[p] * seqs + s, 0)
    row_at = lambda s, p, *_: (0, s * pieces + p)
    total = seqs * length
    return pl.pallas_call(
        partial(forward_kernel, channels),
        name="scan_forward",
        grid_spec=pltpu.PrefetchScalarGridSpec(
            num_scalar_prefetch=3,
            grid=(seqs, pieces),
            in_specs=[
                pl.BlockSpec((STRETCH, pre.shape[1]), at),
                pl.BlockSpec((1, STRETCH), row_at),
                whole(spread.shape), whole(kernel.shape), whole(offset.shape), whole(skip.shape),
                whole(shared_kernel.shape), whole(shared_offset.shape), whole(bias.shape), whole(rate.shape),
            ],
            out_specs=[
                pl.BlockSpec((STRETCH, channels), at),
                pl.BlockSpec((STRETCH, channels), at),
                pl.BlockSpec((1, 1, width // 2, channels), lambda s, p, *_: (s, p, 0, 0)),
                pl.BlockSpec((1, STRETCH), row_at),
            ],
            scratch_shapes=[
                pltpu.VMEM((24, channels), F32), pltpu.VMEM((24, width), F32), pltpu.VMEM((width // 2, channels), F32),
            ],
        ),
        out_shape=[
            jax.ShapeDtypeStruct((total, channels), F32),
            jax.ShapeDtypeStruct((total, channels), BF16),
            jax.ShapeDtypeStruct((seqs, pieces, width // 2, channels), BF16),
            jax.ShapeDtypeStruct((1, total), F32),
        ],
        compiler_params=pltpu.CompilerParams(dimension_semantics=("arbitrary", "arbitrary")),
        cost_estimate=cost(20e9, 40e6),
    )(slots, segments, spans, pre, seg_row, spread, kernel, offset, skip, shared_kernel, shared_offset, bias, rate)


def coupling_step(slots, seqs, gated, grad, gain):
    total, channels = gated.shape
    pieces = total // STRETCH // seqs
    at = lambda s, p, where: (where[p] * seqs + s, 0)
    return pl.pallas_call(
        coupling_kernel,
        name="coupling",
        grid_spec=pltpu.PrefetchScalarGridSpec(
            num_scalar_prefetch=1,
            grid=(seqs, pieces),
            in_specs=[pl.BlockSpec((STRETCH, channels), at), pl.BlockSpec((STRETCH, channels), at), whole(gain.shape)],
            out_specs=pl.BlockSpec((1, STRETCH), lambda s, p, *_: (0, s * pieces + p)),
        ),
        out_shape=jax.ShapeDtypeStruct((1, total), F32),
        compiler_params=limits(8),
        cost_estimate=cost(2e9, 12e6),
    )(slots, gated, grad, gain)


def split_norm_step(owners, numbers, seqs, gated, scale_row, gain, row, give, keep):
    total, channels = gated.shape
    count = total // STRETCH
    pieces = count // seqs

    def kernel(owners, numbers, gated, scale_row, gain, given, kept, near, far, held):
        eye = iota((STRETCH, STRETCH), 0) == iota((STRETCH, STRETCH), 1)
        scale = column_of(scale_row[...], eye)
        low = (gated[...].astype(F32) * gain[...] * scale).astype(BF16)
        held[...] = low
        for out, name in ((given, give), (kept, keep)):
            start = pl.multiple_of(numbers[0, name] * (channels // 2), LANES)
            out[...] = held[:, pl.ds(start, channels // 2)]

        @pl.when(pl.program_id(0) < count // 2)
        def _():
            near[...] = low

        @pl.when(pl.program_id(0) >= count // 2)
        def _():
            far[...] = low

    at = lambda i, *_: (i, 0)
    half_block = pl.BlockSpec((STRETCH, channels // 2), at)
    return pl.pallas_call(
        kernel,
        name="norm_rows",
        grid_spec=pltpu.PrefetchScalarGridSpec(
            num_scalar_prefetch=2,
            grid=(count,),
            in_specs=[
                pl.BlockSpec((STRETCH, channels), at),
                pl.BlockSpec((1, STRETCH), lambda i, own, *_: (0, i % seqs * pieces + own[i // seqs])),
                whole(gain.shape),
            ],
            out_specs=[
                half_block,
                half_block,
                pl.BlockSpec((STRETCH, channels), lambda i, *_: (jnp.minimum(i, count // 2 - 1), 0)),
                pl.BlockSpec((STRETCH, channels), lambda i, *_: (jnp.maximum(i - count // 2, 0), 0)),
            ],
            scratch_shapes=[pltpu.VMEM((STRETCH, channels), BF16)],
        ),
        out_shape=[jax.ShapeDtypeStruct((total, channels // 2), BF16)] * 2
        + [jax.ShapeDtypeStruct((total // 2, channels), BF16)] * 2,
        compiler_params=limits(12),
        cost_estimate=cost(1e9, 12e6),
    )(owners, numbers, gated, scale_row, gain)


def norm_step(slots, seqs, gated, scale_row, gain):
    total, channels = gated.shape
    pieces = total // STRETCH // seqs
    at = lambda s, p, where: (where[p] * seqs + s, 0)
    return pl.pallas_call(
        norm_kernel,
        name="norm_rows",
        grid_spec=pltpu.PrefetchScalarGridSpec(
            num_scalar_prefetch=1,
            grid=(seqs, pieces),
            in_specs=[
                pl.BlockSpec((STRETCH, channels), at),
                pl.BlockSpec((1, STRETCH), lambda s, p, *_: (0, s * pieces + p)),
                whole(gain.shape),
            ],
            out_specs=pl.BlockSpec((STRETCH, channels), at),
        ),
        out_shape=jax.ShapeDtypeStruct((total, channels), BF16),
        compiler_params=limits(8),
        cost_estimate=cost(1e9, 8e6),
    )(slots, gated, scale_row, gain)


def scan_backward(
    start, count, done, slots, segments, spans, pre, grad, y, states, seg_row, scale_row, pull_row, spread, kernel, offset, skip, gain,
    shared_kernel, shared_offset, bias, rate,
):
    seqs, length = segments.shape
    pieces = length // STRETCH
    channels = kernel.shape[1]
    width = shared_kernel.shape[1]
    total = seqs * length
    piece_at = lambda p: pieces - 1 - p
    at = lambda s, p, where, *_: (where[piece_at(p)] * seqs + s + start, 0)
    row_at = lambda s, p, *_: (0, (s + start) * pieces + piece_at(p))
    halo_at = lambda s, p, where, *_: (
        (where[jnp.maximum(piece_at(p) - 1, 0)] * seqs + s + start) * (STRETCH // 32) + STRETCH // 32 - 1, 0
    )
    plain_at = lambda s, p, *_: ((s + start) * pieces + piece_at(p), 0)
    return pl.pallas_call(
        partial(backward_kernel, channels, start),
        name="scan_backward",
        grid_spec=pltpu.PrefetchScalarGridSpec(
            num_scalar_prefetch=3,
            grid=(count, pieces),
            in_specs=[
                pl.BlockSpec((STRETCH, pre.shape[1]), at),
                pl.BlockSpec((32, pre.shape[1]), halo_at),
                pl.BlockSpec((STRETCH, channels), at),
                pl.BlockSpec((STRETCH, channels), at),
                pl.BlockSpec((1, 1, width // 2, channels), lambda s, p, *_: (s + start, piece_at(p), 0, 0)),
                pl.BlockSpec((1, STRETCH), row_at),
                pl.BlockSpec((1, STRETCH), row_at),
                pl.BlockSpec((1, STRETCH), row_at),
                whole(spread.shape), whole(kernel.shape), whole(offset.shape), whole(skip.shape), whole(gain.shape),
                whole(shared_kernel.shape), whole(shared_offset.shape), whole(bias.shape), whole(rate.shape),
            ]
            + ([pl.BlockSpec(memory_space=pl.ANY)] * 3 + [whole(values.shape) for values in done[3:]] if start else []),
            out_specs=[
                pl.BlockSpec((STRETCH, 2 * channels), at),
                pl.BlockSpec((STRETCH, width), plain_at),
                pl.BlockSpec((STRETCH, LANES), at),
                whole((8, channels)),
                whole((8, LANES)),
                whole((8, width)),
            ],
            scratch_shapes=[
                pltpu.VMEM((24, channels), F32), pltpu.VMEM((width // 2, channels), F32), pltpu.VMEM((24, width), F32),
            ],
        ),
        out_shape=[
            jax.ShapeDtypeStruct((total, 2 * channels), BF16),
            jax.ShapeDtypeStruct((total, width), BF16),
            jax.ShapeDtypeStruct((total, LANES), BF16),
            jax.ShapeDtypeStruct((8, channels), F32),
            jax.ShapeDtypeStruct((8, LANES), F32),
            jax.ShapeDtypeStruct((8, width), F32),
        ],
        input_output_aliases={20: 0, 21: 1, 22: 2} if start else {},
        compiler_params=pltpu.CompilerParams(dimension_semantics=("arbitrary", "arbitrary")),
        cost_estimate=cost(22e9 * count, 30e6 * count),
    )(
        slots, segments, spans, pre, pre, grad, y, states, seg_row, scale_row, pull_row, spread, kernel, offset, skip, gain,
        shared_kernel, shared_offset, bias, rate, *(done if start else ()),
    )


def ring_order(devices, across):
    depth = devices // across
    if devices % across or across < 2 or depth < 2 or depth % 2 and across % 2:
        return list(range(devices))
    if across == 2:
        return [z * 2 for z in range(depth)] + [z * 2 + 1 for z in reversed(range(depth))]
    walk = [z * across for z in range(depth)]
    for turn, z in enumerate(reversed(range(depth))):
        xs = range(1, across)
        walk += [z * across + x for x in (xs if turn % 2 == 0 else reversed(xs))]
    return walk


class Numbers:
    def __init__(self, axis, size, columns):
        self.names = {name: i for i, name in enumerate(columns)}
        table = jnp.asarray([[values(i) for values in columns.values()] for i in range(size)], jnp.int32)
        row = lax.dynamic_slice(table, (lax.axis_index(axis), 0), (1, len(columns)), allow_negative_indices=False)
        self.row = lax.optimization_barrier(row)

    def __getitem__(self, name):
        return self.row[0, self.names[name]]


def rows_at(values, start, count, axis=0):
    starts = [start if i == axis else 0 for i in range(values.ndim)]
    sizes = [count if i == axis else size for i, size in enumerate(values.shape)]
    return lax.dynamic_slice(values, starts, sizes, allow_negative_indices=False)


def put_at(values, update, row, column=0):
    return lax.dynamic_update_slice(values, update, (row, column), allow_negative_indices=False)


WAYS = (1, -1)


class Ring:
    def __init__(self, devices, across, height, halved):
        self.size = n = devices
        self.order = order = ring_order(devices, across)
        self.block = block = height // (2 * n)
        self.eighth = eighth = halved // 8
        onward = [(order[i], order[(i + 1) % n]) for i in range(n)]
        self.pairs = {1: onward, -1: [(b, a) for a, b in onward]}
        columns = {}
        for step in range(n):
            for kind, lead in (("add", 0), ("store", 1)):
                for way in WAYS:
                    columns[kind, step, way] = lambda i, w=way, s=step, d=lead: (0 if w > 0 else n) + (
                        order.index(i) + w * (d - s)
                    ) % n
            for way in WAYS:

                def eighth_of(i, w=way, s=step):
                    origin = order[(order.index(i) - w * s) % n]
                    return 2 * ((origin & 1) * 4 + (origin >> 1 & 1) * 2 + (origin >> 2 & 1)) + (0 if w > 0 else 1)

                columns["side", step, way] = eighth_of
        for bit in range(3):
            columns["give", bit] = lambda i, k=bit: 1 - (i >> k & 1)
            columns["keep", bit] = lambda i, k=bit: i >> k & 1
        self.at = Numbers("dp", n, columns)

    def exchange(self, values, bit):
        return lax.ppermute(values, "dp", [(i, i ^ (1 << bit)) for i in range(self.size)])

    def halve(self, kept, arrived, bit):
        rows, columns = kept.shape
        first = self.at.names["give", bit]

        def kernel(row, mine, other, given, held):
            total = (mine[...].astype(F32) + other[...].astype(F32)).astype(BF16)

            @pl.when(pl.program_id(0) == 0)
            def _():
                given[...] = total

            @pl.when(pl.program_id(0) == 1)
            def _():
                held[...] = total

        half = (rows // 2, columns)
        at = pl.BlockSpec(half, lambda i, row: (row[0, first + i], 0))
        return pl.pallas_call(
            kernel,
            name="halve",
            grid_spec=pltpu.PrefetchScalarGridSpec(
                num_scalar_prefetch=1, grid=(2,), in_specs=[at, at], out_specs=[whole(half), whole(half)]
            ),
            out_shape=[jax.ShapeDtypeStruct(half, BF16)] * 2,
            compiler_params=limits(12),
            cost_estimate=cost(1e6, 4e6),
        )(self.at.row, kept, arrived)

    def add(self, parts, arrived, step, extra=None):
        block, columns = self.block, parts.shape[1]
        shape = (block, columns)
        half = 0 if extra is None else extra.shape[0] // 2
        full = (block + half, columns)
        first = self.at.names["add", step, 1]

        def kernel(row, one, two, *rest):
            out_one, out_two = rest[-2:]
            sources = [one[...].astype(F32), two[...].astype(F32)]
            for i in range(len(arrived)):
                sources[i] = sources[i] + rest[i][...].astype(F32)
            out_one[:block] = sources[0].astype(BF16)
            out_two[:block] = sources[1].astype(BF16)
            if half:
                out_one[block:] = rest[2][:half]
                out_two[block:] = rest[2][half:]

        return pl.pallas_call(
            kernel,
            name="ring_add",
            grid_spec=pltpu.PrefetchScalarGridSpec(
                num_scalar_prefetch=1,
                grid=(1,),
                in_specs=[
                    pl.BlockSpec(shape, lambda i, row: (row[0, first], 0)),
                    pl.BlockSpec(shape, lambda i, row: (row[0, first + 1], 0)),
                ]
                + [whole(shape)] * len(arrived)
                + ([whole(extra.shape)] if half else []),
                out_specs=[whole(full), whole(full)],
            ),
            out_shape=[jax.ShapeDtypeStruct(full, BF16)] * 2,
            compiler_params=limits(10),
            cost_estimate=cost(1e6, 4e6),
        )(self.at.row, parts, parts, *arrived, *([extra] if half else []))

    def store(self, sums, held, step):
        block, height = self.block, self.eighth // 2
        channels, model = sums[0].shape[1], sums[2].shape[1]
        first, side = self.at.names["store", step, 1], self.at.names["side", step, 1]

        def kernel(row, one, two, *rest):
            gate, inner, out = rest[3:]
            for way, source in enumerate((one, two)):

                @pl.when(pl.program_id(0) == way)
                def _():
                    gate[...] = source[:block, :channels].astype(F32)
                    inner[...] = source[:block, channels:].astype(F32)
                    out[...] = source[block:, :].astype(F32)

        low_spec = pl.BlockSpec((block, channels), lambda i, row: (row[0, first + i], 0))
        return pl.pallas_call(
            kernel,
            name="ring_store",
            grid_spec=pltpu.PrefetchScalarGridSpec(
                num_scalar_prefetch=1,
                grid=(2,),
                in_specs=[whole(held[0].shape), whole(held[1].shape)] + [pl.BlockSpec(memory_space=pl.ANY)] * 3,
                out_specs=[low_spec, low_spec, pl.BlockSpec((height, model), lambda i, row: (row[0, side + i], 0))],
            ),
            out_shape=[jax.ShapeDtypeStruct(values.shape, F32) for values in sums],
            input_output_aliases={3: 0, 4: 1, 5: 2},
            compiler_params=limits(12),
            cost_estimate=cost(1e6, 6e6),
        )(self.at.row, *held, *sums)

    def all_reduce(self, parts, sums, fillers, finished):
        n, fillers = self.size, list(fillers)

        def send(held, earlier=()):
            arrived = [lax.ppermute(values, "dp", self.pairs[way]) for way, values in zip(WAYS, held)]
            made = fillers.pop(0)(lambda values: after(values, *held)) if fillers else []
            return lax.optimization_barrier((*arrived, *made, *earlier))[:2]

        held = self.add(parts, (), 0)
        for step in range(1, n):
            held = self.add(parts, send(held), step, finished() if step == n - 1 else None)
        for step in range(n):
            if step:
                held = send(held, sums[:1])
            sums = self.store(sums, held, step)
        for filler in fillers:
            filler(lambda values: values)
        return sums, held


class Ranks:
    def __init__(self, size, slab):
        self.size, self.along = size, size // 2
        along = self.along

        def owner(i, slot):
            other, place = divmod(slot, along)
            return ((i - 2 * place) % size) ^ other

        def slot(i, owner):
            other = (owner ^ i) & 1
            return other * along + (i - (owner ^ other)) % size // 2

        columns = {}
        for k in range(size):
            columns["owner", k] = lambda i, k=k: owner(i, k)
        for k in range(size):
            columns["slot", k] = lambda i, k=k: slot(i, k)
        columns["slab"] = lambda i: i * slab
        self.at = Numbers("tensor", size, columns)

    def core(self, values):
        return lax.ppermute(values, "tensor", [(i, i ^ 1) for i in range(self.size)])

    def shift(self, values, places):
        return lax.ppermute(values, "tensor", [(i, (i + 2 * places) % self.size) for i in range(self.size)])

    def gather(self, own):
        held = [own]
        for _ in range(1, self.along):
            held.append(self.shift(held[-1], 1))
        return jnp.concatenate(held + [self.core(values) for values in held], axis=0)


def total_over(values, axis, size):
    step = 1
    while step < size:
        values = values + lax.ppermute(values, axis, [(i, i ^ step) for i in range(size)])
        step *= 2
    return values


def after(values, *earlier):
    return lax.optimization_barrier((values, *earlier))[0]


def body(
    ranks, dps, tokens, pre_gain, weight_gate, weight_inner, weight_step, weight_shared, conv_kernel, conv_offset,
    shared_kernel, shared_offset, step_bias, log_rate, skip_gain, gate_gain, weight_out, cotangent, segments, image_span,
):
    seqs, rows, model = tokens.shape
    length = rows * ranks
    pieces = length // STRETCH
    total = seqs * length
    channels = weight_gate.shape[1]
    heads = step_bias.shape[0]
    inner_width = channels * ranks
    width = weight_shared.shape[1]
    slab = width // ranks
    group = Ranks(ranks, slab)
    local = rows == STRETCH

    mixer = (token_of(jnp.arange(STRETCH))[:, None] == jnp.arange(STRETCH)[None, :]).astype(BF16)

    def reorder(values, dims=NN):
        blocks = values.reshape(-1, STRETCH, values.shape[-1])
        moved = [lax.dot_general(mixer, blocks[i], dims, preferred_element_type=BF16) for i in range(blocks.shape[0])]
        return jnp.concatenate(moved, axis=0).reshape(values.shape)

    def gather(values):
        if local:
            return group.gather(values.reshape(seqs * rows, model))
        every = lax.all_gather(values, "tensor", axis=1, tiled=True).reshape(seqs, pieces, STRETCH, model)
        return reorder(jnp.moveaxis(every, 1, 0)).reshape(total, model)

    def scatter(values):
        every = jnp.moveaxis(reorder(values, TN).reshape(pieces, seqs, STRETCH, model), 0, 1).reshape(seqs, length, model)
        return lax.psum_scatter(every, "tensor", scatter_dimension=1, tiled=True).astype(F32)

    def slabs(values):
        blocks = values.reshape(seqs, pieces, STRETCH, values.shape[-1])
        if not local:
            return jnp.moveaxis(blocks, 1, 0).reshape(values.shape)
        return jnp.concatenate(
            [rows_at(blocks, group.at["owner", slot], 1, 1)[:, 0] for slot in range(ranks)], axis=0
        ).reshape(values.shape)

    slots = jnp.arange(pieces, dtype=jnp.int32)
    if local:
        first = group.at.names["slot", 0]
        slots = group.at.row[0, first : first + pieces]
    own_low = reorder(tokens) if local else tokens
    cot_low = reorder(cotangent) if local else cotangent
    own = own_low.astype(F32)
    row_scale = lax.rsqrt(jnp.mean(own * own, axis=2, keepdims=True) + EPSILON)
    normed_low = (own * row_scale * pre_gain[None, None, :]).astype(BF16)
    tail = min(512, channels) - width - heads
    weight_ss = jnp.concatenate([weight_shared, weight_step, jnp.zeros((model, tail), BF16)], axis=1)
    pad_heads = lambda values: jnp.pad(values, (0, LANES - heads))[None, :]
    bias = pad_heads(step_bias)
    rate = pad_heads(-jnp.exp(log_rate))
    skip = jnp.repeat(skip_gain, HEAD)[None, :]
    heads_of = (jnp.arange(LANES)[:, None] == (jnp.arange(channels) // HEAD)[None, :]).astype(BF16)
    spread = jnp.concatenate([heads_of, heads_of], axis=0)
    seg_row = jnp.swapaxes(segments.astype(F32).reshape(seqs, pieces, 8, STRETCH // 8), 2, 3).reshape(1, total)
    offset_row, shared_offset_row = conv_offset[None, :], shared_offset[None, :]
    gain_row = gate_gain[None, :]

    slab = width // ranks
    weight_low = jnp.concatenate([weight_gate, weight_inner], axis=1)
    weight_side = jnp.concatenate(
        [
            rows_at(weight_shared, group.at["slab"], slab, 1),
            weight_step,
            jnp.zeros((model, LANES - slab - heads), BF16),
        ],
        axis=1,
    )
    blocked = local and ranks == 4
    if blocked:
        own_rows, cot_rows = normed_low.reshape(seqs * rows, model), cot_low.reshape(seqs * rows, model)
        far_rows = group.shift(own_rows, 1)
        far_cot = group.shift(after(cot_rows, own_rows), 1)
        weights = (weight_gate, weight_inner, weight_ss)
        first = fill_rows(own_rows, group.core(own_rows), weights, NN, None)
        first_cot = fill_rows(cot_rows, group.core(cot_rows), (weight_out,), NT, None, BF16)
        far_rows = after(far_rows, first[0], first_cot[0], weight_low, weight_side)
        pre, normed_in = fill_rows(far_rows, group.core(far_rows), weights, NN, first)
    else:
        normed_in, cot_full = gather(normed_low), gather(cot_low)
        weights = jnp.concatenate([weight_gate, weight_inner, weight_ss], axis=1)
        pre = lax.dot_general(normed_in, weights, NN, preferred_element_type=F32)
        grad = lax.dot_general(cot_full, weight_out, NT, preferred_element_type=BF16)
    y, gated, states, squares = scan_forward(
        slots, segments, image_span, pre, seg_row, spread, conv_kernel, offset_row, skip, shared_kernel, shared_offset_row,
        bias, rate,
    )
    if blocked:
        far_cot = after(far_cot, squares)
        grad, cot_full = fill_rows(far_cot, group.core(far_cot), (weight_out,), NT, first_cot, BF16)
    coupling = coupling_step(slots, seqs, gated, grad, gain_row)
    sums = total_over(jnp.concatenate([squares, coupling], axis=0), "tensor", ranks)
    scale_row = lax.rsqrt(sums[0:1] / inner_width + EPSILON)
    pull_row = scale_row * scale_row * scale_row / inner_width * sums[1:2]

    def backward(start, count, done, pull):
        return scan_backward(
            start, count, done, slots, segments, image_span, pre, grad, y, states, seg_row, scale_row, pull, spread,
            conv_kernel, offset_row, skip, gain_row, shared_kernel, shared_offset_row, bias, rate,
        )

    out_product = lambda left: lax.dot_general(left, cot_full, TN, preferred_element_type=BF16)
    made = {}
    ringed = local and dps == 8 and ranks == 4 and seqs > 1 and model == 2 * channels
    if ringed:
        ring = Ring(dps, ranks // 2, model, channels)
        join = lambda mine, arrived: (mine.astype(F32) + arrived.astype(F32)).astype(BF16)
        first = group.at.names["owner", 0]
        to_give, to_keep, norm_near, norm_far = split_norm_step(
            group.at.row[0, first : first + ranks], ring.at.row, seqs, gated, scale_row, gain_row, None,
            ring.at.names["give", 0], ring.at.names["keep", 0],
        )
        given = out_product(to_give)
        arrived = ring.exchange(given, 0)
        kept = out_product(after(to_keep, given))
        done = backward(0, seqs // 2, None, after(pull_row, kept))
        mixed_far = lax.dot_general(after(norm_far, done[0]), weight_out, NN, preferred_element_type=BF16)
        given, kept = ring.halve(after(kept, done[0], mixed_far), arrived, 1)
        arrived = ring.exchange(given, 1)
        done = backward(seqs // 2, seqs - seqs // 2, done, after(pull_row, given))
        given, kept = ring.halve(after(kept, done[0]), arrived, 2)
        low, shared_part, step_low, channel_grads, head_grads, shared_grads = done
        low_part = lax.dot_general(normed_in, after(low, given), TN, preferred_element_type=BF16)
        made["eighth"] = kept, ring.exchange(given, 2)
        low_part = after(low_part, made["eighth"][1])
    else:
        normed_out = norm_step(slots, seqs, gated, scale_row, gain_row)
        norm_near, norm_far = (normed_out[: total // 2], normed_out[total // 2 :]) if local else (normed_out, None)
        out_sum = lax.psum(out_product(normed_out), "dp")
        low, shared_part, step_low, channel_grads, head_grads, shared_grads = backward(0, seqs, None, pull_row)
        low_part = lax.dot_general(normed_in, low, TN, preferred_element_type=BF16)

    cut = total // 2 if local else 0
    half = ranks // 2
    by_rank = lambda values: values.reshape(-1, seqs, rows, model)

    def finished(hold=lambda values: values):
        if "finished" not in made:
            made["finished"] = join(hold(made["eighth"][0]), made["eighth"][1])
        return made["finished"]

    def finish(hold):
        return [finished(hold)] if ringed else []

    def columns_out(hold):
        columns = jnp.moveaxis(hold(shared_part).reshape(total, ranks, slab), 1, 0)
        columns = jnp.concatenate([rows_at(columns, group.at["owner", slot], 1) for slot in range(ranks)], axis=0)
        made["columns"] = columns[:half], group.core(columns[half:])
        return [columns]

    def columns_in(hold):
        shared_low = slabs(take_rows("columns", hold).astype(BF16))
        made["side"] = jnp.concatenate([shared_low, step_low[:, :heads], jnp.zeros((total, LANES - slab - heads), BF16)], axis=1)
        return [made["side"]]

    def pass_on(name):
        def run(hold):
            mine, other = made[name]
            sent = [(hold(mine)[i].astype(F32) + other[i].astype(F32)).astype(BF16) for i in range(1, half)]
            made[name] = mine[0], [other[0]] + [group.shift(values, -1 - i) for i, values in enumerate(sent)]
            return sent

        return run if local or name == "columns" else lambda hold: []

    def take_rows(name, hold):
        mine, others = made[name]
        mine = hold(mine).astype(F32)
        for values in others:
            mine = mine + values.astype(F32)
        return mine

    def input_rows_of(slot):
        part = slice(slot * seqs * rows, (slot + 1) * seqs * rows) if local else slice(0, total)

        def run(hold):
            side, low_rows = lax.optimization_barrier((hold(made["side"]), low))
            summed = lax.dot_general(side[part], weight_side, NT, preferred_element_type=F32)
            summed = (summed + lax.dot_general(low_rows[part], weight_low, NT, preferred_element_type=F32)).astype(BF16)
            if local:
                made["input", slot] = by_rank(summed)[0]
                if slot >= half:
                    made["input", slot] = group.core(made["input", slot])
            else:
                made["input"] = scatter(summed), []
            return [summed]

        return run

    def input_pair(hold):
        if local:
            made["input"] = [made["input", slot] for slot in range(half)], [made["input", slot] for slot in range(half, ranks)]
        return []

    def mix_of(far):
        def run(hold):
            if far and ringed:
                made["mixed far"] = group.core(by_rank(hold(mixed_far)))
                return []
            product = lax.dot_general(hold(norm_far if far else norm_near), weight_out, NN, preferred_element_type=BF16)
            if not local:
                made["mixed"] = scatter(product), []
            elif far:
                made["mixed far"] = group.core(by_rank(product))
            else:
                made["mixed"] = by_rank(product), made["mixed far"]
            return [product]

        return run

    def side_product(hold):
        product = lax.dot_general(hold(made["side"]), normed_in, TN, preferred_element_type=BF16)
        made["side_part"] = product[: slab + heads]
        return [made["side_part"]]

    def input_rows(hold):
        normed_grad = take_rows("input", hold)
        own = hold(own_low).astype(F32)
        weighted = normed_grad * pre_gain[None, None, :]
        projection = jnp.sum(weighted * own, axis=2, keepdims=True)
        own_grad = row_scale * weighted - row_scale * row_scale * row_scale / model * own * projection
        made["pre_gain"] = jnp.sum(normed_grad * own * row_scale, axis=(0, 1))
        made["tokens_grad"] = (cot_low.astype(F32) + own_grad).astype(BF16)
        return [made["tokens_grad"], made["pre_gain"]]

    def input_order(hold):
        if local:
            made["tokens_grad"] = reorder(hold(made["tokens_grad"]), TN)
        return [made["tokens_grad"]]

    def block_rows(hold):
        made["block_out"] = (hold(own_low).astype(F32) + take_rows("mixed", hold)).astype(BF16)
        return [made["block_out"]]

    def block_order(hold):
        if local:
            made["block_out"] = reorder(hold(made["block_out"]), TN)
        return [made["block_out"]]

    def small_start(hold):
        made["small"] = jnp.concatenate(
            [jnp.pad(hold(shared_grads), ((0, 0), (0, channels - width))), made["pre_gain"].reshape(-1, channels)], axis=0
        )
        return []

    def pack(hold):
        made["small"] = jnp.concatenate(
            [channel_grads, jnp.pad(head_grads, ((0, 0), (0, channels - LANES))), made["small"]], axis=0
        )
        return []

    def spread_sum(name, axis, size, bits, kind=F32):
        partners = [0]
        for bit in bits:
            partners += [partner ^ (1 << bit) for partner in partners]

        def send(hold):
            values = hold(made[name])
            made[name] = values, [lax.ppermute(values, axis, [(i, i ^ k) for i in range(size)]) for k in partners[1:]]
            return [values]

        def receive(hold):
            values, others = hold(made[name])
            terms = [values.astype(F32)] + [other.astype(F32) for other in others]
            while len(terms) > 1:
                terms = [terms[i] + terms[i + 1] for i in range(0, len(terms), 2)]
            made[name] = terms[0].astype(kind)
            return [made[name]]

        return send, receive

    def together(*parts):
        def run(hold):
            return [value for part in parts for value in part(hold)]

        return run

    bits_of = lambda size: list(range((size - 1).bit_length()))
    tensor_send, tensor_take = spread_sum("small", "tensor", ranks, bits_of(ranks))
    small_dp = [spread_sum("small", "dp", dps, bits) for bits in (bits_of(dps)[1:], bits_of(dps)[:1])]
    if ringed:
        side_dp = [spread_sum("side_part", "dp", dps, [bit], BF16) for bit in range(3)]
    else:

        def side_whole(hold):
            made["side_part"] = lax.psum(made["side_part"], "dp")
            return []

        side_dp = [(side_whole, lambda hold: [])] + [(lambda hold: [], lambda hold: [])] * 2
    nothing = lambda hold: []
    far = [input_rows_of(slot) for slot in (range(half, ranks) if local else range(1))]
    near = [input_rows_of(slot) for slot in (range(half) if local else range(0))]
    def gather_near(hold):
        slabs_of = hold(made["side_part"])[:slab]
        made["gathered"] = [slabs_of]
        for _ in range(1, half):
            made["gathered"].append(group.shift(made["gathered"][-1], 1))
        return []

    def gather_far(hold):
        made["gathered"] = made["gathered"] + [group.core(hold(values)) for values in made["gathered"]]
        return []

    def side_outputs(hold):
        gathered = jnp.stack([hold(values) for values in made["gathered"]])
        shared = jnp.concatenate([rows_at(gathered, group.at["slot", owner], 1)[0] for owner in range(ranks)], axis=0)
        made["shared"] = shared.T.astype(F32)
        made["step"] = hold(made["side_part"])[slab : slab + heads].T.astype(F32)
        return [made["shared"], made["step"]]

    def small_outputs(hold):
        packed = hold(made["small"])
        shared_sums = packed[16:24, :width]
        made["outputs"] = [
            packed[24:].reshape(model), packed[0:4], packed[4], shared_sums[0:4], shared_sums[4], packed[9, :heads],
            packed[8, :heads], jnp.sum(packed[5].reshape(heads, HEAD), axis=1), packed[6],
        ]
        return []

    fillers = [
        together(mix_of(True) if local else nothing, columns_out),
        together(pass_on("columns"), mix_of(False)),
        together(columns_in, side_product),
        together(side_dp[0][0], *far[:1]),
        together(side_dp[0][1], side_dp[1][0], *far[1:2]),
        *far[2:],
        together(*near[:1], finish),
        together(side_dp[1][1], *near[1:2]),
        *near[2:],
        together(input_pair, pass_on("input")),
        together(pass_on("mixed"), side_dp[2][0]),
        together(input_rows, side_dp[2][1]),
        together(small_start, tensor_send, input_order, gather_near),
        together(tensor_take, pack, small_dp[0][0], block_rows),
        together(block_order, gather_far),
        together(small_dp[0][1], small_dp[1][0], side_outputs),
    ]
    if ringed:
        sums = [blank((model, channels)), blank((model, channels)), blank((channels, model))]
        sums, last = ring.all_reduce(low_part, sums, fillers, finished)
        grads = dict(zip(("gate", "inner", "out"), sums))
    else:
        low_sum = lax.psum(low_part, "dp").astype(F32)
        grads = {"gate": low_sum[:, :channels], "inner": low_sum[:, channels:], "out": out_sum.astype(F32)}
        for filler in fillers:
            filler(lambda values: values)
    finish_small = together(small_dp[1][1], small_outputs)
    finish_small((lambda values: after(values, *last, sums[0])) if ringed else (lambda values: values))
    gain, kernel_grad, offset_grad, shared_kernel_grad, shared_offset_grad, bias_grad, rate_grad, skip_grad, gate_gain_grad = made[
        "outputs"
    ]
    return (
        made["block_out"],
        made["tokens_grad"],
        gain,
        grads["gate"],
        grads["inner"],
        made["step"],
        made["shared"],
        kernel_grad,
        offset_grad,
        shared_kernel_grad,
        shared_offset_grad,
        bias_grad,
        rate_grad,
        skip_grad,
        gate_gain_grad,
        grads["out"],
    )


def solution(mesh):
    placed = (
        P("dp", "tensor", None),
        P(),
        P(None, "tensor"),
        P(None, "tensor"),
        P(None, "tensor"),
        P(),
        P(None, "tensor"),
        P("tensor"),
        P(),
        P(),
        P("tensor"),
        P("tensor"),
        P("tensor"),
        P("tensor"),
        P("tensor", None),
        P("dp", "tensor", None),
        P("dp", None),
        P("dp", None),
    )
    return jax.shard_map(
        partial(body, mesh.shape["tensor"], mesh.shape["dp"]),
        mesh=mesh,
        in_specs=placed,
        out_specs=(
            P("dp", "tensor", None),
            P("dp", "tensor", None),
            P(),
            P(None, "tensor"),
            P(None, "tensor"),
            P(None, "tensor"),
            P(),
            P(None, "tensor"),
            P("tensor"),
            P(),
            P(),
            P("tensor"),
            P("tensor"),
            P("tensor"),
            P("tensor"),
            P("tensor", None),
        ),
        check_vma=False,
    )
```
